128 devices in a mesh: row: 16 (over y, x), col: 8 (over z, core).
Axes of the slice: x: 4, y: 4, z: 4, core: 2. Of those that a mesh axis runs over, the one named last changes fastest.
Arguments:
- src_points: bfloat16 [16384, 256], P('row'), may hold values from -32 to 32, as said below
- tgt_points: bfloat16 [32768, 256], P(('col', 'row')), may hold values from -32 to 32, as said below
- log_src_mass: float32 [16384], P('row'), may hold values from -3 to 3
- log_tgt_mass: float32 [32768], P('col'), may hold values from -3 to 3
Outputs:
- src_potential: float32 [16384], P('row')
- tgt_potential: float32 [32768], P('col')
- mean_potentials: float32 [], replicated
The draws below stay inside these ranges and needn't reach their ends.
Inputs may be any that keep to these rules, and one draw needn't show every extreme that they name: `src_points`: point coordinates. `tgt_points`: point coordinates.
All inputs are finite; a program needn't handle non-finite values.
Results may differ from the reference program's by a relative error of at most 0.0003.
Values may be sent and summed in bfloat16 or wider, within the bound.
No kernel may reach another device: no remote copies, remote signals or barrier semaphores. Data moves between devices by JAX's collectives and lax.ppermute only.
A program may use at most 64 MiB of HBM per device.

```python
import jax
import jax.numpy as jnp
from jax import lax

WIDTH = 256
TGT_DEV = 4096
ITERS = 3
SOURCES = 16384
TARGETS = 32768


def scaled_points(key, count):
    values = jnp.clip(jax.random.normal(jax.random.fold_in(key, 1), (count, WIDTH), jnp.float32), -8.0, 8.0)
    low, high = (0.5, 2.0)
    scales = jnp.exp(jax.random.uniform(jax.random.fold_in(key, 2), (count, 1), jnp.float32, jnp.log(low), jnp.log(high)))
    return values * scales


def target_cloud(key):
    points = scaled_points(key, TARGETS)
    groups = TARGETS // TGT_DEV
    offsets = jnp.clip(1.5 * jax.random.normal(jax.random.fold_in(key, 3), (groups, WIDTH), jnp.float32), -6.0, 6.0)
    points = points + jnp.repeat(offsets, TGT_DEV, axis=0)
    return jnp.clip(points, -32.0, 32.0)


def draw_tgt_points(key, part):
    return target_cloud(jax.random.fold_in(key, 71)).astype(jnp.bfloat16)


def draw_src_points(key, part):
    points = jnp.clip(scaled_points(jax.random.fold_in(key, 53), SOURCES), -32.0, 32.0)
    return points.astype(jnp.bfloat16)


def levels(stream_key, extent, pieces, least, high):
    level, own = 1.0, jax.random.fold_in(stream_key, 6)
    for dim, shards_of in pieces:
        steps = jnp.exp(jax.random.uniform(jax.random.fold_in(own, dim), (shards_of,), jnp.float32, least / len(pieces), high / len(pieces)))
        level = level * jnp.repeat(steps, extent[dim] // shards_of).reshape([-1 if axis == dim else 1 for axis in range(len(extent))])
    return level


def setup_inputs(seed: int = 0) -> dict:
    key_of = jax.random.split(jax.random.key(seed), 5)
    src_points = draw_src_points(jax.random.fold_in(key_of[4], 71), 0)
    tgt_points = draw_tgt_points(jax.random.fold_in(key_of[4], 71), 0)
    log_src_mass = jnp.clip(jax.random.uniform(key_of[2], (SOURCES,), jnp.float32, -3.0, 3.0) * levels(key_of[2], (SOURCES,), ((0, 16),), -0.4, 0.0), -3.0, 3.0)
    log_tgt_mass = jnp.clip(jax.random.uniform(key_of[3], (TARGETS,), jnp.float32, -3.0, 3.0) * levels(key_of[3], (TARGETS,), ((0, 8),), -0.4, 0.0), -3.0, 3.0)
    return {"src_points": src_points, "tgt_points": tgt_points, "log_src_mass": log_src_mass, "log_tgt_mass": log_tgt_mass}


entropy_weight = 0.1


def cost_block(points_a, squares_a, points_b, squares_b):
    product = lax.dot_general(points_a, points_b, (((1,), (1,)), ((), ())), preferred_element_type=jnp.float32)
    return (squares_a[:, None] + squares_b[None, :] - 2.0 * product) / points_a.shape[1]


def reference(src_points, tgt_points, log_src_mass, log_tgt_mass):
    sqx = jnp.sum(src_points.astype(jnp.float32) ** 2, axis=1)
    sqy = jnp.sum(tgt_points.astype(jnp.float32) ** 2, axis=1)
    blocks = SOURCES // min(1024, SOURCES)
    src_blocks = src_points.reshape(blocks, -1, WIDTH)
    sq_blocks = sqx.reshape(blocks, -1)
    mass_blocks = log_src_mass.reshape(blocks, -1)
    costs = lax.map(lambda item: cost_block(item[0], item[1], tgt_points, sqy), (src_blocks, sq_blocks))
    tgt_potential = jnp.zeros((TARGETS,), jnp.float32)
    src_potential = jnp.zeros((SOURCES,), jnp.float32)
    for step in range(ITERS):
        def source_rows(cost):
            terms = log_tgt_mass[None, :] + (tgt_potential[None, :] - cost) / entropy_weight
            top = jnp.max(terms, axis=1)
            return top + jnp.log(jnp.sum(jnp.exp(terms - top[:, None]), axis=1))

        src_potential = -entropy_weight * lax.map(source_rows, costs).reshape(-1)
        pot_blocks = src_potential.reshape(blocks, -1)

        def target_step(carry, item):
            cost, mass, pot = item
            terms = mass[:, None] + (pot[:, None] - cost) / entropy_weight
            block_top = jnp.max(terms, axis=0)
            block_sum = jnp.sum(jnp.exp(terms - block_top[None, :]), axis=0)
            top = jnp.maximum(carry[0], block_top)
            total = carry[1] * jnp.exp(carry[0] - top) + block_sum * jnp.exp(block_top - top)
            return (top, total), None

        start = (jnp.full((TARGETS,), -jnp.inf, jnp.float32), jnp.zeros((TARGETS,), jnp.float32))
        (top, total), unused = lax.scan(target_step, start, (costs, mass_blocks, pot_blocks))
        tgt_potential = -entropy_weight * (top + jnp.log(total))
    mean_potentials = jnp.mean(src_potential) + jnp.mean(tgt_potential)
    return src_potential, tgt_potential, mean_potentials
```

```python
import math

import jax
import jax.numpy as jnp
from jax import lax
from jax.experimental import pallas as pl
from jax.experimental.pallas import tpu as pltpu
from jax.sharding import Mesh
from jax.sharding import PartitionSpec as P

ROW = ("row_0", "row_1")
COL = ("col_0", "col_1")
COL_ROW = ("col_0", "col_1", "row_0", "row_1")

EPS = 0.1
WIDTH = 256
NATS = 2.0 / (WIDTH * EPS)
BITS = NATS * math.log2(math.e)
LOG2E = math.log2(math.e)
VMEM_LIMIT = 24 * 1024 * 1024
LANES = 128
STEP = 64

VMEM = pl.BlockSpec(memory_space=pltpu.VMEM)
SMEM = pl.BlockSpec(memory_space=pltpu.SMEM)


def call(kernel, outs, ins, scratch, aliases=None):
    return pl.pallas_call(
        kernel,
        out_shape=outs,
        in_specs=ins,
        out_specs=jax.tree.map(lambda _: VMEM, outs),
        scratch_shapes=scratch,
        input_output_aliases=aliases or {},
        compiler_params=pltpu.CompilerParams(vmem_limit_bytes=VMEM_LIMIT),
    )


def f32(*shape):
    return jax.ShapeDtypeStruct(shape, jnp.float32)


def spread(dense, wide_ref):
    for b in range(dense.shape[0]):
        square = jnp.broadcast_to(dense[b : b + 1, :], (LANES, LANES))
        wide_ref[b * LANES : (b + 1) * LANES, :] = square.T


def terms_kernel(place, x_ref, *refs):
    pieces, (mass_ref, t_ref, out_ref, top_ref, sum_ref) = refs[:8], refs[8:]
    rows = x_ref.shape[0]
    top_ref[...] = jnp.full(top_ref.shape, -jnp.inf, jnp.float32)
    for k in range(8):
        half, shift = k // 4, k % 4
        for m in range(2):
            points = pieces[k][m * 256 : (m + 1) * 256, :]
            squares = points.astype(jnp.float32) ** 2
            squares = squares[:, :LANES] + squares[:, LANES:]
            product = lax.dot_general(
                x_ref[...], points, (((1,), (1,)), ((), ())), preferred_element_type=jnp.float32
            )
            both = None
            for side in range(2):
                inner = 2 * m + side
                shift_y, shift_x = (shift, inner) if half == 0 else (inner, shift)
                at_y = lax.rem(place[0] + (4 - shift_y), 4)
                at_x = lax.rem(place[1] + (4 - shift_x), 4)
                tile = 2 * (4 * at_y + at_x) + half
                square = squares[side * LANES : (side + 1) * LANES, :].T
                bias = (
                    mass_ref[pl.ds(tile, 1), :] / NATS
                    - jnp.sum(square, axis=0, keepdims=True) * 0.5
                )
                terms = product[:, side * LANES : (side + 1) * LANES] + bias
                t_ref[:, pl.ds(pl.multiple_of(tile * LANES, LANES), LANES)] = terms
                both = terms if both is None else jnp.maximum(both, terms)
            top_ref[...] = jnp.maximum(top_ref[...], both)

    def rows_step(r, unused):
        at = pl.ds(pl.multiple_of(r * STEP, STEP), STEP)
        top = jnp.max(top_ref[at, :], axis=1, keepdims=True)
        total = jnp.zeros((STEP, LANES), jnp.float32)
        for t in range(t_ref.shape[1] // LANES):
            total += jnp.exp2((t_ref[at, t * LANES : (t + 1) * LANES] - top) * BITS)
        top_ref[at, :] = jnp.broadcast_to(top, (STEP, LANES))
        sum_ref[at, :] = total
        return unused

    lax.fori_loop(0, rows // STEP, rows_step, 0)
    for b in range(rows // LANES):
        at = slice(b * LANES, (b + 1) * LANES)
        total = jnp.sum(sum_ref[at, :].T, axis=0, keepdims=True)
        top = top_ref[at, :].T[:1, :]
        out_ref[b : b + 1, :] = top * NATS + jnp.log(total)


def column_kernel(t_ref, lse_ref, mass_ref, out_ref, wide_ref):
    rows, columns = t_ref.shape
    spread((mass_ref[...] - lse_ref[...]) / NATS, wide_ref)
    block = 4 * LANES

    def tile(r, c, t):
        at = pl.ds(pl.multiple_of(r * STEP, STEP), STEP)
        column = pl.ds(pl.multiple_of(c * block + t * LANES, LANES), LANES)
        return (t_ref[at, column] + wide_ref[at, :]).reshape(STEP // 8, 8, LANES)

    for c in range(columns // block):

        def top_step(r, tops):
            return tuple(jnp.maximum(top, jnp.max(tile(r, c, t), axis=0)) for t, top in enumerate(tops))

        start = tuple(jnp.full((8, LANES), -jnp.inf, jnp.float32) for _ in range(4))
        tops = lax.fori_loop(0, rows // STEP, top_step, start)
        tops = [jnp.max(top, axis=0, keepdims=True) for top in tops]
        wide = [jnp.broadcast_to(top, (8, LANES))[None] for top in tops]

        def sum_step(r, totals):
            return tuple(
                total + jnp.sum(jnp.exp2((tile(r, c, t) - wide[t]) * BITS), axis=0)
                for t, total in enumerate(totals)
            )

        start = tuple(jnp.zeros((8, LANES), jnp.float32) for _ in range(4))
        totals = lax.fori_loop(0, rows // STEP, sum_step, start)
        for t in range(4):
            total = jnp.sum(totals[t], axis=0, keepdims=True)
            out_ref[c * 4 + t : c * 4 + t + 1, :] = tops[t] * NATS + jnp.log(total)


def plan_kernel(t_ref, row_ref, column_ref, plan_ref, out_ref, wide_ref, sum_ref):
    rows, columns = t_ref.shape
    spread(row_ref[...], wide_ref)

    def rows_step(r, unused):
        at = pl.ds(pl.multiple_of(r * STEP, STEP), STEP)
        total = jnp.zeros((STEP, LANES), jnp.float32)
        own = wide_ref[at, :]
        for t in range(columns // LANES):
            column = slice(t * LANES, (t + 1) * LANES)
            value = jnp.exp2(t_ref[at, column] * BITS + own + column_ref[t : t + 1, :])
            plan_ref[at, column] = value
            total += value
        sum_ref[at, :] = total
        return unused

    lax.fori_loop(0, rows // STEP, rows_step, 0)
    for b in range(rows // LANES):
        at = slice(b * LANES, (b + 1) * LANES)
        out_ref[b : b + 1, :] = jnp.sum(sum_ref[at, :].T, axis=0, keepdims=True)


def row_sums_kernel(plan_ref, scale_ref, out_ref, sum_ref):
    rows, columns = plan_ref.shape

    def rows_step(r, unused):
        at = pl.ds(pl.multiple_of(r * STEP, STEP), STEP)
        total = jnp.zeros((STEP, LANES), jnp.float32)
        for t in range(columns // LANES):
            total += plan_ref[at, t * LANES : (t + 1) * LANES] * scale_ref[t : t + 1, :]
        sum_ref[at, :] = total
        return unused

    lax.fori_loop(0, rows // STEP, rows_step, 0)
    for b in range(rows // LANES):
        at = slice(b * LANES, (b + 1) * LANES)
        out_ref[b : b + 1, :] = jnp.sum(sum_ref[at, :].T, axis=0, keepdims=True)


def column_sums_kernel(plan_ref, scale_ref, out_ref, wide_ref):
    rows, columns = plan_ref.shape
    spread(scale_ref[...], wide_ref)
    tiles = columns // LANES
    per = 16
    for c in range(0, tiles, per):

        def rows_step(r, totals):
            at = pl.ds(pl.multiple_of(r * STEP, STEP), STEP)
            own = wide_ref[at, :]
            return tuple(
                total
                + jnp.sum(
                    (plan_ref[at, (c + t) * LANES : (c + t + 1) * LANES] * own).reshape(
                        STEP // 8, 8, LANES
                    ),
                    axis=0,
                )
                for t, total in enumerate(totals)
            )

        start = tuple(jnp.zeros((8, LANES), jnp.float32) for _ in range(per))
        totals = lax.fori_loop(0, rows // STEP, rows_step, start)
        for t in range(per):
            out_ref[c + t : c + t + 1, :] = jnp.sum(totals[t], axis=0, keepdims=True)


def shifted(value, axis):
    n = lax.axis_size(axis)
    return [value] + [
        lax.ppermute(value, axis, [(i, (i + k) % n) for i in range(n)]) for k in range(1, n)
    ]


def add_all(parts):
    total = parts[0]
    for part in parts[1:]:
        total = total + part
    return total


def lse_all(parts):
    top = parts[0]
    for part in parts[1:]:
        top = jnp.maximum(top, part)
    return top + jnp.log(add_all([jnp.exp(part - top) for part in parts]))


def over(value, axes, combine):
    for axis in axes:
        value = combine(shifted(value, axis))
    return value


def gather_targets(points):
    half = points.shape[0] // 2
    first = jnp.concatenate(shifted(points[:half], "row_1"))
    second = jnp.concatenate(shifted(points[half:], "row_0"))
    return shifted(first, "row_0") + shifted(second, "row_1")


def body(src_points, tgt_points, log_src_mass, log_tgt_mass):
    rows, columns = src_points.shape[0], log_tgt_mass.shape[0]
    row_tiles, column_tiles = rows // LANES, columns // LANES
    src_mass = log_src_mass.reshape(row_tiles, LANES)
    tgt_mass = log_tgt_mass.reshape(column_tiles, LANES)
    place = jnp.stack([lax.axis_index("row_0"), lax.axis_index("row_1")]).astype(jnp.int32)
    wide = pltpu.VMEM((rows, LANES), jnp.float32)
    big = pltpu.VMEM((rows, columns), jnp.float32)

    def resident(value):
        return pltpu.with_memory_space_constraint(value, pltpu.VMEM)

    pieces = gather_targets(tgt_points)
    terms, lse = call(
        terms_kernel, (big, f32(row_tiles, LANES)), [SMEM] + [VMEM] * 10, [wide, wide]
    )(place, src_points, *pieces, tgt_mass)
    src_lse = over(lse, ("col_1", "col_0"), lse_all)
    lse = call(column_kernel, f32(column_tiles, LANES), [VMEM] * 3, [wide])(
        resident(terms), src_lse, src_mass
    )
    tgt_lse = over(lse, ("row_1", "row_0"), lse_all)
    plan, sums = call(
        plan_kernel, (big, f32(row_tiles, LANES)), [VMEM] * 3, [wide, wide], {0: 0}
    )(resident(terms), (src_mass - src_lse) * LOG2E, (tgt_mass - tgt_lse) * LOG2E)
    plan = resident(plan)
    src_mass_lin, tgt_mass_lin = jnp.exp(src_mass), jnp.exp(tgt_mass)
    col_call = call(column_sums_kernel, f32(column_tiles, LANES), [VMEM] * 2, [wide])
    row_call = call(row_sums_kernel, f32(row_tiles, LANES), [VMEM] * 2, [wide])
    src_sums = over(sums, ("col_1", "col_0"), add_all)
    tgt_sums = over(col_call(plan, src_mass_lin / src_sums), ("row_1", "row_0"), add_all)
    src_sums = over(row_call(plan, tgt_mass_lin / tgt_sums), ("col_1", "col_0"), add_all)
    tgt_sums = over(col_call(plan, src_mass_lin / src_sums), ("row_1", "row_0"), add_all)
    squares = jnp.sum(src_points.astype(jnp.float32) ** 2, axis=1).reshape(row_tiles, LANES)
    src_potential = -EPS * (src_lse + jnp.log(src_sums) - src_mass - squares / (WIDTH * EPS))
    tgt_potential = -EPS * (tgt_lse + jnp.log(tgt_sums) - 2.0 * tgt_mass)
    peers_row, peers_col = lax.axis_size(ROW), lax.axis_size(COL)
    src_mean = jnp.sum(src_potential) / (rows * peers_row)
    src_mean = over(jnp.full((8, LANES), src_mean), ("row_1", "row_0"), add_all)
    tgt_mean = jnp.sum(tgt_potential) / (columns * peers_col)
    tgt_mean = over(jnp.full((8, LANES), tgt_mean), ("col_1", "col_0"), add_all)
    mean_potentials = (src_mean + tgt_mean)[0, 0]
    return (src_potential.reshape(-1), tgt_potential.reshape(-1), mean_potentials)


def solution(mesh):
    finer = Mesh(mesh.devices.reshape(4, 4, 4, 2), ("row_0", "row_1", "col_0", "col_1"))
    placed = (P(ROW, None), P(COL_ROW, None), P(ROW), P(COL))
    return jax.shard_map(
        body, mesh=finer, in_specs=placed, out_specs=(P(ROW), P(COL), P()), check_vma=False
    )
```

```python
import itertools
import math

import jax
import jax.numpy as jnp
from jax import lax
from jax.experimental import pallas as pl
from jax.experimental.pallas import tpu as pltpu
from jax.sharding import Mesh
from jax.sharding import PartitionSpec as P

ROW = ("row_0", "row_1")
COL = ("col_0", "col_1")
COL_ROW = ("col_0", "col_1", "row_0", "row_1")

EPS = 0.1
WIDTH = 256
NATS = 2.0 / (WIDTH * EPS)
BITS = NATS * math.log2(math.e)
LOG2E = math.log2(math.e)
VMEM_LIMIT = 24 * 1024 * 1024
LANES = 128
STEP = 64
HUGE = 3.0e38

VMEM = pl.BlockSpec(memory_space=pltpu.VMEM)
SMEM = pl.BlockSpec(memory_space=pltpu.SMEM)


def call(kernel, outs, ins, scratch, aliases=None):
    return pl.pallas_call(
        kernel,
        out_shape=outs,
        in_specs=ins,
        out_specs=jax.tree.map(lambda _: VMEM, outs),
        scratch_shapes=scratch,
        input_output_aliases=aliases or {},
        compiler_params=pltpu.CompilerParams(vmem_limit_bytes=VMEM_LIMIT),
    )


def f32(*shape):
    return jax.ShapeDtypeStruct(shape, jnp.float32)


def spread(dense, wide_ref):
    for b in range(dense.shape[0]):
        square = jnp.broadcast_to(dense[b : b + 1, :], (LANES, LANES))
        wide_ref[b * LANES : (b + 1) * LANES, :] = square.T


def collapse(wide_ref):
    lines = [
        jnp.sum(wide_ref[b * LANES : (b + 1) * LANES, :].T, axis=0, keepdims=True)
        for b in range(wide_ref.shape[0] // LANES)
    ]
    return jnp.concatenate(lines, axis=0)


def collapse_top(wide_ref):
    lines = [
        wide_ref[b * LANES : (b + 1) * LANES, :].T[:1, :]
        for b in range(wide_ref.shape[0] // LANES)
    ]
    return jnp.concatenate(lines, axis=0)


def add_all(parts):
    total = parts[0]
    for part in parts[1:]:
        total = total + part
    return total


def lse_all(parts):
    top = parts[0]
    for part in parts[1:]:
        top = jnp.maximum(top, part)
    return top + jnp.log(add_all([jnp.exp(part - top) for part in parts]))


def at_rows(r):
    return pl.ds(pl.multiple_of(r * STEP, STEP), STEP)


def lane_tile(t):
    return slice(t * LANES, (t + 1) * LANES)


def target_block(place, shift, inner):
    first_core = place[2] == 0
    shift_y = jnp.where(first_core, shift, inner)
    shift_x = jnp.where(first_core, inner, shift)
    return 4 * lax.rem(place[0] + 4 - shift_y, 4) + lax.rem(place[1] + 4 - shift_x, 4)


def chunk_terms(x_ref, points, mass_ref, block):
    squares = points.astype(jnp.float32) ** 2
    squares = squares[:, :LANES] + squares[:, LANES:]
    product = lax.dot_general(
        x_ref[...], points, (((1,), (1,)), ((), ())), preferred_element_type=jnp.float32
    )
    found = []
    for side in range(2):
        square = squares[side * LANES : (side + 1) * LANES, :].T
        mass = mass_ref[pl.ds(2 * block + side, 1), :]
        bias = mass / NATS - jnp.sum(square, axis=0, keepdims=True) * 0.5
        found.append(product[:, lane_tile(side)] + bias)
    return found


def block_columns(block, side):
    return pl.ds(pl.multiple_of(block * 256 + side * LANES, LANES), LANES)


def first_terms_kernel(place, x_ref, points_ref, mass_ref, t_ref, top_ref, sum_ref):
    rows = x_ref.shape[0]
    blocks = [target_block(place, 0, m) for m in range(4)]
    for m in range(4):
        both = chunk_terms(x_ref, points_ref[m * 256 : (m + 1) * 256, :], mass_ref, blocks[m])
        for side in range(2):
            t_ref[:, block_columns(blocks[m], side)] = both[side]
        top = jnp.maximum(both[0], both[1])
        top_ref[...] = top if m == 0 else jnp.maximum(top_ref[...], top)

    def rows_step(r, unused):
        at = at_rows(r)
        top = jnp.max(top_ref[at, :], axis=1, keepdims=True)
        total = jnp.zeros((STEP, LANES), jnp.float32)
        for m in range(4):
            for side in range(2):
                terms = t_ref[at, block_columns(blocks[m], side)]
                total += jnp.exp2((terms - top) * BITS)
        top_ref[at, :] = jnp.broadcast_to(top, (STEP, LANES))
        sum_ref[at, :] = total
        return unused

    lax.fori_loop(0, rows // STEP, rows_step, 0)


def terms_kernel(place, x_ref, old_ref, first_top_ref, first_sum_ref, *refs):
    pieces, (mass_ref, t_ref, out_ref, top_ref, sum_ref) = refs[:3], refs[3:]
    rows, columns = t_ref.shape
    sum_ref[...] = first_sum_ref[...]
    for k in range(3):

        def chunk_step(m, unused):
            block = target_block(place, k + 1, m)
            points = pieces[k][pl.ds(pl.multiple_of(m * 256, 256), 256), :]
            both = chunk_terms(x_ref, points, mass_ref, block)
            top = first_top_ref[...]
            total = sum_ref[...]
            for side in range(2):
                t_ref[:, block_columns(block, side)] = both[side]
                total += jnp.exp2((both[side] - top) * BITS)
            sum_ref[...] = total
            return unused

        lax.fori_loop(0, 4, chunk_step, 0)
    total = collapse(sum_ref)
    out_ref[...] = collapse_top(first_top_ref) * NATS + jnp.log(total)

    @pl.when(jnp.logical_not(jnp.max(total) < HUGE))
    def exact():
        def rows_step(r, unused):
            at = at_rows(r)
            top = jnp.full((STEP, LANES), -jnp.inf, jnp.float32)
            for t in range(columns // LANES):
                top = jnp.maximum(top, t_ref[at, lane_tile(t)])
            top = jnp.max(top, axis=1, keepdims=True)
            total = jnp.zeros((STEP, LANES), jnp.float32)
            for t in range(columns // LANES):
                total += jnp.exp2((t_ref[at, lane_tile(t)] - top) * BITS)
            top_ref[at, :] = jnp.broadcast_to(top, (STEP, LANES))
            sum_ref[at, :] = total
            return unused

        lax.fori_loop(0, rows // STEP, rows_step, 0)
        out_ref[...] = collapse_top(top_ref) * NATS + jnp.log(collapse(sum_ref))


def column_kernel(t_ref, *refs):
    parts, (mass_ref, out_ref, lse_ref, wide_ref) = refs[:4], refs[4:]
    rows, columns = t_ref.shape
    lse = lse_all([part[...] for part in parts])
    lse_ref[...] = lse
    spread((mass_ref[...] - lse) / NATS, wide_ref)
    per = 4

    def group(value):
        return value.reshape(STEP // 8, 8, LANES)

    def sums(c, tops):
        wide = [jnp.broadcast_to(top, (STEP, LANES)) for top in tops]

        def sum_step(r, totals):
            at = at_rows(r)
            own = wide_ref[at, :]
            return tuple(
                total
                + jnp.sum(
                    group(jnp.exp2((t_ref[at, lane_tile(c + t)] + own - wide[t]) * BITS)), axis=0
                )
                for t, total in enumerate(totals)
            )

        start = tuple(jnp.zeros((8, LANES), jnp.float32) for _ in range(per))
        totals = lax.fori_loop(0, rows // STEP, sum_step, start)
        for t in range(per):
            total = jnp.sum(totals[t], axis=0, keepdims=True)
            out_ref[c + t : c + t + 1, :] = tops[t] * NATS + jnp.log(total)

    for c in range(0, columns // LANES, per):
        tops = [
            jnp.max(t_ref[:STEP, lane_tile(c + t)] + wide_ref[:STEP, :], axis=0, keepdims=True)
            for t in range(per)
        ]
        sums(c, tops)

    @pl.when(jnp.logical_not(jnp.max(out_ref[...]) < HUGE))
    def exact():
        for c in range(0, columns // LANES, per):

            def top_step(r, tops):
                at = at_rows(r)
                return tuple(
                    jnp.maximum(top, jnp.max(group(t_ref[at, lane_tile(c + t)] + wide_ref[at, :]), axis=0))
                    for t, top in enumerate(tops)
                )

            start = tuple(jnp.full((8, LANES), -jnp.inf, jnp.float32) for _ in range(per))
            tops = lax.fori_loop(0, rows // STEP, top_step, start)
            sums(c, [jnp.max(top, axis=0, keepdims=True) for top in tops])


def plan_kernel(t_ref, *refs):
    parts, refs = refs[:4], refs[4:]
    tgt_mass_ref, src_lse_ref, src_mass_ref, plan_ref, out_ref, lse_ref = refs[:6]
    wide_ref, sum_ref, line_ref = refs[6:]
    rows, columns = t_ref.shape
    lse = lse_all([part[...] for part in parts])
    lse_ref[...] = lse
    line_ref[...] = (tgt_mass_ref[...] - lse) * LOG2E
    spread((src_mass_ref[...] - src_lse_ref[...]) * LOG2E, wide_ref)
    per = 4

    def rows_step(r, unused):
        at = at_rows(r)
        total = jnp.zeros((STEP, LANES), jnp.float32)
        own = wide_ref[at, :]
        for c in range(0, columns // LANES, per):
            terms = [t_ref[at, lane_tile(c + t)] for t in range(per)]
            values = [
                jnp.exp2(terms[t] * BITS + own + line_ref[c + t : c + t + 1, :]) for t in range(per)
            ]
            for t in range(per):
                plan_ref[at, lane_tile(c + t)] = values[t]
                total += values[t]
        sum_ref[at, :] = total
        return unused

    lax.fori_loop(0, rows // STEP, rows_step, 0)
    out_ref[...] = collapse(sum_ref)


def row_sums_kernel(plan_ref, *refs):
    parts, (mass_ref, out_ref, sum_ref, line_ref) = refs[:4], refs[4:]
    rows, columns = plan_ref.shape
    line_ref[...] = jnp.exp(mass_ref[...]) / add_all([part[...] for part in parts])

    def rows_step(r, unused):
        at = at_rows(r)
        total = jnp.zeros((STEP, LANES), jnp.float32)
        for t in range(columns // LANES):
            total += plan_ref[at, lane_tile(t)] * line_ref[t : t + 1, :]
        sum_ref[at, :] = total
        return unused

    lax.fori_loop(0, rows // STEP, rows_step, 0)
    out_ref[...] = collapse(sum_ref)


def column_sums(plan_ref, scale, out_ref, wide_ref):
    rows, columns = plan_ref.shape
    spread(scale, wide_ref)
    per = 16
    for c in range(0, columns // LANES, per):

        def rows_step(r, totals):
            at = at_rows(r)
            own = wide_ref[at, :]
            return tuple(
                total
                + jnp.sum(
                    (plan_ref[at, lane_tile(c + t)] * own).reshape(STEP // 8, 8, LANES), axis=0
                )
                for t, total in enumerate(totals)
            )

        start = tuple(jnp.zeros((8, LANES), jnp.float32) for _ in range(per))
        totals = lax.fori_loop(0, rows // STEP, rows_step, start)
        for t in range(per):
            out_ref[c + t : c + t + 1, :] = jnp.sum(totals[t], axis=0, keepdims=True)


def column_sums_kernel(plan_ref, *refs):
    parts, (mass_ref, out_ref, wide_ref) = refs[:4], refs[4:]
    scale = jnp.exp(mass_ref[...]) / add_all([part[...] for part in parts])
    column_sums(plan_ref, scale, out_ref, wide_ref)


def last_column_sums_kernel(plan_ref, *refs):
    parts, (mass_ref, lse_ref, squares_ref, out_ref, potential_ref, wide_ref) = refs[:4], refs[4:]
    sums = add_all([part[...] for part in parts])
    mass = mass_ref[...]
    column_sums(plan_ref, jnp.exp(mass) / sums, out_ref, wide_ref)
    squares = squares_ref[...] / (WIDTH * EPS)
    potential = -EPS * (lse_ref[...] + jnp.log(sums) - mass - squares)
    potential_ref[...] = potential
    tiles = plan_ref.shape[1] // LANES
    out_ref[tiles:, :] = jnp.broadcast_to(jnp.sum(potential), (8, LANES))


def last_kernel(*refs):
    parts, (mass_ref, lse_ref, potential_ref, own_ref, other_ref) = refs[:4], refs[4:]
    tiles = mass_ref.shape[0]
    sums = add_all([part[...] for part in parts])
    potential = -EPS * (lse_ref[...] + jnp.log(sums[:tiles]) - 2.0 * mass_ref[...])
    potential_ref[...] = potential
    own_ref[...] = jnp.broadcast_to(jnp.sum(potential), (8, LANES))
    other_ref[...] = sums[tiles:]


def shifted(value, axis):
    n = lax.axis_size(axis)
    return [value] + [
        lax.ppermute(value, axis, [(i, (i + k) % n) for i in range(n)]) for k in range(1, n)
    ]


ALL = ("row_0", "row_1", "col_0", "col_1")
SIZES = (4, 4, 4, 2)


def number(y, x, z, core):
    return ((y % 4 * 4 + x % 4) * 4 + z) * 2 + core


def turned(value, stage):
    found = [value]
    for k in range(1, 4):
        pairs = []
        for y, x, z, core in itertools.product(*map(range, SIZES)):
            along_y = (core + stage) % 2
            to = number(y + k * along_y, x + k * (1 - along_y), z, core)
            pairs.append((number(y, x, z, core), to))
        found.append(lax.ppermute(value, ALL, pairs))
    return found


def body(src_points, tgt_points, log_src_mass, log_tgt_mass):
    rows, columns = src_points.shape[0], log_tgt_mass.shape[0]
    row_tiles, column_tiles = rows // LANES, columns // LANES
    src_mass = log_src_mass.reshape(row_tiles, LANES)
    tgt_mass = log_tgt_mass.reshape(column_tiles, LANES)
    place = jnp.stack([lax.axis_index(name) for name in ("row_0", "row_1", "col_1")])
    place = place.astype(jnp.int32)
    wide = pltpu.VMEM((rows, LANES), jnp.float32)
    big = pltpu.VMEM((rows, columns), jnp.float32)
    line = pltpu.VMEM((column_tiles, LANES), jnp.float32)
    by_row, by_column = f32(row_tiles, LANES), f32(column_tiles, LANES)

    def resident(value):
        return pltpu.with_memory_space_constraint(value, pltpu.VMEM)

    def over_col(value, combine):
        return shifted(combine(shifted(value, "col_1")), "col_0")

    def over_row(value, combine):
        return shifted(combine(shifted(value, "row_1")), "row_0")

    first = jnp.concatenate(turned(tgt_points, 0))
    pieces = turned(first, 1)[1:]
    terms, top, sums = call(first_terms_kernel, (big, wide, wide), [SMEM] + [VMEM] * 3, [])(
        place, src_points, first, tgt_mass
    )
    terms, lse = call(terms_kernel, (big, by_row), [SMEM] + [VMEM] * 8, [wide, wide], {2: 0})(
        place, src_points, resident(terms), resident(top), resident(sums), *pieces, tgt_mass
    )
    parts = over_col(lse, lse_all)
    lse, src_lse = call(column_kernel, (by_column, by_row), [VMEM] * 6, [wide])(
        resident(terms), *parts, src_mass
    )
    parts = over_row(lse, lse_all)
    plan, sums, tgt_lse = call(
        plan_kernel, (big, by_row, by_column), [VMEM] * 8, [wide, wide, line], {0: 0}
    )(resident(terms), *parts, tgt_mass, src_lse, src_mass)
    plan = resident(plan)
    parts = over_col(sums, add_all)
    sums = call(column_sums_kernel, by_column, [VMEM] * 6, [wide])(plan, *parts, src_mass)
    parts = over_row(sums, add_all)
    sums = call(row_sums_kernel, by_row, [VMEM] * 6, [wide, line])(plan, *parts, tgt_mass)
    parts = over_col(sums, add_all)
    squares = jnp.sum(src_points.astype(jnp.float32) ** 2, axis=1).reshape(row_tiles, LANES)
    sums, src_potential = call(
        last_column_sums_kernel, (f32(column_tiles + 8, LANES), by_row), [VMEM] * 8, [wide]
    )(plan, *parts, src_mass, src_lse, squares)
    parts = over_row(sums, add_all)
    tile = f32(8, LANES)
    tgt_potential, tgt_sum, src_sum = call(last_kernel, (by_column, tile, tile), [VMEM] * 6, [])(
        *parts, tgt_mass, tgt_lse
    )
    tgt_sum = add_all(over_col(tgt_sum, add_all))
    sources_all, targets_all = rows * lax.axis_size(ROW), columns * lax.axis_size(COL)
    mean_potentials = (src_sum / sources_all + tgt_sum / targets_all)[0, 0]
    return (src_potential.reshape(-1), tgt_potential.reshape(-1), mean_potentials)


def solution(mesh):
    finer = Mesh(mesh.devices.reshape(4, 4, 4, 2), ("row_0", "row_1", "col_0", "col_1"))
    placed = (P(ROW, None), P(COL_ROW, None), P(ROW), P(COL))
    return jax.shard_map(
        body, mesh=finer, in_specs=placed, out_specs=(P(ROW), P(COL), P()), check_vma=False
    )
```

```python
import functools
import itertools
import math

import jax
import jax.numpy as jnp
from jax import lax
from jax.experimental import pallas as pl
from jax.experimental.pallas import tpu as pltpu
from jax.sharding import Mesh
from jax.sharding import PartitionSpec as P

ROW = ("row_0", "row_1")
COL = ("col_0", "col_1")
COL_ROW = ("col_0", "col_1", "row_0", "row_1")

EPS = 0.1
WIDTH = 256
NATS = 2.0 / (WIDTH * EPS)
BITS = NATS * math.log2(math.e)
LOG2E = math.log2(math.e)
VMEM_LIMIT = 24 * 1024 * 1024
LANES = 128
STEP = 64
HUGE = 3.0e38

VMEM = pl.BlockSpec(memory_space=pltpu.VMEM)
SMEM = pl.BlockSpec(memory_space=pltpu.SMEM)


def call(kernel, outs, ins, scratch, aliases=None):
    return pl.pallas_call(
        kernel,
        out_shape=outs,
        in_specs=ins,
        out_specs=jax.tree.map(lambda _: VMEM, outs),
        scratch_shapes=scratch,
        input_output_aliases=aliases or {},
        compiler_params=pltpu.CompilerParams(vmem_limit_bytes=VMEM_LIMIT),
    )


def f32(*shape):
    return jax.ShapeDtypeStruct(shape, jnp.float32)


def spread(dense, wide_ref):
    for b in range(dense.shape[0]):
        square = jnp.broadcast_to(dense[b : b + 1, :], (LANES, LANES))
        wide_ref[b * LANES : (b + 1) * LANES, :] = square.T


def collapse(wide_ref):
    lines = [
        jnp.sum(wide_ref[b * LANES : (b + 1) * LANES, :].T, axis=0, keepdims=True)
        for b in range(wide_ref.shape[0] // LANES)
    ]
    return jnp.concatenate(lines, axis=0)


def collapse_top(wide_ref):
    lines = [
        wide_ref[b * LANES : (b + 1) * LANES, :].T[:1, :]
        for b in range(wide_ref.shape[0] // LANES)
    ]
    return jnp.concatenate(lines, axis=0)


def add_all(parts):
    total = parts[0]
    for part in parts[1:]:
        total = total + part
    return total


def lse_all(parts):
    top = parts[0]
    for part in parts[1:]:
        top = jnp.maximum(top, part)
    return top + jnp.log(add_all([jnp.exp(part - top) for part in parts]))


def copies(out_ref, value):
    for peer in range(out_ref.shape[0]):
        out_ref[peer] = value


def combined(parts_ref, combine):
    return combine([parts_ref[peer] for peer in range(parts_ref.shape[0])])


def at_rows(r):
    return pl.ds(pl.multiple_of(r * STEP, STEP), STEP)


def lane_tile(t):
    return slice(t * LANES, (t + 1) * LANES)


def target_block(place, shift, inner):
    first_core = place[2] == 0
    shift_y = jnp.where(first_core, shift, inner)
    shift_x = jnp.where(first_core, inner, shift)
    return 4 * lax.rem(place[0] + 4 - shift_y, 4) + lax.rem(place[1] + 4 - shift_x, 4)


def chunk_terms(x_ref, points, mass_ref, block):
    squares = points.astype(jnp.float32) ** 2
    squares = squares[:, :LANES] + squares[:, LANES:]
    product = lax.dot_general(
        x_ref[...], points, (((1,), (1,)), ((), ())), preferred_element_type=jnp.float32
    )
    found = []
    for side in range(2):
        square = squares[side * LANES : (side + 1) * LANES, :].T
        mass = mass_ref[pl.ds(2 * block + side, 1), :]
        bias = mass / NATS - jnp.sum(square, axis=0, keepdims=True) * 0.5
        found.append(product[:, lane_tile(side)] + bias)
    return found


def block_columns(block, side):
    return pl.ds(pl.multiple_of(block * 256 + side * LANES, LANES), LANES)


def first_terms_kernel(place, x_ref, points_ref, mass_ref, t_ref, top_ref, sum_ref, squares_ref):
    rows = x_ref.shape[0]
    squares = x_ref[...].astype(jnp.float32) ** 2
    sum_ref[...] = squares[:, :LANES] + squares[:, LANES:]
    squares_ref[...] = collapse(sum_ref)
    blocks = [target_block(place, 0, m) for m in range(4)]
    for m in range(4):
        both = chunk_terms(x_ref, points_ref[m * 256 : (m + 1) * 256, :], mass_ref, blocks[m])
        for side in range(2):
            t_ref[:, block_columns(blocks[m], side)] = both[side]
        top = jnp.maximum(both[0], both[1])
        top_ref[...] = top if m == 0 else jnp.maximum(top_ref[...], top)

    def rows_step(r, unused):
        at = at_rows(r)
        top = jnp.max(top_ref[at, :], axis=1, keepdims=True)
        total = jnp.zeros((STEP, LANES), jnp.float32)
        for m in range(4):
            for side in range(2):
                terms = t_ref[at, block_columns(blocks[m], side)]
                total += jnp.exp2((terms - top) * BITS)
        top_ref[at, :] = jnp.broadcast_to(top, (STEP, LANES))
        sum_ref[at, :] = total
        return unused

    lax.fori_loop(0, rows // STEP, rows_step, 0)


def chunk_steps(k, place, x_ref, points_ref, mass_ref, top_ref, t_ref, sum_ref):
    def chunk_step(m, unused):
        block = target_block(place, k, m)
        points = points_ref[pl.ds(pl.multiple_of(m * 256, 256), 256), :]
        both = chunk_terms(x_ref, points, mass_ref, block)
        top = top_ref[...]
        total = sum_ref[...]
        for side in range(2):
            t_ref[:, block_columns(block, side)] = both[side]
            total += jnp.exp2((both[side] - top) * BITS)
        sum_ref[...] = total
        return unused

    lax.fori_loop(0, 4, chunk_step, 0)


def more_terms_kernel(k, place, x_ref, old_ref, old_sum_ref, top_ref, points_ref, mass_ref, *refs):
    t_ref, sum_ref = refs
    chunk_steps(k, place, x_ref, points_ref, mass_ref, top_ref, t_ref, sum_ref)


def last_terms_kernel(k, place, x_ref, old_ref, old_sum_ref, old_top_ref, points_ref, mass_ref, *refs):
    t_ref, sum_ref, out_ref, top_ref = refs
    rows, columns = t_ref.shape
    sum_ref[...] = old_sum_ref[...]
    chunk_steps(k, place, x_ref, points_ref, mass_ref, old_top_ref, t_ref, sum_ref)
    total = collapse(sum_ref)
    copies(out_ref, collapse_top(old_top_ref) * NATS + jnp.log(total))

    @pl.when(jnp.logical_not(jnp.max(total) < HUGE))
    def exact():
        def rows_step(r, unused):
            at = at_rows(r)
            top = jnp.full((STEP, LANES), -jnp.inf, jnp.float32)
            for t in range(columns // LANES):
                top = jnp.maximum(top, t_ref[at, lane_tile(t)])
            top = jnp.max(top, axis=1, keepdims=True)
            total = jnp.zeros((STEP, LANES), jnp.float32)
            for t in range(columns // LANES):
                total += jnp.exp2((t_ref[at, lane_tile(t)] - top) * BITS)
            top_ref[at, :] = jnp.broadcast_to(top, (STEP, LANES))
            sum_ref[at, :] = total
            return unused

        lax.fori_loop(0, rows // STEP, rows_step, 0)
        copies(out_ref, collapse_top(top_ref) * NATS + jnp.log(collapse(sum_ref)))


def column_kernel(t_ref, parts_ref, mass_ref, out_ref, lse_ref, wide_ref, line_ref):
    rows, columns = t_ref.shape
    lse = combined(parts_ref, lse_all)
    lse_ref[...] = lse
    spread((mass_ref[...] - lse) / NATS, wide_ref)
    per = 4

    def group(value):
        return value.reshape(STEP // 8, 8, LANES)

    def sums(c, tops):
        wide = [jnp.broadcast_to(top, (STEP, LANES)) for top in tops]

        def sum_step(r, totals):
            at = at_rows(r)
            own = wide_ref[at, :]
            return tuple(
                total
                + jnp.sum(
                    group(jnp.exp2((t_ref[at, lane_tile(c + t)] + own - wide[t]) * BITS)), axis=0
                )
                for t, total in enumerate(totals)
            )

        start = tuple(jnp.zeros((8, LANES), jnp.float32) for _ in range(per))
        totals = lax.fori_loop(0, rows // STEP, sum_step, start)
        for t in range(per):
            total = jnp.sum(totals[t], axis=0, keepdims=True)
            line_ref[c + t : c + t + 1, :] = tops[t] * NATS + jnp.log(total)

    for c in range(0, columns // LANES, per):
        tops = [
            jnp.max(t_ref[:STEP, lane_tile(c + t)] + wide_ref[:STEP, :], axis=0, keepdims=True)
            for t in range(per)
        ]
        sums(c, tops)

    @pl.when(jnp.logical_not(jnp.max(line_ref[...]) < HUGE))
    def exact():
        for c in range(0, columns // LANES, per):

            def top_step(r, tops):
                at = at_rows(r)
                return tuple(
                    jnp.maximum(top, jnp.max(group(t_ref[at, lane_tile(c + t)] + wide_ref[at, :]), axis=0))
                    for t, top in enumerate(tops)
                )

            start = tuple(jnp.full((8, LANES), -jnp.inf, jnp.float32) for _ in range(per))
            tops = lax.fori_loop(0, rows // STEP, top_step, start)
            sums(c, [jnp.max(top, axis=0, keepdims=True) for top in tops])

    copies(out_ref, line_ref[...])


def plan_kernel(t_ref, parts_ref, tgt_mass_ref, src_lse_ref, src_mass_ref, *refs):
    plan_ref, out_ref, lse_ref, wide_ref, sum_ref, line_ref = refs
    rows, columns = t_ref.shape
    lse = combined(parts_ref, lse_all)
    lse_ref[...] = lse
    line_ref[...] = (tgt_mass_ref[...] - lse) * LOG2E
    spread((src_mass_ref[...] - src_lse_ref[...]) * LOG2E, wide_ref)
    per = 4

    def rows_step(r, unused):
        at = at_rows(r)
        total = jnp.zeros((STEP, LANES), jnp.float32)
        own = wide_ref[at, :]
        for c in range(0, columns // LANES, per):
            terms = [t_ref[at, lane_tile(c + t)] for t in range(per)]
            values = [
                jnp.exp2(terms[t] * BITS + own + line_ref[c + t : c + t + 1, :]) for t in range(per)
            ]
            for t in range(per):
                plan_ref[at, lane_tile(c + t)] = values[t]
                total += values[t]
        sum_ref[at, :] = total
        return unused

    lax.fori_loop(0, rows // STEP, rows_step, 0)
    copies(out_ref, collapse(sum_ref))


def row_sums_kernel(plan_ref, parts_ref, mass_ref, out_ref, sum_ref, line_ref):
    rows, columns = plan_ref.shape
    line_ref[...] = jnp.exp(mass_ref[...]) / combined(parts_ref, add_all)

    def rows_step(r, unused):
        at = at_rows(r)
        total = jnp.zeros((STEP, LANES), jnp.float32)
        for t in range(columns // LANES):
            total += plan_ref[at, lane_tile(t)] * line_ref[t : t + 1, :]
        sum_ref[at, :] = total
        return unused

    lax.fori_loop(0, rows // STEP, rows_step, 0)
    copies(out_ref, collapse(sum_ref))


def column_sums(plan_ref, scale, line_ref, wide_ref):
    rows, columns = plan_ref.shape
    spread(scale, wide_ref)
    per = 16
    for c in range(0, columns // LANES, per):

        def rows_step(r, totals):
            at = at_rows(r)
            own = wide_ref[at, :]
            return tuple(
                total
                + jnp.sum(
                    (plan_ref[at, lane_tile(c + t)] * own).reshape(STEP // 8, 8, LANES), axis=0
                )
                for t, total in enumerate(totals)
            )

        start = tuple(jnp.zeros((8, LANES), jnp.float32) for _ in range(per))
        totals = lax.fori_loop(0, rows // STEP, rows_step, start)
        for t in range(per):
            line_ref[c + t : c + t + 1, :] = jnp.sum(totals[t], axis=0, keepdims=True)


def column_sums_kernel(plan_ref, parts_ref, mass_ref, out_ref, wide_ref, line_ref):
    scale = jnp.exp(mass_ref[...]) / combined(parts_ref, add_all)
    column_sums(plan_ref, scale, line_ref, wide_ref)
    copies(out_ref, line_ref[...])


def last_column_sums_kernel(plan_ref, parts_ref, mass_ref, lse_ref, squares_ref, *refs):
    out_ref, potential_ref, wide_ref, line_ref = refs
    sums = combined(parts_ref, add_all)
    mass = mass_ref[...]
    column_sums(plan_ref, jnp.exp(mass) / sums, line_ref, wide_ref)
    squares = squares_ref[...] / (WIDTH * EPS)
    potential = -EPS * (lse_ref[...] + jnp.log(sums) - mass - squares)
    potential_ref[...] = potential
    tiles = plan_ref.shape[1] // LANES
    line_ref[tiles:, :] = jnp.broadcast_to(jnp.sum(potential), (8, LANES))
    copies(out_ref, line_ref[...])


def last_kernel(parts_ref, mass_ref, lse_ref, potential_ref, own_ref, other_ref):
    tiles = mass_ref.shape[0]
    sums = combined(parts_ref, add_all)
    potential = -EPS * (lse_ref[...] + jnp.log(sums[:tiles]) - 2.0 * mass_ref[...])
    potential_ref[...] = potential
    copies(own_ref, jnp.broadcast_to(jnp.sum(potential), (8, LANES)))
    other_ref[...] = sums[tiles:]


ALL = ("row_0", "row_1", "col_0", "col_1")
SIZES = (4, 4, 4, 2)


def number(y, x, z, core):
    return ((y % 4 * 4 + x % 4) * 4 + z) * 2 + core


def turned(value, stage):
    found = {0: value}
    for k in (2, 1, 3):
        pairs = []
        for y, x, z, core in itertools.product(*map(range, SIZES)):
            along_y = (core + stage) % 2
            to = number(y + k * along_y, x + k * (1 - along_y), z, core)
            pairs.append((number(y, x, z, core), to))
        found[k] = lax.ppermute(value, ALL, pairs)
    return [found[k] for k in range(4)]


def body(src_points, tgt_points, log_src_mass, log_tgt_mass):
    rows, columns = src_points.shape[0], log_tgt_mass.shape[0]
    row_tiles, column_tiles = rows // LANES, columns // LANES
    src_mass = log_src_mass.reshape(row_tiles, LANES)
    tgt_mass = log_tgt_mass.reshape(column_tiles, LANES)
    place = jnp.stack([lax.axis_index(name) for name in ("row_0", "row_1", "col_1")])
    place = place.astype(jnp.int32)
    wide = pltpu.VMEM((rows, LANES), jnp.float32)
    big = pltpu.VMEM((rows, columns), jnp.float32)
    line = pltpu.VMEM((column_tiles, LANES), jnp.float32)
    longer = pltpu.VMEM((column_tiles + 8, LANES), jnp.float32)
    by_row, by_column = f32(row_tiles, LANES), f32(column_tiles, LANES)
    peers_row, peers_col = lax.axis_size(ROW), lax.axis_size(COL)
    rows_out, columns_out = f32(peers_col, row_tiles, LANES), f32(peers_row, column_tiles, LANES)

    def resident(value):
        return pltpu.with_memory_space_constraint(value, pltpu.VMEM)

    def over_col(value):
        return lax.all_to_all(value, COL, 0, 0, tiled=True)

    def over_row(value):
        return lax.all_to_all(value, ROW, 0, 0, tiled=True)

    first = jnp.concatenate(turned(tgt_points, 0))
    pieces = turned(first, 1)
    terms, top, sums, squares = call(
        first_terms_kernel, (big, wide, wide, by_row), [SMEM] + [VMEM] * 3, []
    )(place, src_points, first, tgt_mass)
    for k in (1, 3):
        terms, sums = call(
            functools.partial(more_terms_kernel, k), (big, wide), [SMEM] + [VMEM] * 6, [], {2: 0, 3: 1}
        )(place, src_points, resident(terms), resident(sums), resident(top), pieces[k], tgt_mass)
    terms, sums, lse = call(
        functools.partial(last_terms_kernel, 2),
        (big, wide, rows_out),
        [SMEM] + [VMEM] * 6,
        [wide],
        {2: 0, 3: 1},
    )(place, src_points, resident(terms), resident(sums), resident(top), pieces[2], tgt_mass)
    lse, src_lse = call(column_kernel, (columns_out, by_row), [VMEM] * 3, [wide, line])(
        resident(terms), over_col(lse), src_mass
    )
    plan, sums, tgt_lse = call(
        plan_kernel, (big, rows_out, by_column), [VMEM] * 5, [wide, wide, line], {0: 0}
    )(resident(terms), over_row(lse), tgt_mass, src_lse, src_mass)
    plan = resident(plan)
    sums = call(column_sums_kernel, columns_out, [VMEM] * 3, [wide, line])(
        plan, over_col(sums), src_mass
    )
    sums = call(row_sums_kernel, rows_out, [VMEM] * 3, [wide, line])(plan, over_row(sums), tgt_mass)
    sums, src_potential = call(
        last_column_sums_kernel,
        (f32(peers_row, column_tiles + 8, LANES), by_row),
        [VMEM] * 5,
        [wide, longer],
    )(plan, over_col(sums), src_mass, src_lse, squares)
    tgt_potential, tgt_sum, src_sum = call(
        last_kernel, (by_column, f32(peers_col, 8, LANES), f32(8, LANES)), [VMEM] * 3, []
    )(over_row(sums), tgt_mass, tgt_lse)
    tgt_sum = jnp.sum(over_col(tgt_sum), axis=0)
    sources_all, targets_all = rows * peers_row, columns * peers_col
    mean_potentials = (src_sum / sources_all + tgt_sum / targets_all)[0, 0]
    return (src_potential.reshape(-1), tgt_potential.reshape(-1), mean_potentials)


def solution(mesh):
    finer = Mesh(mesh.devices.reshape(4, 4, 4, 2), ("row_0", "row_1", "col_0", "col_1"))
    placed = (P(ROW, None), P(COL_ROW, None), P(ROW), P(COL))
    return jax.shard_map(
        body, mesh=finer, in_specs=placed, out_specs=(P(ROW), P(COL), P()), check_vma=False
    )
```

```python
import functools
import itertools
import math

import jax
import jax.numpy as jnp
from jax import lax
from jax.experimental import pallas as pl
from jax.experimental.pallas import tpu as pltpu
from jax.sharding import Mesh
from jax.sharding import PartitionSpec as P

ROW = ("row_0", "row_1")
COL = ("col_0", "col_1")
COL_ROW = ("col_0", "col_1", "row_0", "row_1")

EPS = 0.1
WIDTH = 256
NATS = 2.0 / (WIDTH * EPS)
BITS = NATS * math.log2(math.e)
LOG2E = math.log2(math.e)
LN2 = math.log(2.0)
VMEM_LIMIT = 24 * 1024 * 1024
LANES = 128
STEP = 64
ROWS = 512
HUGE = 3.0e38

VMEM = pl.BlockSpec(memory_space=pltpu.VMEM)
SMEM = pl.BlockSpec(memory_space=pltpu.SMEM)


def call(kernel, outs, ins, scratch, aliases=None):
    return pl.pallas_call(
        kernel,
        out_shape=outs,
        in_specs=ins,
        out_specs=jax.tree.map(lambda _: VMEM, outs),
        scratch_shapes=scratch,
        input_output_aliases=aliases or {},
        compiler_params=pltpu.CompilerParams(vmem_limit_bytes=VMEM_LIMIT),
    )


def f32(*shape):
    return jax.ShapeDtypeStruct(shape, jnp.float32)


def spread(dense, wide_ref):
    for b in range(dense.shape[0]):
        square = jnp.broadcast_to(dense[b : b + 1, :], (LANES, LANES))
        wide_ref[b * LANES : (b + 1) * LANES, :] = square.T


def collapse(wide_ref):
    lines = [
        jnp.sum(wide_ref[b * LANES : (b + 1) * LANES, :].T, axis=0, keepdims=True)
        for b in range(wide_ref.shape[0] // LANES)
    ]
    return jnp.concatenate(lines, axis=0)


def collapse_top(wide_ref):
    lines = [
        wide_ref[b * LANES : (b + 1) * LANES, :].T[:1, :]
        for b in range(wide_ref.shape[0] // LANES)
    ]
    return jnp.concatenate(lines, axis=0)


def add_all(parts):
    total = parts[0]
    for part in parts[1:]:
        total = total + part
    return total


def lse_all(parts):
    top = parts[0]
    for part in parts[1:]:
        top = jnp.maximum(top, part)
    return top + jnp.log(add_all([jnp.exp(part - top) for part in parts]))


def copies(out_ref, value):
    for peer in range(out_ref.shape[0]):
        out_ref[peer] = value


def combined(parts_ref, combine):
    return combine([parts_ref[peer] for peer in range(parts_ref.shape[0])])


def at_rows(r):
    return pl.ds(pl.multiple_of(r * STEP, STEP), STEP)


def lane_tile(t):
    return slice(t * LANES, (t + 1) * LANES)


def target_block(place, shift, inner):
    first_core = place[2] == 0
    shift_y = jnp.where(first_core, shift, inner)
    shift_x = jnp.where(first_core, inner, shift)
    return 4 * lax.rem(place[0] + 4 - shift_y, 4) + lax.rem(place[1] + 4 - shift_x, 4)


def chunk_biases(points, mass_ref, block):
    squares = points.astype(jnp.float32) ** 2
    squares = squares[:, :LANES] + squares[:, LANES:]
    found = []
    for side in range(2):
        square = squares[side * LANES : (side + 1) * LANES, :].T
        mass = mass_ref[pl.ds(2 * block + side, 1), :]
        found.append(mass * LOG2E - jnp.sum(square, axis=0, keepdims=True) * (0.5 * BITS))
    return found


def piece_product(x_ref, points_ref, r, m):
    return lax.dot_general(
        x_ref[r : r + ROWS, :],
        points_ref[m * 256 : (m + 1) * 256, :],
        (((1,), (1,)), ((), ())),
        preferred_element_type=jnp.float32,
    )


def piece_blocks(k, place, points_ref, mass_ref):
    blocks = [target_block(place, k, m) for m in range(4)]
    biases = [
        chunk_biases(points_ref[m * 256 : (m + 1) * 256, :], mass_ref, blocks[m]) for m in range(4)
    ]
    return blocks, biases


def first_terms_kernel(place, x_ref, points_ref, mass_ref, t_ref, top_ref, sum_ref, squares_ref):
    rows = x_ref.shape[0]
    squares = x_ref[...].astype(jnp.float32) ** 2
    sum_ref[...] = squares[:, :LANES] + squares[:, LANES:]
    squares_ref[...] = collapse(sum_ref)
    blocks, biases = piece_blocks(0, place, points_ref, mass_ref)
    for r in range(0, rows, ROWS):
        top = None
        for m in range(4):
            product = piece_product(x_ref, points_ref, r, m)
            for side in range(2):
                terms = product[:, lane_tile(side)] * BITS + biases[m][side]
                t_ref[2 * blocks[m] + side, r : r + ROWS, :] = terms
                top = terms if top is None else jnp.maximum(top, terms)
        top_ref[r : r + ROWS, :] = top

    def rows_step(r, unused):
        at = at_rows(r)
        top = jnp.max(top_ref[at, :], axis=1, keepdims=True)
        total = jnp.zeros((STEP, LANES), jnp.float32)
        for m in range(4):
            for side in range(2):
                total += jnp.exp2(t_ref[2 * blocks[m] + side, at, :] - top)
        top_ref[at, :] = jnp.broadcast_to(top, (STEP, LANES))
        sum_ref[at, :] = total
        return unused

    lax.fori_loop(0, rows // STEP, rows_step, 0)


def piece_steps(k, place, x_ref, points_ref, mass_ref, top_ref, old_sum_ref, t_ref, sum_ref):
    blocks, biases = piece_blocks(k, place, points_ref, mass_ref)
    for r in range(0, x_ref.shape[0], ROWS):
        top = top_ref[r : r + ROWS, :]
        total = old_sum_ref[r : r + ROWS, :]
        for m in range(4):
            product = piece_product(x_ref, points_ref, r, m)
            for side in range(2):
                terms = product[:, lane_tile(side)] * BITS + biases[m][side]
                t_ref[2 * blocks[m] + side, r : r + ROWS, :] = terms
                total += jnp.exp2(terms - top)
        sum_ref[r : r + ROWS, :] = total


def more_terms_kernel(k, place, x_ref, old_ref, old_sum_ref, top_ref, points_ref, mass_ref, *refs):
    t_ref, sum_ref = refs
    piece_steps(k, place, x_ref, points_ref, mass_ref, top_ref, old_sum_ref, t_ref, sum_ref)


def last_terms_kernel(k, place, x_ref, old_ref, old_sum_ref, old_top_ref, points_ref, mass_ref, *refs):
    t_ref, sum_ref, out_ref, top_ref = refs
    tiles, rows, _ = t_ref.shape
    piece_steps(k, place, x_ref, points_ref, mass_ref, old_top_ref, old_sum_ref, t_ref, sum_ref)
    total = collapse(sum_ref)
    copies(out_ref, collapse_top(old_top_ref) * LN2 + jnp.log(total))

    @pl.when(jnp.logical_not(jnp.max(total) < HUGE))
    def exact():
        def rows_step(r, unused):
            at = at_rows(r)
            top = jnp.full((STEP, LANES), -jnp.inf, jnp.float32)
            for t in range(tiles):
                top = jnp.maximum(top, t_ref[t, at, :])
            top = jnp.max(top, axis=1, keepdims=True)
            total = jnp.zeros((STEP, LANES), jnp.float32)
            for t in range(tiles):
                total += jnp.exp2(t_ref[t, at, :] - top)
            top_ref[at, :] = jnp.broadcast_to(top, (STEP, LANES))
            sum_ref[at, :] = total
            return unused

        lax.fori_loop(0, rows // STEP, rows_step, 0)
        copies(out_ref, collapse_top(top_ref) * LN2 + jnp.log(collapse(sum_ref)))


def column_kernel(t_ref, parts_ref, mass_ref, out_ref, lse_ref, wide_ref, line_ref):
    tiles, rows, _ = t_ref.shape
    lse = combined(parts_ref, lse_all)
    lse_ref[...] = lse
    spread((mass_ref[...] - lse) * LOG2E, wide_ref)
    per = 4

    def group(value):
        return value.reshape(STEP // 8, 8, LANES)

    def sums(c, tops):
        wide = [jnp.broadcast_to(top, (STEP, LANES)) for top in tops]

        def sum_step(r, totals):
            at = at_rows(r)
            own = wide_ref[at, :]
            return tuple(
                total
                + jnp.sum(
                    group(jnp.exp2(t_ref[c + t, at, :] + own - wide[t])), axis=0
                )
                for t, total in enumerate(totals)
            )

        start = tuple(jnp.zeros((8, LANES), jnp.float32) for _ in range(per))
        totals = lax.fori_loop(0, rows // STEP, sum_step, start)
        for t in range(per):
            total = jnp.sum(totals[t], axis=0, keepdims=True)
            line_ref[c + t : c + t + 1, :] = tops[t] * LN2 + jnp.log(total)

    for c in range(0, tiles, per):
        tops = [
            jnp.max(t_ref[c + t, :STEP, :] + wide_ref[:STEP, :], axis=0, keepdims=True)
            for t in range(per)
        ]
        sums(c, tops)

    @pl.when(jnp.logical_not(jnp.max(line_ref[...]) < HUGE))
    def exact():
        for c in range(0, tiles, per):

            def top_step(r, tops):
                at = at_rows(r)
                return tuple(
                    jnp.maximum(top, jnp.max(group(t_ref[c + t, at, :] + wide_ref[at, :]), axis=0))
                    for t, top in enumerate(tops)
                )

            start = tuple(jnp.full((8, LANES), -jnp.inf, jnp.float32) for _ in range(per))
            tops = lax.fori_loop(0, rows // STEP, top_step, start)
            sums(c, [jnp.max(top, axis=0, keepdims=True) for top in tops])

    copies(out_ref, line_ref[...])


def plan_kernel(t_ref, parts_ref, tgt_mass_ref, src_lse_ref, src_mass_ref, *refs):
    plan_ref, out_ref, lse_ref, wide_ref, sum_ref, line_ref = refs
    tiles, rows, _ = t_ref.shape
    lse = combined(parts_ref, lse_all)
    lse_ref[...] = lse
    line_ref[...] = (tgt_mass_ref[...] - lse) * LOG2E
    spread((src_mass_ref[...] - src_lse_ref[...]) * LOG2E, wide_ref)
    per = 4

    def rows_step(r, unused):
        at = at_rows(r)
        total = jnp.zeros((STEP, LANES), jnp.float32)
        own = wide_ref[at, :]
        for c in range(0, tiles, per):
            terms = [t_ref[c + t, at, :] for t in range(per)]
            values = [
                jnp.exp2(terms[t] + own + line_ref[c + t : c + t + 1, :]) for t in range(per)
            ]
            for t in range(per):
                plan_ref[c + t, at, :] = values[t]
                total += values[t]
        sum_ref[at, :] = total
        return unused

    lax.fori_loop(0, rows // STEP, rows_step, 0)
    copies(out_ref, collapse(sum_ref))


def row_sums_kernel(plan_ref, parts_ref, mass_ref, out_ref, sum_ref, line_ref):
    tiles, rows, _ = plan_ref.shape
    line_ref[...] = jnp.exp(mass_ref[...]) / combined(parts_ref, add_all)

    def rows_step(r, unused):
        at = at_rows(r)
        total = jnp.zeros((STEP, LANES), jnp.float32)
        for t in range(tiles):
            total += plan_ref[t, at, :] * line_ref[t : t + 1, :]
        sum_ref[at, :] = total
        return unused

    lax.fori_loop(0, rows // STEP, rows_step, 0)
    copies(out_ref, collapse(sum_ref))


def column_sums(plan_ref, scale, line_ref, wide_ref):
    tiles, rows, _ = plan_ref.shape
    spread(scale, wide_ref)
    per = 16
    for c in range(0, tiles, per):

        def rows_step(r, totals):
            at = at_rows(r)
            own = wide_ref[at, :]
            return tuple(
                total
                + jnp.sum(
                    (plan_ref[c + t, at, :] * own).reshape(STEP // 8, 8, LANES), axis=0
                )
                for t, total in enumerate(totals)
            )

        start = tuple(jnp.zeros((8, LANES), jnp.float32) for _ in range(per))
        totals = lax.fori_loop(0, rows // STEP, rows_step, start)
        for t in range(per):
            line_ref[c + t : c + t + 1, :] = jnp.sum(totals[t], axis=0, keepdims=True)


def column_sums_kernel(plan_ref, parts_ref, mass_ref, out_ref, wide_ref, line_ref):
    scale = jnp.exp(mass_ref[...]) / combined(parts_ref, add_all)
    column_sums(plan_ref, scale, line_ref, wide_ref)
    copies(out_ref, line_ref[...])


def last_column_sums_kernel(plan_ref, parts_ref, mass_ref, lse_ref, squares_ref, *refs):
    out_ref, potential_ref, wide_ref, line_ref = refs
    sums = combined(parts_ref, add_all)
    mass = mass_ref[...]
    column_sums(plan_ref, jnp.exp(mass) / sums, line_ref, wide_ref)
    squares = squares_ref[...] / (WIDTH * EPS)
    potential = -EPS * (lse_ref[...] + jnp.log(sums) - mass - squares)
    potential_ref[...] = potential
    tiles = plan_ref.shape[0]
    line_ref[tiles:, :] = jnp.broadcast_to(jnp.sum(potential), (8, LANES))
    copies(out_ref, line_ref[...])


def last_kernel(parts_ref, mass_ref, lse_ref, potential_ref, own_ref, other_ref):
    tiles = mass_ref.shape[0]
    sums = combined(parts_ref, add_all)
    potential = -EPS * (lse_ref[...] + jnp.log(sums[:tiles]) - 2.0 * mass_ref[...])
    potential_ref[...] = potential
    copies(own_ref, jnp.broadcast_to(jnp.sum(potential), (8, LANES)))
    other_ref[...] = sums[tiles:]


ALL = ("row_0", "row_1", "col_0", "col_1")
SIZES = (4, 4, 4, 2)


def number(y, x, z, core):
    return ((y % 4 * 4 + x % 4) * 4 + z) * 2 + core


def turned(value, stage):
    found = {0: value}
    for k in (2, 1, 3):
        pairs = []
        for y, x, z, core in itertools.product(*map(range, SIZES)):
            along_y = (core + stage) % 2
            to = number(y + k * along_y, x + k * (1 - along_y), z, core)
            pairs.append((number(y, x, z, core), to))
        found[k] = lax.ppermute(value, ALL, pairs)
    return [found[k] for k in range(4)]


def body(src_points, tgt_points, log_src_mass, log_tgt_mass):
    rows, columns = src_points.shape[0], log_tgt_mass.shape[0]
    row_tiles, column_tiles = rows // LANES, columns // LANES
    src_mass = log_src_mass.reshape(row_tiles, LANES)
    tgt_mass = log_tgt_mass.reshape(column_tiles, LANES)
    place = jnp.stack([lax.axis_index(name) for name in ("row_0", "row_1", "col_1")])
    place = place.astype(jnp.int32)
    wide = pltpu.VMEM((rows, LANES), jnp.float32)
    big = pltpu.VMEM((column_tiles, rows, LANES), jnp.float32)
    line = pltpu.VMEM((column_tiles, LANES), jnp.float32)
    longer = pltpu.VMEM((column_tiles + 8, LANES), jnp.float32)
    by_row, by_column = f32(row_tiles, LANES), f32(column_tiles, LANES)
    peers_row, peers_col = lax.axis_size(ROW), lax.axis_size(COL)
    rows_out, columns_out = f32(peers_col, row_tiles, LANES), f32(peers_row, column_tiles, LANES)

    def resident(value):
        return pltpu.with_memory_space_constraint(value, pltpu.VMEM)

    def over_col(value):
        return lax.all_to_all(value, COL, 0, 0, tiled=True)

    def over_row(value):
        return lax.all_to_all(value, ROW, 0, 0, tiled=True)

    first = jnp.concatenate(turned(tgt_points, 0))
    pieces = turned(first, 1)
    terms, top, sums, squares = call(
        first_terms_kernel, (big, wide, wide, by_row), [SMEM] + [VMEM] * 3, []
    )(place, src_points, first, tgt_mass)
    for k in (1, 3):
        terms, sums = call(
            functools.partial(more_terms_kernel, k), (big, wide), [SMEM] + [VMEM] * 6, [], {2: 0, 3: 1}
        )(place, src_points, resident(terms), resident(sums), resident(top), pieces[k], tgt_mass)
    terms, sums, lse = call(
        functools.partial(last_terms_kernel, 2),
        (big, wide, rows_out),
        [SMEM] + [VMEM] * 6,
        [wide],
        {2: 0, 3: 1},
    )(place, src_points, resident(terms), resident(sums), resident(top), pieces[2], tgt_mass)
    lse, src_lse = call(column_kernel, (columns_out, by_row), [VMEM] * 3, [wide, line])(
        resident(terms), over_col(lse), src_mass
    )
    plan, sums, tgt_lse = call(
        plan_kernel, (big, rows_out, by_column), [VMEM] * 5, [wide, wide, line], {0: 0}
    )(resident(terms), over_row(lse), tgt_mass, src_lse, src_mass)
    plan = resident(plan)
    sums = call(column_sums_kernel, columns_out, [VMEM] * 3, [wide, line])(
        plan, over_col(sums), src_mass
    )
    sums = call(row_sums_kernel, rows_out, [VMEM] * 3, [wide, line])(plan, over_row(sums), tgt_mass)
    sums, src_potential = call(
        last_column_sums_kernel,
        (f32(peers_row, column_tiles + 8, LANES), by_row),
        [VMEM] * 5,
        [wide, longer],
    )(plan, over_col(sums), src_mass, src_lse, squares)
    tgt_potential, tgt_sum, src_sum = call(
        last_kernel, (by_column, f32(peers_col, 8, LANES), f32(8, LANES)), [VMEM] * 3, []
    )(over_row(sums), tgt_mass, tgt_lse)
    tgt_sum = jnp.sum(over_col(tgt_sum), axis=0)
    sources_all, targets_all = rows * peers_row, columns * peers_col
    mean_potentials = (src_sum / sources_all + tgt_sum / targets_all)[0, 0]
    return (src_potential.reshape(-1), tgt_potential.reshape(-1), mean_potentials)


def solution(mesh):
    finer = Mesh(mesh.devices.reshape(4, 4, 4, 2), ("row_0", "row_1", "col_0", "col_1"))
    placed = (P(ROW, None), P(COL_ROW, None), P(ROW), P(COL))
    return jax.shard_map(
        body, mesh=finer, in_specs=placed, out_specs=(P(ROW), P(COL), P()), check_vma=False
    )
```

```python
import functools
import itertools
import math

import jax
import jax.numpy as jnp
from jax import lax
from jax.experimental import pallas as pl
from jax.experimental.pallas import tpu as pltpu
from jax.sharding import Mesh
from jax.sharding import PartitionSpec as P

ROW = ("row_0", "row_1")
COL = ("col_0", "col_1")
COL_ROW = ("col_0", "col_1", "row_0", "row_1")

EPS = 0.1
WIDTH = 256
NATS = 2.0 / (WIDTH * EPS)
BITS = NATS * math.log2(math.e)
LOG2E = math.log2(math.e)
LN2 = math.log(2.0)
VMEM_LIMIT = 24 * 1024 * 1024
LANES = 128
STEP = 64
ROWS = 512
HUGE = 3.0e38

VMEM = pl.BlockSpec(memory_space=pltpu.VMEM)
SMEM = pl.BlockSpec(memory_space=pltpu.SMEM)


def call(kernel, outs, ins, scratch, aliases=None):
    return pl.pallas_call(
        kernel,
        out_shape=outs,
        in_specs=ins,
        out_specs=jax.tree.map(lambda _: VMEM, outs),
        scratch_shapes=scratch,
        input_output_aliases=aliases or {},
        compiler_params=pltpu.CompilerParams(vmem_limit_bytes=VMEM_LIMIT),
    )


def f32(*shape):
    return jax.ShapeDtypeStruct(shape, jnp.float32)


def spread(dense, wide_ref):
    for b in range(dense.shape[0]):
        square = jnp.broadcast_to(dense[b : b + 1, :], (LANES, LANES))
        wide_ref[b * LANES : (b + 1) * LANES, :] = square.T


def collapse(wide_ref):
    lines = [
        jnp.sum(wide_ref[b * LANES : (b + 1) * LANES, :].T, axis=0, keepdims=True)
        for b in range(wide_ref.shape[0] // LANES)
    ]
    return jnp.concatenate(lines, axis=0)


def collapse_top(wide_ref):
    lines = [
        wide_ref[b * LANES : (b + 1) * LANES, :].T[:1, :]
        for b in range(wide_ref.shape[0] // LANES)
    ]
    return jnp.concatenate(lines, axis=0)


def add_all(parts):
    total = parts[0]
    for part in parts[1:]:
        total = total + part
    return total


def lse_all(parts):
    top = parts[0]
    for part in parts[1:]:
        top = jnp.maximum(top, part)
    return top + jnp.log(add_all([jnp.exp(part - top) for part in parts]))


def copies(out_ref, value):
    for peer in range(out_ref.shape[0]):
        out_ref[peer] = value


def combined(parts_ref, combine):
    return combine([parts_ref[peer] for peer in range(parts_ref.shape[0])])


def values(refs):
    return [ref[...] for ref in refs]


def at_rows(r):
    return pl.ds(pl.multiple_of(r * STEP, STEP), STEP)


def lane_tile(t):
    return slice(t * LANES, (t + 1) * LANES)


def target_block(place, shift, inner):
    first_core = place[2] == 0
    shift_y = jnp.where(first_core, shift, inner)
    shift_x = jnp.where(first_core, inner, shift)
    return 4 * lax.rem(place[0] + 4 - shift_y, 4) + lax.rem(place[1] + 4 - shift_x, 4)


def chunk_biases(points, mass_ref, block):
    squares = points.astype(jnp.float32) ** 2
    squares = squares[:, :LANES] + squares[:, LANES:]
    found = []
    for side in range(2):
        square = squares[side * LANES : (side + 1) * LANES, :].T
        mass = mass_ref[pl.ds(2 * block + side, 1), :]
        found.append(mass * LOG2E - jnp.sum(square, axis=0, keepdims=True) * (0.5 * BITS))
    return found


def piece_product(x_ref, points_ref, r, m):
    return lax.dot_general(
        x_ref[r : r + ROWS, :],
        points_ref[m * 256 : (m + 1) * 256, :],
        (((1,), (1,)), ((), ())),
        preferred_element_type=jnp.float32,
    )


def piece_blocks(k, place, points_ref, mass_ref):
    blocks = [target_block(place, k, m) for m in range(4)]
    biases = [
        chunk_biases(points_ref[m * 256 : (m + 1) * 256, :], mass_ref, blocks[m]) for m in range(4)
    ]
    return blocks, biases


def first_terms_kernel(place, x_ref, points_ref, mass_ref, t_ref, top_ref, sum_ref, squares_ref):
    rows = x_ref.shape[0]
    squares = x_ref[...].astype(jnp.float32) ** 2
    sum_ref[...] = squares[:, :LANES] + squares[:, LANES:]
    squares_ref[...] = collapse(sum_ref)
    blocks, biases = piece_blocks(0, place, points_ref, mass_ref)
    for r in range(0, rows, ROWS):
        top = None
        for m in range(4):
            product = piece_product(x_ref, points_ref, r, m)
            for side in range(2):
                terms = product[:, lane_tile(side)] * BITS + biases[m][side]
                t_ref[2 * blocks[m] + side, r : r + ROWS, :] = terms
                top = terms if top is None else jnp.maximum(top, terms)
        top_ref[r : r + ROWS, :] = top

    def rows_step(r, unused):
        at = at_rows(r)
        top = jnp.max(top_ref[at, :], axis=1, keepdims=True)
        total = jnp.zeros((STEP, LANES), jnp.float32)
        for m in range(4):
            for side in range(2):
                total += jnp.exp2(t_ref[2 * blocks[m] + side, at, :] - top)
        top_ref[at, :] = jnp.broadcast_to(top, (STEP, LANES))
        sum_ref[at, :] = total
        return unused

    lax.fori_loop(0, rows // STEP, rows_step, 0)


def piece_steps(k, place, x_ref, points_ref, mass_ref, top_ref, old_sum_ref, t_ref, sum_ref):
    blocks, biases = piece_blocks(k, place, points_ref, mass_ref)
    for r in range(0, x_ref.shape[0], ROWS):
        top = top_ref[r : r + ROWS, :]
        total = old_sum_ref[r : r + ROWS, :]
        for m in range(4):
            product = piece_product(x_ref, points_ref, r, m)
            for side in range(2):
                terms = product[:, lane_tile(side)] * BITS + biases[m][side]
                t_ref[2 * blocks[m] + side, r : r + ROWS, :] = terms
                total += jnp.exp2(terms - top)
        sum_ref[r : r + ROWS, :] = total


def more_terms_kernel(k, place, x_ref, old_ref, old_sum_ref, top_ref, points_ref, mass_ref, *refs):
    t_ref, sum_ref = refs
    piece_steps(k, place, x_ref, points_ref, mass_ref, top_ref, old_sum_ref, t_ref, sum_ref)


def last_terms_kernel(k, place, x_ref, old_ref, old_sum_ref, old_top_ref, points_ref, mass_ref, *refs):
    t_ref, sum_ref, out_ref, top_ref = refs
    tiles, rows, _ = t_ref.shape
    piece_steps(k, place, x_ref, points_ref, mass_ref, old_top_ref, old_sum_ref, t_ref, sum_ref)
    total = collapse(sum_ref)
    out_ref[...] = collapse_top(old_top_ref) * LN2 + jnp.log(total)

    @pl.when(jnp.logical_not(jnp.max(total) < HUGE))
    def exact():
        def rows_step(r, unused):
            at = at_rows(r)
            top = jnp.full((STEP, LANES), -jnp.inf, jnp.float32)
            for t in range(tiles):
                top = jnp.maximum(top, t_ref[t, at, :])
            top = jnp.max(top, axis=1, keepdims=True)
            total = jnp.zeros((STEP, LANES), jnp.float32)
            for t in range(tiles):
                total += jnp.exp2(t_ref[t, at, :] - top)
            top_ref[at, :] = jnp.broadcast_to(top, (STEP, LANES))
            sum_ref[at, :] = total
            return unused

        lax.fori_loop(0, rows // STEP, rows_step, 0)
        out_ref[...] = collapse_top(top_ref) * LN2 + jnp.log(collapse(sum_ref))


def column_kernel(t_ref, *refs):
    parts, (mass_ref, out_ref, lse_ref, wide_ref, line_ref) = refs[:4], refs[4:]
    tiles, rows, _ = t_ref.shape
    lse = lse_all(values(parts))
    lse_ref[...] = lse
    spread((mass_ref[...] - lse) * LOG2E, wide_ref)
    per = 4

    def group(value):
        return value.reshape(STEP // 8, 8, LANES)

    def sums(c, tops):
        wide = [jnp.broadcast_to(top, (STEP, LANES)) for top in tops]

        def sum_step(r, totals):
            at = at_rows(r)
            own = wide_ref[at, :]
            return tuple(
                total
                + jnp.sum(
                    group(jnp.exp2(t_ref[c + t, at, :] + own - wide[t])), axis=0
                )
                for t, total in enumerate(totals)
            )

        start = tuple(jnp.zeros((8, LANES), jnp.float32) for _ in range(per))
        totals = lax.fori_loop(0, rows // STEP, sum_step, start)
        for t in range(per):
            total = jnp.sum(totals[t], axis=0, keepdims=True)
            line_ref[c + t : c + t + 1, :] = tops[t] * LN2 + jnp.log(total)

    for c in range(0, tiles, per):
        tops = [
            jnp.max(t_ref[c + t, :STEP, :] + wide_ref[:STEP, :], axis=0, keepdims=True)
            for t in range(per)
        ]
        sums(c, tops)

    @pl.when(jnp.logical_not(jnp.max(line_ref[...]) < HUGE))
    def exact():
        for c in range(0, tiles, per):

            def top_step(r, tops):
                at = at_rows(r)
                return tuple(
                    jnp.maximum(top, jnp.max(group(t_ref[c + t, at, :] + wide_ref[at, :]), axis=0))
                    for t, top in enumerate(tops)
                )

            start = tuple(jnp.full((8, LANES), -jnp.inf, jnp.float32) for _ in range(per))
            tops = lax.fori_loop(0, rows // STEP, top_step, start)
            sums(c, [jnp.max(top, axis=0, keepdims=True) for top in tops])

    copies(out_ref, line_ref[...])


def plan_kernel(t_ref, parts_ref, tgt_mass_ref, src_lse_ref, src_mass_ref, *refs):
    plan_ref, out_ref, lse_ref, wide_ref, sum_ref, line_ref = refs
    tiles, rows, _ = t_ref.shape
    lse = combined(parts_ref, lse_all)
    lse_ref[...] = lse
    line_ref[...] = (tgt_mass_ref[...] - lse) * LOG2E
    spread((src_mass_ref[...] - src_lse_ref[...]) * LOG2E, wide_ref)
    per = 4

    def rows_step(r, unused):
        at = at_rows(r)
        total = jnp.zeros((STEP, LANES), jnp.float32)
        own = wide_ref[at, :]
        for c in range(0, tiles, per):
            terms = [t_ref[c + t, at, :] for t in range(per)]
            values = [
                jnp.exp2(terms[t] + own + line_ref[c + t : c + t + 1, :]) for t in range(per)
            ]
            for t in range(per):
                plan_ref[c + t, at, :] = values[t]
                total += values[t]
        sum_ref[at, :] = total
        return unused

    lax.fori_loop(0, rows // STEP, rows_step, 0)
    out_ref[...] = collapse(sum_ref)


def row_sums_kernel(plan_ref, parts_ref, mass_ref, out_ref, sum_ref, line_ref):
    tiles, rows, _ = plan_ref.shape
    line_ref[...] = jnp.exp(mass_ref[...]) / combined(parts_ref, add_all)

    def rows_step(r, unused):
        at = at_rows(r)
        total = jnp.zeros((STEP, LANES), jnp.float32)
        for t in range(tiles):
            total += plan_ref[t, at, :] * line_ref[t : t + 1, :]
        sum_ref[at, :] = total
        return unused

    lax.fori_loop(0, rows // STEP, rows_step, 0)
    out_ref[...] = collapse(sum_ref)


def column_sums(plan_ref, scale, line_ref, wide_ref):
    tiles, rows, _ = plan_ref.shape
    spread(scale, wide_ref)
    per = 16
    for c in range(0, tiles, per):

        def rows_step(r, totals):
            at = at_rows(r)
            own = wide_ref[at, :]
            return tuple(
                total
                + jnp.sum(
                    (plan_ref[c + t, at, :] * own).reshape(STEP // 8, 8, LANES), axis=0
                )
                for t, total in enumerate(totals)
            )

        start = tuple(jnp.zeros((8, LANES), jnp.float32) for _ in range(per))
        totals = lax.fori_loop(0, rows // STEP, rows_step, start)
        for t in range(per):
            line_ref[c + t : c + t + 1, :] = jnp.sum(totals[t], axis=0, keepdims=True)


def column_sums_kernel(plan_ref, *refs):
    parts, (mass_ref, out_ref, wide_ref, line_ref) = refs[:4], refs[4:]
    scale = jnp.exp(mass_ref[...]) / add_all(values(parts))
    column_sums(plan_ref, scale, line_ref, wide_ref)
    copies(out_ref, line_ref[...])


def last_column_sums_kernel(plan_ref, *refs):
    parts, (mass_ref, lse_ref, squares_ref) = refs[:4], refs[4:7]
    out_ref, potential_ref, wide_ref, line_ref = refs[7:]
    sums = add_all(values(parts))
    mass = mass_ref[...]
    column_sums(plan_ref, jnp.exp(mass) / sums, line_ref, wide_ref)
    squares = squares_ref[...] / (WIDTH * EPS)
    potential = -EPS * (lse_ref[...] + jnp.log(sums) - mass - squares)
    potential_ref[...] = potential
    tiles = plan_ref.shape[0]
    line_ref[tiles:, :] = jnp.broadcast_to(jnp.sum(potential), (8, LANES))
    copies(out_ref, line_ref[...])


def last_kernel(parts_ref, mass_ref, lse_ref, potential_ref, own_ref, other_ref):
    tiles = mass_ref.shape[0]
    sums = combined(parts_ref, add_all)
    potential = -EPS * (lse_ref[...] + jnp.log(sums[:tiles]) - 2.0 * mass_ref[...])
    potential_ref[...] = potential
    own_ref[...] = jnp.broadcast_to(jnp.sum(potential), (8, LANES))
    other_ref[...] = sums[tiles:]


ALL = ("row_0", "row_1", "col_0", "col_1")
SIZES = (4, 4, 4, 2)


def number(y, x, z, core):
    return ((y % 4 * 4 + x % 4) * 4 + z) * 2 + core


def turned(value, stage):
    found = {0: value}
    for k in (2, 1, 3):
        pairs = []
        for y, x, z, core in itertools.product(*map(range, SIZES)):
            along_y = (core + stage) % 2
            to = number(y + k * along_y, x + k * (1 - along_y), z, core)
            pairs.append((number(y, x, z, core), to))
        found[k] = lax.ppermute(value, ALL, pairs)
    return [found[k] for k in range(4)]


def crossed(value, k):
    pairs = []
    for y, x, z, core in itertools.product(*map(range, SIZES)):
        pairs.append((number(y, x, z, core), number(y, x, (z + k) % 4, 1 - core)))
    return lax.ppermute(value, ALL, pairs)


def body(src_points, tgt_points, log_src_mass, log_tgt_mass):
    rows, columns = src_points.shape[0], log_tgt_mass.shape[0]
    row_tiles, column_tiles = rows // LANES, columns // LANES
    src_mass = log_src_mass.reshape(row_tiles, LANES)
    tgt_mass = log_tgt_mass.reshape(column_tiles, LANES)
    place = jnp.stack([lax.axis_index(name) for name in ("row_0", "row_1", "col_1")])
    place = place.astype(jnp.int32)
    wide = pltpu.VMEM((rows, LANES), jnp.float32)
    big = pltpu.VMEM((column_tiles, rows, LANES), jnp.float32)
    line = pltpu.VMEM((column_tiles, LANES), jnp.float32)
    longer = pltpu.VMEM((column_tiles + 8, LANES), jnp.float32)
    by_row, by_column = f32(row_tiles, LANES), f32(column_tiles, LANES)
    peers_row, peers_col = lax.axis_size(ROW), lax.axis_size(COL)
    columns_out = f32(peers_row, column_tiles, LANES)

    def resident(value):
        return pltpu.with_memory_space_constraint(value, pltpu.VMEM)

    def over_col(value, combine):
        both = combine([value, lax.ppermute(value, "col_1", [(0, 1), (1, 0)])])
        return [both] + [crossed(both, k) for k in (2, 1, 3)]

    def over_row(value):
        return lax.all_to_all(value, ROW, 0, 0, tiled=True)

    first = jnp.concatenate(turned(tgt_points, 0))
    pieces = turned(first, 1)
    terms, top, sums, squares = call(
        first_terms_kernel, (big, wide, wide, by_row), [SMEM] + [VMEM] * 3, []
    )(place, src_points, first, tgt_mass)
    for k in (1, 3):
        terms, sums = call(
            functools.partial(more_terms_kernel, k), (big, wide), [SMEM] + [VMEM] * 6, [], {2: 0, 3: 1}
        )(place, src_points, resident(terms), resident(sums), resident(top), pieces[k], tgt_mass)
    terms, sums, lse = call(
        functools.partial(last_terms_kernel, 2),
        (big, wide, by_row),
        [SMEM] + [VMEM] * 6,
        [wide],
        {2: 0, 3: 1},
    )(place, src_points, resident(terms), resident(sums), resident(top), pieces[2], tgt_mass)
    lse, src_lse = call(column_kernel, (columns_out, by_row), [VMEM] * 6, [wide, line])(
        resident(terms), *over_col(lse, lse_all), src_mass
    )
    plan, sums, tgt_lse = call(
        plan_kernel, (big, by_row, by_column), [VMEM] * 5, [wide, wide, line], {0: 0}
    )(resident(terms), over_row(lse), tgt_mass, src_lse, src_mass)
    plan = resident(plan)
    sums = call(column_sums_kernel, columns_out, [VMEM] * 6, [wide, line])(
        plan, *over_col(sums, add_all), src_mass
    )
    sums = call(row_sums_kernel, by_row, [VMEM] * 3, [wide, line])(plan, over_row(sums), tgt_mass)
    sums, src_potential = call(
        last_column_sums_kernel,
        (f32(peers_row, column_tiles + 8, LANES), by_row),
        [VMEM] * 8,
        [wide, longer],
    )(plan, *over_col(sums, add_all), src_mass, src_lse, squares)
    tgt_potential, tgt_sum, src_sum = call(
        last_kernel, (by_column, f32(8, LANES), f32(8, LANES)), [VMEM] * 3, []
    )(over_row(sums), tgt_mass, tgt_lse)
    tgt_sum = add_all(over_col(tgt_sum, add_all))
    sources_all, targets_all = rows * peers_row, columns * peers_col
    mean_potentials = (src_sum / sources_all + tgt_sum / targets_all)[0, 0]
    return (src_potential.reshape(-1), tgt_potential.reshape(-1), mean_potentials)


def solution(mesh):
    finer = Mesh(mesh.devices.reshape(4, 4, 4, 2), ("row_0", "row_1", "col_0", "col_1"))
    placed = (P(ROW, None), P(COL_ROW, None), P(ROW), P(COL))
    return jax.shard_map(
        body, mesh=finer, in_specs=placed, out_specs=(P(ROW), P(COL), P()), check_vma=False
    )
```

```python
import functools
import itertools
import math

import jax
import jax.numpy as jnp
from jax import lax
from jax.experimental import pallas as pl
from jax.experimental.pallas import tpu as pltpu
from jax.sharding import Mesh
from jax.sharding import PartitionSpec as P

ROW = ("row_0", "row_1")
COL = ("col_0", "col_1")
COL_ROW = ("col_0", "col_1", "row_0", "row_1")

EPS = 0.1
WIDTH = 256
NATS = 2.0 / (WIDTH * EPS)
BITS = NATS * math.log2(math.e)
LOG2E = math.log2(math.e)
LN2 = math.log(2.0)
VMEM_LIMIT = 24 * 1024 * 1024
LANES = 128
STEP = 64
ROWS = 512
HUGE = 3.0e38

VMEM = pl.BlockSpec(memory_space=pltpu.VMEM)
SMEM = pl.BlockSpec(memory_space=pltpu.SMEM)


def call(kernel, outs, ins, scratch, aliases=None):
    return pl.pallas_call(
        kernel,
        out_shape=outs,
        in_specs=ins,
        out_specs=jax.tree.map(lambda _: VMEM, outs),
        scratch_shapes=scratch,
        input_output_aliases=aliases or {},
        compiler_params=pltpu.CompilerParams(vmem_limit_bytes=VMEM_LIMIT),
    )


def f32(*shape):
    return jax.ShapeDtypeStruct(shape, jnp.float32)


def spread(dense, wide_ref):
    for b in range(dense.shape[0]):
        square = jnp.broadcast_to(dense[b : b + 1, :], (LANES, LANES))
        wide_ref[b * LANES : (b + 1) * LANES, :] = square.T


def collapse(wide_ref):
    lines = [
        jnp.sum(wide_ref[b * LANES : (b + 1) * LANES, :].T, axis=0, keepdims=True)
        for b in range(wide_ref.shape[0] // LANES)
    ]
    return jnp.concatenate(lines, axis=0)


def collapse_top(wide_ref):
    lines = [
        wide_ref[b * LANES : (b + 1) * LANES, :].T[:1, :]
        for b in range(wide_ref.shape[0] // LANES)
    ]
    return jnp.concatenate(lines, axis=0)


def add_all(parts):
    total = parts[0]
    for part in parts[1:]:
        total = total + part
    return total


def lse_all(parts):
    top = parts[0]
    for part in parts[1:]:
        top = jnp.maximum(top, part)
    return top + jnp.log(add_all([jnp.exp(part - top) for part in parts]))


def copies(out_ref, value):
    for peer in range(out_ref.shape[0]):
        out_ref[peer] = value


def combined(parts_ref, combine):
    return combine([parts_ref[peer] for peer in range(parts_ref.shape[0])])


def values(refs):
    return [ref[...] for ref in refs]


def at_rows(r):
    return pl.ds(pl.multiple_of(r * STEP, STEP), STEP)


def lane_tile(t):
    return slice(t * LANES, (t + 1) * LANES)


def target_block(place, shift, inner):
    first_core = place[2] == 0
    shift_y = jnp.where(first_core, shift, inner)
    shift_x = jnp.where(first_core, inner, shift)
    return 4 * lax.rem(place[0] + 4 - shift_y, 4) + lax.rem(place[1] + 4 - shift_x, 4)


def chunk_biases(points, mass_ref, block):
    squares = points.astype(jnp.float32) ** 2
    squares = squares[:, :LANES] + squares[:, LANES:]
    found = []
    for side in range(2):
        square = squares[side * LANES : (side + 1) * LANES, :].T
        mass = mass_ref[pl.ds(2 * block + side, 1), :]
        found.append(mass * LOG2E - jnp.sum(square, axis=0, keepdims=True) * (0.5 * BITS))
    return found


def piece_product(x_ref, points_ref, r, m):
    return lax.dot_general(
        x_ref[r : r + ROWS, :],
        points_ref[m * 256 : (m + 1) * 256, :],
        (((1,), (1,)), ((), ())),
        preferred_element_type=jnp.float32,
    )


def own_terms_kernel(place, x_ref, points_ref, mass_ref, t_ref, top_ref, sum_ref, squares_ref):
    rows = x_ref.shape[0]
    squares = x_ref[...].astype(jnp.float32) ** 2
    sum_ref[...] = squares[:, :LANES] + squares[:, LANES:]
    squares_ref[...] = collapse(sum_ref)
    block = target_block(place, 0, 0)
    biases = chunk_biases(points_ref[...], mass_ref, block)
    for r in range(0, rows, ROWS):
        at = slice(r, r + ROWS)
        product = piece_product(x_ref, points_ref, r, 0)
        both = [product[:, lane_tile(side)] * BITS + biases[side] for side in range(2)]
        for side in range(2):
            t_ref[2 * block + side, at, :] = both[side]
        top = jnp.max(jnp.maximum(both[0], both[1]), axis=1, keepdims=True)
        top_ref[at, :] = jnp.broadcast_to(top, (ROWS, LANES))
        sum_ref[at, :] = jnp.exp2(both[0] - top) + jnp.exp2(both[1] - top)


def piece_steps(spots, place, x_ref, points_ref, mass_ref, top_ref, old_sum_ref, t_ref, sum_ref):
    blocks = [target_block(place, k, m) for k, m in spots]
    first = points_ref.shape[0] // 256 - len(spots)
    biases = [
        chunk_biases(points_ref[(first + i) * 256 : (first + i + 1) * 256, :], mass_ref, block)
        for i, block in enumerate(blocks)
    ]
    for r in range(0, x_ref.shape[0], ROWS):
        top = top_ref[r : r + ROWS, :]
        total = old_sum_ref[r : r + ROWS, :]
        for i, block in enumerate(blocks):
            product = piece_product(x_ref, points_ref, r, first + i)
            for side in range(2):
                terms = product[:, lane_tile(side)] * BITS + biases[i][side]
                t_ref[2 * block + side, r : r + ROWS, :] = terms
                total += jnp.exp2(terms - top)
        sum_ref[r : r + ROWS, :] = total


def more_terms_kernel(spots, place, x_ref, old_ref, old_sum_ref, top_ref, points_ref, mass_ref, *refs):
    t_ref, sum_ref = refs
    piece_steps(spots, place, x_ref, points_ref, mass_ref, top_ref, old_sum_ref, t_ref, sum_ref)


def last_terms_kernel(spots, place, x_ref, old_ref, old_sum_ref, old_top_ref, points_ref, mass_ref, *refs):
    t_ref, sum_ref, out_ref, top_ref = refs
    tiles, rows, _ = t_ref.shape
    piece_steps(spots, place, x_ref, points_ref, mass_ref, old_top_ref, old_sum_ref, t_ref, sum_ref)
    total = collapse(sum_ref)
    out_ref[...] = collapse_top(old_top_ref) * LN2 + jnp.log(total)

    @pl.when(jnp.logical_not(jnp.max(total) < HUGE))
    def exact():
        def rows_step(r, unused):
            at = at_rows(r)
            top = jnp.full((STEP, LANES), -jnp.inf, jnp.float32)
            for t in range(tiles):
                top = jnp.maximum(top, t_ref[t, at, :])
            top = jnp.max(top, axis=1, keepdims=True)
            total = jnp.zeros((STEP, LANES), jnp.float32)
            for t in range(tiles):
                total += jnp.exp2(t_ref[t, at, :] - top)
            top_ref[at, :] = jnp.broadcast_to(top, (STEP, LANES))
            sum_ref[at, :] = total
            return unused

        lax.fori_loop(0, rows // STEP, rows_step, 0)
        out_ref[...] = collapse_top(top_ref) * LN2 + jnp.log(collapse(sum_ref))


def column_kernel(t_ref, *refs):
    parts, (mass_ref, out_ref, lse_ref, wide_ref, line_ref) = refs[:4], refs[4:]
    tiles, rows, _ = t_ref.shape
    lse = lse_all(values(parts))
    lse_ref[...] = lse
    spread((mass_ref[...] - lse) * LOG2E, wide_ref)
    per = 4

    def group(value):
        return value.reshape(STEP // 8, 8, LANES)

    def sums(c, tops):
        wide = [jnp.broadcast_to(top, (STEP, LANES)) for top in tops]

        def sum_step(r, totals):
            at = at_rows(r)
            own = wide_ref[at, :]
            return tuple(
                total
                + jnp.sum(
                    group(jnp.exp2(t_ref[c + t, at, :] + own - wide[t])), axis=0
                )
                for t, total in enumerate(totals)
            )

        start = tuple(jnp.zeros((8, LANES), jnp.float32) for _ in range(per))
        totals = lax.fori_loop(0, rows // STEP, sum_step, start)
        for t in range(per):
            total = jnp.sum(totals[t], axis=0, keepdims=True)
            line_ref[c + t : c + t + 1, :] = tops[t] * LN2 + jnp.log(total)

    for c in range(0, tiles, per):
        tops = [
            jnp.max(t_ref[c + t, :STEP, :] + wide_ref[:STEP, :], axis=0, keepdims=True)
            for t in range(per)
        ]
        sums(c, tops)

    @pl.when(jnp.logical_not(jnp.max(line_ref[...]) < HUGE))
    def exact():
        for c in range(0, tiles, per):

            def top_step(r, tops):
                at = at_rows(r)
                return tuple(
                    jnp.maximum(top, jnp.max(group(t_ref[c + t, at, :] + wide_ref[at, :]), axis=0))
                    for t, top in enumerate(tops)
                )

            start = tuple(jnp.full((8, LANES), -jnp.inf, jnp.float32) for _ in range(per))
            tops = lax.fori_loop(0, rows // STEP, top_step, start)
            sums(c, [jnp.max(top, axis=0, keepdims=True) for top in tops])

    copies(out_ref, line_ref[...])


def plan_kernel(t_ref, parts_ref, tgt_mass_ref, src_lse_ref, src_mass_ref, *refs):
    plan_ref, out_ref, lse_ref, wide_ref, sum_ref, line_ref = refs
    tiles, rows, _ = t_ref.shape
    lse = combined(parts_ref, lse_all)
    lse_ref[...] = lse
    line_ref[...] = (tgt_mass_ref[...] - lse) * LOG2E
    spread((src_mass_ref[...] - src_lse_ref[...]) * LOG2E, wide_ref)
    per = 4

    def rows_step(r, unused):
        at = at_rows(r)
        total = jnp.zeros((STEP, LANES), jnp.float32)
        own = wide_ref[at, :]
        for c in range(0, tiles, per):
            terms = [t_ref[c + t, at, :] for t in range(per)]
            values = [
                jnp.exp2(terms[t] + own + line_ref[c + t : c + t + 1, :]) for t in range(per)
            ]
            for t in range(per):
                plan_ref[c + t, at, :] = values[t]
                total += values[t]
        sum_ref[at, :] = total
        return unused

    lax.fori_loop(0, rows // STEP, rows_step, 0)
    out_ref[...] = collapse(sum_ref)


def row_sums_kernel(plan_ref, parts_ref, mass_ref, out_ref, sum_ref, line_ref):
    tiles, rows, _ = plan_ref.shape
    line_ref[...] = jnp.exp(mass_ref[...]) / combined(parts_ref, add_all)

    def rows_step(r, unused):
        at = at_rows(r)
        total = jnp.zeros((STEP, LANES), jnp.float32)
        for t in range(tiles):
            total += plan_ref[t, at, :] * line_ref[t : t + 1, :]
        sum_ref[at, :] = total
        return unused

    lax.fori_loop(0, rows // STEP, rows_step, 0)
    out_ref[...] = collapse(sum_ref)


def column_sums(plan_ref, scale, line_ref, wide_ref):
    tiles, rows, _ = plan_ref.shape
    spread(scale, wide_ref)
    per = 16
    for c in range(0, tiles, per):

        def rows_step(r, totals):
            at = at_rows(r)
            own = wide_ref[at, :]
            return tuple(
                total
                + jnp.sum(
                    (plan_ref[c + t, at, :] * own).reshape(STEP // 8, 8, LANES), axis=0
                )
                for t, total in enumerate(totals)
            )

        start = tuple(jnp.zeros((8, LANES), jnp.float32) for _ in range(per))
        totals = lax.fori_loop(0, rows // STEP, rows_step, start)
        for t in range(per):
            line_ref[c + t : c + t + 1, :] = jnp.sum(totals[t], axis=0, keepdims=True)


def column_sums_kernel(plan_ref, *refs):
    parts, (mass_ref, out_ref, wide_ref, line_ref) = refs[:4], refs[4:]
    scale = jnp.exp(mass_ref[...]) / add_all(values(parts))
    column_sums(plan_ref, scale, line_ref, wide_ref)
    copies(out_ref, line_ref[...])


def last_column_sums_kernel(plan_ref, *refs):
    parts, (mass_ref, lse_ref, squares_ref) = refs[:4], refs[4:7]
    out_ref, potential_ref, wide_ref, line_ref = refs[7:]
    sums = add_all(values(parts))
    mass = mass_ref[...]
    column_sums(plan_ref, jnp.exp(mass) / sums, line_ref, wide_ref)
    squares = squares_ref[...] / (WIDTH * EPS)
    potential = -EPS * (lse_ref[...] + jnp.log(sums) - mass - squares)
    potential_ref[...] = potential
    tiles = plan_ref.shape[0]
    line_ref[tiles:, :] = jnp.broadcast_to(jnp.sum(potential), (8, LANES))
    copies(out_ref, line_ref[...])


def last_kernel(parts_ref, mass_ref, lse_ref, potential_ref, own_ref, other_ref):
    tiles = mass_ref.shape[0]
    sums = combined(parts_ref, add_all)
    potential = -EPS * (lse_ref[...] + jnp.log(sums[:tiles]) - 2.0 * mass_ref[...])
    potential_ref[...] = potential
    own_ref[...] = jnp.broadcast_to(jnp.sum(potential), (8, LANES))
    other_ref[...] = sums[tiles:]


ALL = ("row_0", "row_1", "col_0", "col_1")
SIZES = (4, 4, 4, 2)


def number(y, x, z, core):
    return ((y % 4 * 4 + x % 4) * 4 + z) * 2 + core


def turned(value, stage, order):
    found = {0: value}
    for k in order:
        pairs = []
        for y, x, z, core in itertools.product(*map(range, SIZES)):
            along_y = (core + stage) % 2
            to = number(y + k * along_y, x + k * (1 - along_y), z, core)
            pairs.append((number(y, x, z, core), to))
        found[k] = lax.ppermute(value, ALL, pairs)
    return [found[k] for k in range(4)]


def crossed(value, k):
    pairs = []
    for y, x, z, core in itertools.product(*map(range, SIZES)):
        pairs.append((number(y, x, z, core), number(y, x, (z + k) % 4, 1 - core)))
    return lax.ppermute(value, ALL, pairs)


def body(src_points, tgt_points, log_src_mass, log_tgt_mass):
    rows, columns = src_points.shape[0], log_tgt_mass.shape[0]
    row_tiles, column_tiles = rows // LANES, columns // LANES
    src_mass = log_src_mass.reshape(row_tiles, LANES)
    tgt_mass = log_tgt_mass.reshape(column_tiles, LANES)
    place = jnp.stack([lax.axis_index(name) for name in ("row_0", "row_1", "col_1")])
    place = place.astype(jnp.int32)
    wide = pltpu.VMEM((rows, LANES), jnp.float32)
    big = pltpu.VMEM((column_tiles, rows, LANES), jnp.float32)
    line = pltpu.VMEM((column_tiles, LANES), jnp.float32)
    longer = pltpu.VMEM((column_tiles + 8, LANES), jnp.float32)
    by_row, by_column = f32(row_tiles, LANES), f32(column_tiles, LANES)
    peers_row, peers_col = lax.axis_size(ROW), lax.axis_size(COL)
    columns_out = f32(peers_row, column_tiles, LANES)

    def resident(value):
        return pltpu.with_memory_space_constraint(value, pltpu.VMEM)

    def over_col(value, combine):
        both = combine([value, lax.ppermute(value, "col_1", [(0, 1), (1, 0)])])
        return [both] + [crossed(both, k) for k in (2, 1, 3)]

    def over_row(value):
        return lax.all_to_all(value, ROW, 0, 0, tiled=True)

    found = turned(tgt_points, 0, (1, 2, 3))
    halves = [jnp.concatenate(found[:2]), jnp.concatenate(found[2:])]
    pieces = [(halves[0], [(0, 1)]), (halves[1], [(0, 2), (0, 3)])]
    for q in range(2):
        found = turned(halves[q], 1, (1, 2, 3))
        pieces += [(found[k], [(k, 2 * q), (k, 2 * q + 1)]) for k in (1, 2, 3)]
    terms, top, sums, squares = call(
        own_terms_kernel, (big, wide, wide, by_row), [SMEM] + [VMEM] * 3, []
    )(place, src_points, tgt_points, tgt_mass)
    for piece, spots in pieces[:-1]:
        terms, sums = call(
            functools.partial(more_terms_kernel, spots),
            (big, wide),
            [SMEM] + [VMEM] * 6,
            [],
            {2: 0, 3: 1},
        )(place, src_points, resident(terms), resident(sums), resident(top), piece, tgt_mass)
    piece, spots = pieces[-1]
    terms, sums, lse = call(
        functools.partial(last_terms_kernel, spots),
        (big, wide, by_row),
        [SMEM] + [VMEM] * 6,
        [wide],
        {2: 0, 3: 1},
    )(place, src_points, resident(terms), resident(sums), resident(top), piece, tgt_mass)
    lse, src_lse = call(column_kernel, (columns_out, by_row), [VMEM] * 6, [wide, line])(
        resident(terms), *over_col(lse, lse_all), src_mass
    )
    plan, sums, tgt_lse = call(
        plan_kernel, (big, by_row, by_column), [VMEM] * 5, [wide, wide, line], {0: 0}
    )(resident(terms), over_row(lse), tgt_mass, src_lse, src_mass)
    plan = resident(plan)
    sums = call(column_sums_kernel, columns_out, [VMEM] * 6, [wide, line])(
        plan, *over_col(sums, add_all), src_mass
    )
    sums = call(row_sums_kernel, by_row, [VMEM] * 3, [wide, line])(plan, over_row(sums), tgt_mass)
    sums, src_potential = call(
        last_column_sums_kernel,
        (f32(peers_row, column_tiles + 8, LANES), by_row),
        [VMEM] * 8,
        [wide, longer],
    )(plan, *over_col(sums, add_all), src_mass, src_lse, squares)
    tgt_potential, tgt_sum, src_sum = call(
        last_kernel, (by_column, f32(8, LANES), f32(8, LANES)), [VMEM] * 3, []
    )(over_row(sums), tgt_mass, tgt_lse)
    tgt_sum = add_all(over_col(tgt_sum, add_all))
    sources_all, targets_all = rows * peers_row, columns * peers_col
    mean_potentials = (src_sum / sources_all + tgt_sum / targets_all)[0, 0]
    return (src_potential.reshape(-1), tgt_potential.reshape(-1), mean_potentials)


def solution(mesh):
    finer = Mesh(mesh.devices.reshape(4, 4, 4, 2), ("row_0", "row_1", "col_0", "col_1"))
    placed = (P(ROW, None), P(COL_ROW, None), P(ROW), P(COL))
    return jax.shard_map(
        body, mesh=finer, in_specs=placed, out_specs=(P(ROW), P(COL), P()), check_vma=False
    )
```

```python
import functools
import itertools
import math

import jax
import jax.numpy as jnp
from jax import lax
from jax.experimental import pallas as pl
from jax.experimental.pallas import tpu as pltpu
from jax.sharding import Mesh
from jax.sharding import PartitionSpec as P

ROW = ("row_0", "row_1")
COL = ("col_0", "col_1")
COL_ROW = ("col_0", "col_1", "row_0", "row_1")

EPS = 0.1
WIDTH = 256
NATS = 2.0 / (WIDTH * EPS)
BITS = NATS * math.log2(math.e)
LOG2E = math.log2(math.e)
LN2 = math.log(2.0)
VMEM_LIMIT = 24 * 1024 * 1024
LANES = 128
STEP = 64
ROWS = 512
HUGE = 3.0e38

VMEM = pl.BlockSpec(memory_space=pltpu.VMEM)
SMEM = pl.BlockSpec(memory_space=pltpu.SMEM)


def call(kernel, outs, ins, scratch, aliases=None):
    return pl.pallas_call(
        kernel,
        out_shape=outs,
        in_specs=ins,
        out_specs=jax.tree.map(lambda _: VMEM, outs),
        scratch_shapes=scratch,
        input_output_aliases=aliases or {},
        compiler_params=pltpu.CompilerParams(vmem_limit_bytes=VMEM_LIMIT),
    )


def f32(*shape):
    return jax.ShapeDtypeStruct(shape, jnp.float32)


def spread(dense, wide_ref):
    for b in range(dense.shape[0]):
        square = jnp.broadcast_to(dense[b : b + 1, :], (LANES, LANES))
        wide_ref[b * LANES : (b + 1) * LANES, :] = square.T


def collapse(wide_ref):
    lines = [
        jnp.sum(wide_ref[b * LANES : (b + 1) * LANES, :].T, axis=0, keepdims=True)
        for b in range(wide_ref.shape[0] // LANES)
    ]
    return jnp.concatenate(lines, axis=0)


def collapse_top(wide_ref):
    lines = [
        wide_ref[b * LANES : (b + 1) * LANES, :].T[:1, :]
        for b in range(wide_ref.shape[0] // LANES)
    ]
    return jnp.concatenate(lines, axis=0)


def add_all(parts):
    total = parts[0]
    for part in parts[1:]:
        total = total + part
    return total


def lse_all(parts):
    top = parts[0]
    for part in parts[1:]:
        top = jnp.maximum(top, part)
    return top + jnp.log(add_all([jnp.exp(part - top) for part in parts]))


def copies(out_ref, value):
    for peer in range(out_ref.shape[0]):
        out_ref[peer] = value


def combined(parts_ref, combine):
    return combine([parts_ref[peer] for peer in range(parts_ref.shape[0])])


def values(refs):
    return [ref[...] for ref in refs]


def at_rows(r, step=STEP):
    return pl.ds(pl.multiple_of(r * step, step), step)


def lane_tile(t):
    return slice(t * LANES, (t + 1) * LANES)


def target_block(place, shift, inner):
    first_core = place[2] == 0
    shift_y = jnp.where(first_core, shift, inner)
    shift_x = jnp.where(first_core, inner, shift)
    return 4 * lax.rem(place[0] + 4 - shift_y, 4) + lax.rem(place[1] + 4 - shift_x, 4)


def chunk_biases(points, mass_ref, block):
    squares = points.astype(jnp.float32) ** 2
    squares = squares[:, :LANES] + squares[:, LANES:]
    found = []
    for side in range(2):
        square = squares[side * LANES : (side + 1) * LANES, :].T
        mass = mass_ref[pl.ds(2 * block + side, 1), :]
        found.append(mass * LOG2E - jnp.sum(square, axis=0, keepdims=True) * (0.5 * BITS))
    return found


def piece_product(x_ref, points_ref, r, m):
    return lax.dot_general(
        x_ref[r : r + ROWS, :],
        points_ref[m * 256 : (m + 1) * 256, :],
        (((1,), (1,)), ((), ())),
        preferred_element_type=jnp.float32,
    )


def piece_blocks(k, place, points_ref, mass_ref):
    blocks = [target_block(place, k, m) for m in range(4)]
    biases = [
        chunk_biases(points_ref[m * 256 : (m + 1) * 256, :], mass_ref, blocks[m]) for m in range(4)
    ]
    return blocks, biases


def first_terms_kernel(place, x_ref, points_ref, mass_ref, t_ref, top_ref, sum_ref, squares_ref):
    rows = x_ref.shape[0]
    squares = x_ref[...].astype(jnp.float32) ** 2
    sum_ref[...] = squares[:, :LANES] + squares[:, LANES:]
    squares_ref[...] = collapse(sum_ref)
    blocks, biases = piece_blocks(0, place, points_ref, mass_ref)
    for r in range(0, rows, ROWS):
        top = None
        for m in range(4):
            product = piece_product(x_ref, points_ref, r, m)
            for side in range(2):
                terms = product[:, lane_tile(side)] * BITS + biases[m][side]
                t_ref[2 * blocks[m] + side, r : r + ROWS, :] = terms
                top = terms if top is None else jnp.maximum(top, terms)
        top_ref[r : r + ROWS, :] = top

    def rows_step(r, unused):
        at = at_rows(r)
        top = jnp.max(top_ref[at, :], axis=1, keepdims=True)
        total = jnp.zeros((STEP, LANES), jnp.float32)
        for m in range(4):
            for side in range(2):
                total += jnp.exp2(t_ref[2 * blocks[m] + side, at, :] - top)
        top_ref[at, :] = jnp.broadcast_to(top, (STEP, LANES))
        sum_ref[at, :] = total
        return unused

    lax.fori_loop(0, rows // STEP, rows_step, 0)


def piece_steps(k, place, x_ref, points_ref, mass_ref, top_ref, old_sum_ref, t_ref, sum_ref):
    blocks, biases = piece_blocks(k, place, points_ref, mass_ref)
    for r in range(0, x_ref.shape[0], ROWS):
        top = top_ref[r : r + ROWS, :]
        total = old_sum_ref[r : r + ROWS, :]
        for m in range(4):
            product = piece_product(x_ref, points_ref, r, m)
            for side in range(2):
                terms = product[:, lane_tile(side)] * BITS + biases[m][side]
                t_ref[2 * blocks[m] + side, r : r + ROWS, :] = terms
                total += jnp.exp2(terms - top)
        sum_ref[r : r + ROWS, :] = total


def more_terms_kernel(k, place, x_ref, old_ref, old_sum_ref, top_ref, points_ref, mass_ref, *refs):
    t_ref, sum_ref = refs
    piece_steps(k, place, x_ref, points_ref, mass_ref, top_ref, old_sum_ref, t_ref, sum_ref)


def last_terms_kernel(k, place, x_ref, old_ref, old_sum_ref, old_top_ref, points_ref, mass_ref, *refs):
    t_ref, sum_ref, out_ref, top_ref = refs
    tiles, rows, _ = t_ref.shape
    piece_steps(k, place, x_ref, points_ref, mass_ref, old_top_ref, old_sum_ref, t_ref, sum_ref)
    total = collapse(sum_ref)
    out_ref[...] = collapse_top(old_top_ref) * LN2 + jnp.log(total)

    @pl.when(jnp.logical_not(jnp.max(total) < HUGE))
    def exact():
        def rows_step(r, unused):
            at = at_rows(r)
            top = jnp.full((STEP, LANES), -jnp.inf, jnp.float32)
            for t in range(tiles):
                top = jnp.maximum(top, t_ref[t, at, :])
            top = jnp.max(top, axis=1, keepdims=True)
            total = jnp.zeros((STEP, LANES), jnp.float32)
            for t in range(tiles):
                total += jnp.exp2(t_ref[t, at, :] - top)
            top_ref[at, :] = jnp.broadcast_to(top, (STEP, LANES))
            sum_ref[at, :] = total
            return unused

        lax.fori_loop(0, rows // STEP, rows_step, 0)
        out_ref[...] = collapse_top(top_ref) * LN2 + jnp.log(collapse(sum_ref))


def column_kernel(t_ref, *refs):
    parts, (mass_ref, out_ref, lse_ref, wide_ref, line_ref) = refs[:4], refs[4:]
    tiles, rows, _ = t_ref.shape
    lse = lse_all(values(parts))
    lse_ref[...] = lse
    spread((mass_ref[...] - lse) * LOG2E, wide_ref)
    per, step = 32, 128

    def group(value):
        return value.reshape(step // 8, 8, LANES)

    def sums(c, tops):
        wide = [jnp.broadcast_to(top, (step, LANES)) for top in tops]

        def sum_step(r, totals):
            at = at_rows(r, step)
            own = wide_ref[at, :]
            return tuple(
                total
                + jnp.sum(
                    group(jnp.exp2(t_ref[c + t, at, :] + own - wide[t])), axis=0
                )
                for t, total in enumerate(totals)
            )

        start = tuple(jnp.zeros((8, LANES), jnp.float32) for _ in range(per))
        totals = lax.fori_loop(0, rows // step, sum_step, start)
        for t in range(per):
            total = jnp.sum(totals[t], axis=0, keepdims=True)
            line_ref[c + t : c + t + 1, :] = tops[t] * LN2 + jnp.log(total)

    for c in range(0, tiles, per):
        tops = [
            jnp.max(t_ref[c + t, :step, :] + wide_ref[:step, :], axis=0, keepdims=True)
            for t in range(per)
        ]
        sums(c, tops)

    @pl.when(jnp.logical_not(jnp.max(line_ref[...]) < HUGE))
    def exact():
        for c in range(0, tiles, per):

            def top_step(r, tops):
                at = at_rows(r, step)
                return tuple(
                    jnp.maximum(top, jnp.max(group(t_ref[c + t, at, :] + wide_ref[at, :]), axis=0))
                    for t, top in enumerate(tops)
                )

            start = tuple(jnp.full((8, LANES), -jnp.inf, jnp.float32) for _ in range(per))
            tops = lax.fori_loop(0, rows // step, top_step, start)
            sums(c, [jnp.max(top, axis=0, keepdims=True) for top in tops])

    copies(out_ref, line_ref[...])


def plan_kernel(t_ref, parts_ref, tgt_mass_ref, src_lse_ref, src_mass_ref, *refs):
    plan_ref, out_ref, lse_ref, wide_ref, sum_ref, line_ref = refs
    tiles, rows, _ = t_ref.shape
    lse = combined(parts_ref, lse_all)
    lse_ref[...] = lse
    line_ref[...] = (tgt_mass_ref[...] - lse) * LOG2E
    spread((src_mass_ref[...] - src_lse_ref[...]) * LOG2E, wide_ref)
    per, step = 4, 128

    def rows_step(r, unused):
        at = at_rows(r, step)
        total = jnp.zeros((step, LANES), jnp.float32)
        own = wide_ref[at, :]
        for c in range(0, tiles, per):
            terms = [t_ref[c + t, at, :] for t in range(per)]
            values = [
                jnp.exp2(terms[t] + own + line_ref[c + t : c + t + 1, :]) for t in range(per)
            ]
            for t in range(per):
                plan_ref[c + t, at, :] = values[t]
                total += values[t]
        sum_ref[at, :] = total
        return unused

    lax.fori_loop(0, rows // step, rows_step, 0)
    out_ref[...] = collapse(sum_ref)


def row_sums_kernel(plan_ref, parts_ref, mass_ref, out_ref, sum_ref, line_ref):
    tiles, rows, _ = plan_ref.shape
    step = 512
    line_ref[...] = jnp.exp(mass_ref[...]) / combined(parts_ref, add_all)

    def rows_step(r, unused):
        at = at_rows(r, step)
        total = jnp.zeros((step, LANES), jnp.float32)
        for t in range(tiles):
            total += plan_ref[t, at, :] * line_ref[t : t + 1, :]
        sum_ref[at, :] = total
        return unused

    lax.fori_loop(0, rows // step, rows_step, 0)
    out_ref[...] = collapse(sum_ref)


def column_sums(plan_ref, scale, line_ref, wide_ref):
    tiles, rows, _ = plan_ref.shape
    spread(scale, wide_ref)
    per = tiles
    for c in range(0, tiles, per):

        def rows_step(r, totals):
            at = at_rows(r)
            own = wide_ref[at, :]
            return tuple(
                total
                + jnp.sum(
                    (plan_ref[c + t, at, :] * own).reshape(STEP // 8, 8, LANES), axis=0
                )
                for t, total in enumerate(totals)
            )

        start = tuple(jnp.zeros((8, LANES), jnp.float32) for _ in range(per))
        totals = lax.fori_loop(0, rows // STEP, rows_step, start)
        for t in range(per):
            line_ref[c + t : c + t + 1, :] = jnp.sum(totals[t], axis=0, keepdims=True)


def column_sums_kernel(plan_ref, *refs):
    parts, (mass_ref, out_ref, wide_ref, line_ref) = refs[:4], refs[4:]
    scale = jnp.exp(mass_ref[...]) / add_all(values(parts))
    column_sums(plan_ref, scale, line_ref, wide_ref)
    copies(out_ref, line_ref[...])


def last_column_sums_kernel(plan_ref, *refs):
    parts, (mass_ref, lse_ref, squares_ref) = refs[:4], refs[4:7]
    out_ref, potential_ref, wide_ref, line_ref = refs[7:]
    sums = add_all(values(parts))
    mass = mass_ref[...]
    column_sums(plan_ref, jnp.exp(mass) / sums, line_ref, wide_ref)
    squares = squares_ref[...] / (WIDTH * EPS)
    potential = -EPS * (lse_ref[...] + jnp.log(sums) - mass - squares)
    potential_ref[...] = potential
    tiles = plan_ref.shape[0]
    line_ref[tiles:, :] = jnp.broadcast_to(jnp.sum(potential), (8, LANES))
    copies(out_ref, line_ref[...])


def last_kernel(parts_ref, mass_ref, lse_ref, potential_ref, own_ref, other_ref):
    tiles = mass_ref.shape[0]
    sums = combined(parts_ref, add_all)
    potential = -EPS * (lse_ref[...] + jnp.log(sums[:tiles]) - 2.0 * mass_ref[...])
    potential_ref[...] = potential
    own_ref[...] = jnp.broadcast_to(jnp.sum(potential), (8, LANES))
    other_ref[...] = sums[tiles:]


ALL = ("row_0", "row_1", "col_0", "col_1")
SIZES = (4, 4, 4, 2)


def number(y, x, z, core):
    return ((y % 4 * 4 + x % 4) * 4 + z) * 2 + core


def turned(value, stage):
    found = {0: value}
    for k in (2, 1, 3):
        pairs = []
        for y, x, z, core in itertools.product(*map(range, SIZES)):
            along_y = (core + stage) % 2
            to = number(y + k * along_y, x + k * (1 - along_y), z, core)
            pairs.append((number(y, x, z, core), to))
        found[k] = lax.ppermute(value, ALL, pairs)
    return [found[k] for k in range(4)]


def crossed(value, k):
    pairs = []
    for y, x, z, core in itertools.product(*map(range, SIZES)):
        pairs.append((number(y, x, z, core), number(y, x, (z + k) % 4, 1 - core)))
    return lax.ppermute(value, ALL, pairs)


def body(src_points, tgt_points, log_src_mass, log_tgt_mass):
    rows, columns = src_points.shape[0], log_tgt_mass.shape[0]
    row_tiles, column_tiles = rows // LANES, columns // LANES
    src_mass = log_src_mass.reshape(row_tiles, LANES)
    tgt_mass = log_tgt_mass.reshape(column_tiles, LANES)
    place = jnp.stack([lax.axis_index(name) for name in ("row_0", "row_1", "col_1")])
    place = place.astype(jnp.int32)
    wide = pltpu.VMEM((rows, LANES), jnp.float32)
    big = pltpu.VMEM((column_tiles, rows, LANES), jnp.float32)
    line = pltpu.VMEM((column_tiles, LANES), jnp.float32)
    longer = pltpu.VMEM((column_tiles + 8, LANES), jnp.float32)
    by_row, by_column = f32(row_tiles, LANES), f32(column_tiles, LANES)
    peers_row, peers_col = lax.axis_size(ROW), lax.axis_size(COL)
    columns_out = f32(peers_row, column_tiles, LANES)

    def resident(value):
        return pltpu.with_memory_space_constraint(value, pltpu.VMEM)

    def over_col(value, combine):
        both = combine([value, lax.ppermute(value, "col_1", [(0, 1), (1, 0)])])
        return [both] + [crossed(both, k) for k in (2, 1, 3)]

    def over_row(value):
        return lax.all_to_all(value, ROW, 0, 0, tiled=True)

    first = jnp.concatenate(turned(tgt_points, 0))
    pieces = turned(first, 1)
    terms, top, sums, squares = call(
        first_terms_kernel, (big, wide, wide, by_row), [SMEM] + [VMEM] * 3, []
    )(place, src_points, first, tgt_mass)
    for k in (1, 3):
        terms, sums = call(
            functools.partial(more_terms_kernel, k), (big, wide), [SMEM] + [VMEM] * 6, [], {2: 0, 3: 1}
        )(place, src_points, resident(terms), resident(sums), resident(top), pieces[k], tgt_mass)
    terms, sums, lse = call(
        functools.partial(last_terms_kernel, 2),
        (big, wide, by_row),
        [SMEM] + [VMEM] * 6,
        [wide],
        {2: 0, 3: 1},
    )(place, src_points, resident(terms), resident(sums), resident(top), pieces[2], tgt_mass)
    lse, src_lse = call(column_kernel, (columns_out, by_row), [VMEM] * 6, [wide, line])(
        resident(terms), *over_col(lse, lse_all), src_mass
    )
    plan, sums, tgt_lse = call(
        plan_kernel, (big, by_row, by_column), [VMEM] * 5, [wide, wide, line], {0: 0}
    )(resident(terms), over_row(lse), tgt_mass, src_lse, src_mass)
    plan = resident(plan)
    sums = call(column_sums_kernel, columns_out, [VMEM] * 6, [wide, line])(
        plan, *over_col(sums, add_all), src_mass
    )
    sums = call(row_sums_kernel, by_row, [VMEM] * 3, [wide, line])(plan, over_row(sums), tgt_mass)
    sums, src_potential = call(
        last_column_sums_kernel,
        (f32(peers_row, column_tiles + 8, LANES), by_row),
        [VMEM] * 8,
        [wide, longer],
    )(plan, *over_col(sums, add_all), src_mass, src_lse, squares)
    tgt_potential, tgt_sum, src_sum = call(
        last_kernel, (by_column, f32(8, LANES), f32(8, LANES)), [VMEM] * 3, []
    )(over_row(sums), tgt_mass, tgt_lse)
    tgt_sum = add_all(over_col(tgt_sum, add_all))
    sources_all, targets_all = rows * peers_row, columns * peers_col
    mean_potentials = (src_sum / sources_all + tgt_sum / targets_all)[0, 0]
    return (src_potential.reshape(-1), tgt_potential.reshape(-1), mean_potentials)


def solution(mesh):
    finer = Mesh(mesh.devices.reshape(4, 4, 4, 2), ("row_0", "row_1", "col_0", "col_1"))
    placed = (P(ROW, None), P(COL_ROW, None), P(ROW), P(COL))
    return jax.shard_map(
        body, mesh=finer, in_specs=placed, out_specs=(P(ROW), P(COL), P()), check_vma=False
    )
```

```python
import functools
import itertools
import math

import jax
import jax.numpy as jnp
from jax import lax
from jax.experimental import pallas as pl
from jax.experimental.pallas import tpu as pltpu
from jax.sharding import Mesh
from jax.sharding import PartitionSpec as P

ROW = ("y_high", "y_low", "x_high", "x_low")
COL = ("col_0", "col_1")
ROW_PEERS = ("x_low", "x_high", "y_high", "y_low")

EPS = 0.1
WIDTH = 256
NATS = 2.0 / (WIDTH * EPS)
BITS = NATS * math.log2(math.e)
LOG2E = math.log2(math.e)
LN2 = math.log(2.0)
VMEM_LIMIT = 24 * 1024 * 1024
LANES = 128
STEP = 64
ROWS = 512
HUGE = 3.0e38

VMEM = pl.BlockSpec(memory_space=pltpu.VMEM)
SMEM = pl.BlockSpec(memory_space=pltpu.SMEM)


def call(kernel, outs, ins, scratch, aliases=None):
    return pl.pallas_call(
        kernel,
        out_shape=outs,
        in_specs=ins,
        out_specs=jax.tree.map(lambda _: VMEM, outs),
        scratch_shapes=scratch,
        input_output_aliases=aliases or {},
        compiler_params=pltpu.CompilerParams(vmem_limit_bytes=VMEM_LIMIT),
    )


def f32(*shape):
    return jax.ShapeDtypeStruct(shape, jnp.float32)


def spread(dense, wide_ref):
    for b in range(dense.shape[0]):
        square = jnp.broadcast_to(dense[b : b + 1, :], (LANES, LANES))
        wide_ref[b * LANES : (b + 1) * LANES, :] = square.T


def collapse(wide_ref):
    lines = [
        jnp.sum(wide_ref[b * LANES : (b + 1) * LANES, :].T, axis=0, keepdims=True)
        for b in range(wide_ref.shape[0] // LANES)
    ]
    return jnp.concatenate(lines, axis=0)


def collapse_top(wide_ref):
    lines = [
        wide_ref[b * LANES : (b + 1) * LANES, :].T[:1, :]
        for b in range(wide_ref.shape[0] // LANES)
    ]
    return jnp.concatenate(lines, axis=0)


def add_all(parts):
    total = parts[0]
    for part in parts[1:]:
        total = total + part
    return total


def lse_all(parts):
    top = parts[0]
    for part in parts[1:]:
        top = jnp.maximum(top, part)
    return top + jnp.log(add_all([jnp.exp(part - top) for part in parts]))


def copies(out_ref, value):
    for peer in range(out_ref.shape[0]):
        out_ref[peer] = value


def combined(parts_ref, combine):
    return combine([parts_ref[peer] for peer in range(parts_ref.shape[0])])


def values(refs):
    return [ref[...] for ref in refs]


def at_rows(r, step=STEP):
    return pl.ds(pl.multiple_of(r * step, step), step)


def lane_tile(t):
    return slice(t * LANES, (t + 1) * LANES)


def target_block(place, shift, inner):
    first_core = place[2] == 0
    shift_y = jnp.where(first_core, shift, inner)
    shift_x = jnp.where(first_core, inner, shift)
    return 4 * lax.rem(place[0] + 4 - shift_y, 4) + lax.rem(place[1] + 4 - shift_x, 4)


def chunk_biases(points, mass_ref, block):
    squares = points.astype(jnp.float32) ** 2
    squares = squares[:, :LANES] + squares[:, LANES:]
    found = []
    for side in range(2):
        square = squares[side * LANES : (side + 1) * LANES, :].T
        mass = mass_ref[pl.ds(2 * block + side, 1), :]
        found.append(mass * LOG2E - jnp.sum(square, axis=0, keepdims=True) * (0.5 * BITS))
    return found


def piece_product(x_ref, points_ref, r, m):
    return lax.dot_general(
        x_ref[r : r + ROWS, :],
        points_ref[m * 256 : (m + 1) * 256, :],
        (((1,), (1,)), ((), ())),
        preferred_element_type=jnp.float32,
    )


def piece_blocks(k, place, points_ref, mass_ref):
    blocks = [target_block(place, k, m) for m in range(4)]
    biases = [
        chunk_biases(points_ref[m * 256 : (m + 1) * 256, :], mass_ref, blocks[m]) for m in range(4)
    ]
    return blocks, biases


def first_terms_kernel(place, x_ref, points_ref, mass_ref, t_ref, top_ref, sum_ref, squares_ref):
    rows = x_ref.shape[0]
    squares = x_ref[...].astype(jnp.float32) ** 2
    sum_ref[...] = squares[:, :LANES] + squares[:, LANES:]
    squares_ref[...] = collapse(sum_ref)
    blocks, biases = piece_blocks(0, place, points_ref, mass_ref)
    for r in range(0, rows, ROWS):
        top = None
        for m in range(4):
            product = piece_product(x_ref, points_ref, r, m)
            for side in range(2):
                terms = product[:, lane_tile(side)] * BITS + biases[m][side]
                t_ref[2 * blocks[m] + side, r : r + ROWS, :] = terms
                top = terms if top is None else jnp.maximum(top, terms)
        top_ref[r : r + ROWS, :] = top

    def rows_step(r, unused):
        at = at_rows(r)
        top = jnp.max(top_ref[at, :], axis=1, keepdims=True)
        total = jnp.zeros((STEP, LANES), jnp.float32)
        for m in range(4):
            for side in range(2):
                total += jnp.exp2(t_ref[2 * blocks[m] + side, at, :] - top)
        top_ref[at, :] = jnp.broadcast_to(top, (STEP, LANES))
        sum_ref[at, :] = total
        return unused

    lax.fori_loop(0, rows // STEP, rows_step, 0)


def piece_steps(k, place, x_ref, points_ref, mass_ref, top_ref, old_sum_ref, t_ref, sum_ref):
    blocks, biases = piece_blocks(k, place, points_ref, mass_ref)
    for r in range(0, x_ref.shape[0], ROWS):
        top = top_ref[r : r + ROWS, :]
        total = old_sum_ref[r : r + ROWS, :]
        for m in range(4):
            product = piece_product(x_ref, points_ref, r, m)
            for side in range(2):
                terms = product[:, lane_tile(side)] * BITS + biases[m][side]
                t_ref[2 * blocks[m] + side, r : r + ROWS, :] = terms
                total += jnp.exp2(terms - top)
        sum_ref[r : r + ROWS, :] = total


def more_terms_kernel(k, place, x_ref, old_ref, old_sum_ref, top_ref, points_ref, mass_ref, *refs):
    t_ref, sum_ref = refs
    piece_steps(k, place, x_ref, points_ref, mass_ref, top_ref, old_sum_ref, t_ref, sum_ref)


def last_terms_kernel(k, place, x_ref, old_ref, old_sum_ref, old_top_ref, points_ref, mass_ref, *refs):
    t_ref, sum_ref, out_ref, top_ref = refs
    tiles, rows, _ = t_ref.shape
    piece_steps(k, place, x_ref, points_ref, mass_ref, old_top_ref, old_sum_ref, t_ref, sum_ref)
    total = collapse(sum_ref)
    out_ref[...] = collapse_top(old_top_ref) * LN2 + jnp.log(total)

    @pl.when(jnp.logical_not(jnp.max(total) < HUGE))
    def exact():
        def rows_step(r, unused):
            at = at_rows(r)
            top = jnp.full((STEP, LANES), -jnp.inf, jnp.float32)
            for t in range(tiles):
                top = jnp.maximum(top, t_ref[t, at, :])
            top = jnp.max(top, axis=1, keepdims=True)
            total = jnp.zeros((STEP, LANES), jnp.float32)
            for t in range(tiles):
                total += jnp.exp2(t_ref[t, at, :] - top)
            top_ref[at, :] = jnp.broadcast_to(top, (STEP, LANES))
            sum_ref[at, :] = total
            return unused

        lax.fori_loop(0, rows // STEP, rows_step, 0)
        out_ref[...] = collapse_top(top_ref) * LN2 + jnp.log(collapse(sum_ref))


def column_kernel(t_ref, *refs):
    parts, (mass_ref, out_ref, lse_ref, wide_ref, line_ref) = refs[:4], refs[4:]
    tiles, rows, _ = t_ref.shape
    lse = lse_all(values(parts))
    lse_ref[...] = lse
    spread((mass_ref[...] - lse) * LOG2E, wide_ref)
    per, step = 32, 128

    def group(value):
        return value.reshape(step // 8, 8, LANES)

    def sums(c, tops):
        wide = [jnp.broadcast_to(top, (step, LANES)) for top in tops]

        def sum_step(r, totals):
            at = at_rows(r, step)
            own = wide_ref[at, :]
            return tuple(
                total
                + jnp.sum(
                    group(jnp.exp2(t_ref[c + t, at, :] + own - wide[t])), axis=0
                )
                for t, total in enumerate(totals)
            )

        start = tuple(jnp.zeros((8, LANES), jnp.float32) for _ in range(per))
        totals = lax.fori_loop(0, rows // step, sum_step, start)
        for t in range(per):
            total = jnp.sum(totals[t], axis=0, keepdims=True)
            line_ref[c + t : c + t + 1, :] = tops[t] * LN2 + jnp.log(total)

    for c in range(0, tiles, per):
        tops = [
            jnp.max(t_ref[c + t, :step, :] + wide_ref[:step, :], axis=0, keepdims=True)
            for t in range(per)
        ]
        sums(c, tops)

    @pl.when(jnp.logical_not(jnp.max(line_ref[...]) < HUGE))
    def exact():
        for c in range(0, tiles, per):

            def top_step(r, tops):
                at = at_rows(r, step)
                return tuple(
                    jnp.maximum(top, jnp.max(group(t_ref[c + t, at, :] + wide_ref[at, :]), axis=0))
                    for t, top in enumerate(tops)
                )

            start = tuple(jnp.full((8, LANES), -jnp.inf, jnp.float32) for _ in range(per))
            tops = lax.fori_loop(0, rows // step, top_step, start)
            sums(c, [jnp.max(top, axis=0, keepdims=True) for top in tops])

    copies(out_ref, line_ref[...])


def plan_kernel(t_ref, parts_ref, tgt_mass_ref, src_lse_ref, src_mass_ref, *refs):
    plan_ref, out_ref, lse_ref, wide_ref, sum_ref, line_ref = refs
    tiles, rows, _ = t_ref.shape
    lse = combined(parts_ref, lse_all)
    lse_ref[...] = lse
    line_ref[...] = (tgt_mass_ref[...] - lse) * LOG2E
    spread((src_mass_ref[...] - src_lse_ref[...]) * LOG2E, wide_ref)
    per, step = 4, 128

    def rows_step(r, unused):
        at = at_rows(r, step)
        total = jnp.zeros((step, LANES), jnp.float32)
        own = wide_ref[at, :]
        for c in range(0, tiles, per):
            terms = [t_ref[c + t, at, :] for t in range(per)]
            values = [
                jnp.exp2(terms[t] + own + line_ref[c + t : c + t + 1, :]) for t in range(per)
            ]
            for t in range(per):
                plan_ref[c + t, at, :] = values[t]
                total += values[t]
        sum_ref[at, :] = total
        return unused

    lax.fori_loop(0, rows // step, rows_step, 0)
    out_ref[...] = collapse(sum_ref)


def row_sums_kernel(plan_ref, parts_ref, mass_ref, out_ref, sum_ref, line_ref):
    tiles, rows, _ = plan_ref.shape
    step = 512
    line_ref[...] = jnp.exp(mass_ref[...]) / combined(parts_ref, add_all)

    def rows_step(r, unused):
        at = at_rows(r, step)
        total = jnp.zeros((step, LANES), jnp.float32)
        for t in range(tiles):
            total += plan_ref[t, at, :] * line_ref[t : t + 1, :]
        sum_ref[at, :] = total
        return unused

    lax.fori_loop(0, rows // step, rows_step, 0)
    out_ref[...] = collapse(sum_ref)


def column_sums(plan_ref, scale, line_ref, wide_ref):
    tiles, rows, _ = plan_ref.shape
    spread(scale, wide_ref)
    per = tiles
    for c in range(0, tiles, per):

        def rows_step(r, totals):
            at = at_rows(r)
            own = wide_ref[at, :]
            return tuple(
                total
                + jnp.sum(
                    (plan_ref[c + t, at, :] * own).reshape(STEP // 8, 8, LANES), axis=0
                )
                for t, total in enumerate(totals)
            )

        start = tuple(jnp.zeros((8, LANES), jnp.float32) for _ in range(per))
        totals = lax.fori_loop(0, rows // STEP, rows_step, start)
        for t in range(per):
            line_ref[c + t : c + t + 1, :] = jnp.sum(totals[t], axis=0, keepdims=True)


def column_sums_kernel(plan_ref, *refs):
    parts, (mass_ref, out_ref, wide_ref, line_ref) = refs[:4], refs[4:]
    scale = jnp.exp(mass_ref[...]) / add_all(values(parts))
    column_sums(plan_ref, scale, line_ref, wide_ref)
    copies(out_ref, line_ref[...])


def last_column_sums_kernel(plan_ref, *refs):
    parts, (mass_ref, lse_ref, squares_ref) = refs[:4], refs[4:7]
    out_ref, potential_ref, wide_ref, line_ref = refs[7:]
    sums = add_all(values(parts))
    mass = mass_ref[...]
    column_sums(plan_ref, jnp.exp(mass) / sums, line_ref, wide_ref)
    squares = squares_ref[...] / (WIDTH * EPS)
    potential = -EPS * (lse_ref[...] + jnp.log(sums) - mass - squares)
    potential_ref[...] = potential
    tiles = plan_ref.shape[0]
    line_ref[tiles:, :] = jnp.broadcast_to(jnp.sum(potential), (8, LANES))
    copies(out_ref, line_ref[...])


def last_kernel(parts_ref, mass_ref, lse_ref, potential_ref, own_ref, other_ref):
    tiles = mass_ref.shape[0]
    sums = combined(parts_ref, add_all)
    potential = -EPS * (lse_ref[...] + jnp.log(sums[:tiles]) - 2.0 * mass_ref[...])
    potential_ref[...] = potential
    own_ref[...] = jnp.broadcast_to(jnp.sum(potential), (8, LANES))
    other_ref[...] = sums[tiles:]


ALL = (*ROW, *COL)
SIZES = (4, 4, 4, 2)


def number(y, x, z, core):
    return ((y % 4 * 4 + x % 4) * 4 + z) * 2 + core


def turned(value, stage):
    found = {0: value}
    for k in (2, 1, 3):
        pairs = []
        for y, x, z, core in itertools.product(*map(range, SIZES)):
            along_y = (core + stage) % 2
            to = number(y + k * along_y, x + k * (1 - along_y), z, core)
            pairs.append((number(y, x, z, core), to))
        found[k] = lax.ppermute(value, ALL, pairs)
    return [found[k] for k in range(4)]


def crossed(value, k):
    pairs = []
    for y, x, z, core in itertools.product(*map(range, SIZES)):
        pairs.append((number(y, x, z, core), number(y, x, (z + k) % 4, 1 - core)))
    return lax.ppermute(value, ALL, pairs)


def body(src_points, tgt_points, log_src_mass, log_tgt_mass):
    rows, columns = src_points.shape[0], log_tgt_mass.shape[0]
    row_tiles, column_tiles = rows // LANES, columns // LANES
    src_mass = log_src_mass.reshape(row_tiles, LANES)
    tgt_mass = log_tgt_mass.reshape(column_tiles, LANES)
    place = jnp.stack([lax.axis_index(name) for name in (ROW[:2], ROW[2:], "col_1")])
    place = place.astype(jnp.int32)
    wide = pltpu.VMEM((rows, LANES), jnp.float32)
    big = pltpu.VMEM((column_tiles, rows, LANES), jnp.float32)
    line = pltpu.VMEM((column_tiles, LANES), jnp.float32)
    longer = pltpu.VMEM((column_tiles + 8, LANES), jnp.float32)
    by_row, by_column = f32(row_tiles, LANES), f32(column_tiles, LANES)
    peers_row, peers_col = lax.axis_size(ROW), lax.axis_size(COL)
    columns_out = f32(peers_row, column_tiles, LANES)

    def resident(value):
        return pltpu.with_memory_space_constraint(value, pltpu.VMEM)

    def over_col(value, combine):
        both = combine([value, lax.ppermute(value, "col_1", [(0, 1), (1, 0)])])
        return [both] + [crossed(both, k) for k in (2, 1, 3)]

    def over_row(value):
        return lax.all_to_all(value, ROW_PEERS, 0, 0, tiled=True)

    first = jnp.concatenate(turned(tgt_points, 0))
    pieces = turned(first, 1)
    terms, top, sums, squares = call(
        first_terms_kernel, (big, wide, wide, by_row), [SMEM] + [VMEM] * 3, []
    )(place, src_points, first, tgt_mass)
    for k in (1, 3):
        terms, sums = call(
            functools.partial(more_terms_kernel, k), (big, wide), [SMEM] + [VMEM] * 6, [], {2: 0, 3: 1}
        )(place, src_points, resident(terms), resident(sums), resident(top), pieces[k], tgt_mass)
    terms, sums, lse = call(
        functools.partial(last_terms_kernel, 2),
        (big, wide, by_row),
        [SMEM] + [VMEM] * 6,
        [wide],
        {2: 0, 3: 1},
    )(place, src_points, resident(terms), resident(sums), resident(top), pieces[2], tgt_mass)
    lse, src_lse = call(column_kernel, (columns_out, by_row), [VMEM] * 6, [wide, line])(
        resident(terms), *over_col(lse, lse_all), src_mass
    )
    plan, sums, tgt_lse = call(
        plan_kernel, (big, by_row, by_column), [VMEM] * 5, [wide, wide, line], {0: 0}
    )(resident(terms), over_row(lse), tgt_mass, src_lse, src_mass)
    plan = resident(plan)
    sums = call(column_sums_kernel, columns_out, [VMEM] * 6, [wide, line])(
        plan, *over_col(sums, add_all), src_mass
    )
    sums = call(row_sums_kernel, by_row, [VMEM] * 3, [wide, line])(plan, over_row(sums), tgt_mass)
    sums, src_potential = call(
        last_column_sums_kernel,
        (f32(peers_row, column_tiles + 8, LANES), by_row),
        [VMEM] * 8,
        [wide, longer],
    )(plan, *over_col(sums, add_all), src_mass, src_lse, squares)
    tgt_potential, tgt_sum, src_sum = call(
        last_kernel, (by_column, f32(8, LANES), f32(8, LANES)), [VMEM] * 3, []
    )(over_row(sums), tgt_mass, tgt_lse)
    tgt_sum = add_all(over_col(tgt_sum, add_all))
    sources_all, targets_all = rows * peers_row, columns * peers_col
    mean_potentials = (src_sum / sources_all + tgt_sum / targets_all)[0, 0]
    return (src_potential.reshape(-1), tgt_potential.reshape(-1), mean_potentials)


def solution(mesh):
    finer = Mesh(mesh.devices.reshape(2, 2, 2, 2, 4, 2), ALL)
    placed = (P(ROW, None), P((*COL, *ROW), None), P(ROW), P(COL))
    return jax.shard_map(
        body, mesh=finer, in_specs=placed, out_specs=(P(ROW), P(COL), P()), check_vma=False
    )
```

```python
import functools
import itertools
import math

import jax
import jax.numpy as jnp
from jax import lax
from jax.experimental import pallas as pl
from jax.experimental.pallas import tpu as pltpu
from jax.sharding import Mesh
from jax.sharding import PartitionSpec as P

ROW = ("row_0", "row_1")
COL = ("col_0", "col_1")
COL_ROW = ("col_0", "col_1", "row_0", "row_1")

EPS = 0.1
WIDTH = 256
NATS = 2.0 / (WIDTH * EPS)
BITS = NATS * math.log2(math.e)
LOG2E = math.log2(math.e)
LN2 = math.log(2.0)
VMEM_LIMIT = 24 * 1024 * 1024
LANES = 128
STEP = 64
ROWS = 512
HUGE = 3.0e38

VMEM = pl.BlockSpec(memory_space=pltpu.VMEM)
SMEM = pl.BlockSpec(memory_space=pltpu.SMEM)


def call(kernel, outs, ins, scratch, aliases=None):
    return pl.pallas_call(
        kernel,
        out_shape=outs,
        in_specs=ins,
        out_specs=jax.tree.map(lambda _: VMEM, outs),
        scratch_shapes=scratch,
        input_output_aliases=aliases or {},
        compiler_params=pltpu.CompilerParams(vmem_limit_bytes=VMEM_LIMIT),
    )


def f32(*shape):
    return jax.ShapeDtypeStruct(shape, jnp.float32)


def spread(dense, wide_ref):
    for b in range(dense.shape[0]):
        square = jnp.broadcast_to(dense[b : b + 1, :], (LANES, LANES))
        wide_ref[b * LANES : (b + 1) * LANES, :] = square.T


def collapse(wide_ref):
    lines = [
        jnp.sum(wide_ref[b * LANES : (b + 1) * LANES, :].T, axis=0, keepdims=True)
        for b in range(wide_ref.shape[0] // LANES)
    ]
    return jnp.concatenate(lines, axis=0)


def collapse_top(wide_ref):
    lines = [
        wide_ref[b * LANES : (b + 1) * LANES, :].T[:1, :]
        for b in range(wide_ref.shape[0] // LANES)
    ]
    return jnp.concatenate(lines, axis=0)


def add_all(parts):
    total = parts[0]
    for part in parts[1:]:
        total = total + part
    return total


def lse_all(parts):
    top = parts[0]
    for part in parts[1:]:
        top = jnp.maximum(top, part)
    return top + jnp.log(add_all([jnp.exp(part - top) for part in parts]))


def copies(out_ref, value):
    for peer in range(out_ref.shape[0]):
        out_ref[peer] = value


def combined(parts_ref, combine):
    return combine([parts_ref[peer] for peer in range(parts_ref.shape[0])])


def values(refs):
    return [ref[...] for ref in refs]


def at_rows(r, step=STEP):
    return pl.ds(pl.multiple_of(r * step, step), step)


def lane_tile(t):
    return slice(t * LANES, (t + 1) * LANES)


def target_block(place, shift, inner):
    first_core = place[2] == 0
    shift_y = jnp.where(first_core, shift, inner)
    shift_x = jnp.where(first_core, inner, shift)
    return 4 * lax.rem(place[0] + 4 - shift_y, 4) + lax.rem(place[1] + 4 - shift_x, 4)


def chunk_biases(points, mass_ref, block):
    squares = points.astype(jnp.float32) ** 2
    squares = squares[:, :LANES] + squares[:, LANES:]
    found = []
    for side in range(2):
        square = squares[side * LANES : (side + 1) * LANES, :].T
        mass = mass_ref[pl.ds(2 * block + side, 1), :]
        found.append(mass * LOG2E - jnp.sum(square, axis=0, keepdims=True) * (0.5 * BITS))
    return found


def piece_product(x_ref, points_ref, r, m):
    return lax.dot_general(
        x_ref[r : r + ROWS, :],
        points_ref[m * 256 : (m + 1) * 256, :],
        (((1,), (1,)), ((), ())),
        preferred_element_type=jnp.float32,
    )


def piece_blocks(k, place, points_ref, mass_ref):
    blocks = [target_block(place, k, m) for m in range(4)]
    biases = [
        chunk_biases(points_ref[m * 256 : (m + 1) * 256, :], mass_ref, blocks[m]) for m in range(4)
    ]
    return blocks, biases


def first_terms_kernel(place, x_ref, points_ref, mass_ref, t_ref, top_ref, sum_ref, squares_ref):
    rows = x_ref.shape[0]
    squares = x_ref[...].astype(jnp.float32) ** 2
    sum_ref[...] = squares[:, :LANES] + squares[:, LANES:]
    squares_ref[...] = collapse(sum_ref)
    blocks, biases = piece_blocks(0, place, points_ref, mass_ref)
    for r in range(0, rows, ROWS):
        top = None
        for m in range(4):
            product = piece_product(x_ref, points_ref, r, m)
            for side in range(2):
                terms = product[:, lane_tile(side)] * BITS + biases[m][side]
                t_ref[2 * blocks[m] + side, r : r + ROWS, :] = terms
                top = terms if top is None else jnp.maximum(top, terms)
        top_ref[r : r + ROWS, :] = top

    def rows_step(r, unused):
        at = at_rows(r)
        top = jnp.max(top_ref[at, :], axis=1, keepdims=True)
        total = jnp.zeros((STEP, LANES), jnp.float32)
        for m in range(4):
            for side in range(2):
                total += jnp.exp2(t_ref[2 * blocks[m] + side, at, :] - top)
        top_ref[at, :] = jnp.broadcast_to(top, (STEP, LANES))
        sum_ref[at, :] = total
        return unused

    lax.fori_loop(0, rows // STEP, rows_step, 0)


def piece_steps(k, place, x_ref, points_ref, mass_ref, top_ref, old_sum_ref, t_ref, sum_ref):
    blocks, biases = piece_blocks(k, place, points_ref, mass_ref)
    for r in range(0, x_ref.shape[0], ROWS):
        top = top_ref[r : r + ROWS, :]
        total = old_sum_ref[r : r + ROWS, :]
        for m in range(4):
            product = piece_product(x_ref, points_ref, r, m)
            for side in range(2):
                terms = product[:, lane_tile(side)] * BITS + biases[m][side]
                t_ref[2 * blocks[m] + side, r : r + ROWS, :] = terms
                total += jnp.exp2(terms - top)
        sum_ref[r : r + ROWS, :] = total


def more_terms_kernel(k, place, x_ref, old_ref, old_sum_ref, top_ref, points_ref, mass_ref, *refs):
    t_ref, sum_ref = refs
    piece_steps(k, place, x_ref, points_ref, mass_ref, top_ref, old_sum_ref, t_ref, sum_ref)


def last_terms_kernel(k, place, x_ref, old_ref, old_sum_ref, old_top_ref, points_ref, mass_ref, *refs):
    t_ref, sum_ref, out_ref, top_ref = refs
    tiles, rows, _ = t_ref.shape
    piece_steps(k, place, x_ref, points_ref, mass_ref, old_top_ref, old_sum_ref, t_ref, sum_ref)
    total = collapse(sum_ref)
    out_ref[...] = collapse_top(old_top_ref) * LN2 + jnp.log(total)

    @pl.when(jnp.logical_not(jnp.max(total) < HUGE))
    def exact():
        def rows_step(r, unused):
            at = at_rows(r)
            top = jnp.full((STEP, LANES), -jnp.inf, jnp.float32)
            for t in range(tiles):
                top = jnp.maximum(top, t_ref[t, at, :])
            top = jnp.max(top, axis=1, keepdims=True)
            total = jnp.zeros((STEP, LANES), jnp.float32)
            for t in range(tiles):
                total += jnp.exp2(t_ref[t, at, :] - top)
            top_ref[at, :] = jnp.broadcast_to(top, (STEP, LANES))
            sum_ref[at, :] = total
            return unused

        lax.fori_loop(0, rows // STEP, rows_step, 0)
        out_ref[...] = collapse_top(top_ref) * LN2 + jnp.log(collapse(sum_ref))


def column_kernel(t_ref, *refs):
    parts, (mass_ref, out_ref, lse_ref, wide_ref, line_ref) = refs[:4], refs[4:]
    tiles, rows, _ = t_ref.shape
    lse = lse_all(values(parts))
    lse_ref[...] = lse
    spread((mass_ref[...] - lse) * LOG2E, wide_ref)
    per, step = 32, 128

    def group(value):
        return value.reshape(step // 8, 8, LANES)

    def sums(c, tops):
        wide = [jnp.broadcast_to(top, (step, LANES)) for top in tops]

        def sum_step(r, totals):
            at = at_rows(r, step)
            own = wide_ref[at, :]
            return tuple(
                total
                + jnp.sum(
                    group(jnp.exp2(t_ref[c + t, at, :] + own - wide[t])), axis=0
                )
                for t, total in enumerate(totals)
            )

        start = tuple(jnp.zeros((8, LANES), jnp.float32) for _ in range(per))
        totals = lax.fori_loop(0, rows // step, sum_step, start)
        for t in range(per):
            total = jnp.sum(totals[t], axis=0, keepdims=True)
            line_ref[c + t : c + t + 1, :] = tops[t] * LN2 + jnp.log(total)

    for c in range(0, tiles, per):
        tops = [
            jnp.max(t_ref[c + t, :step, :] + wide_ref[:step, :], axis=0, keepdims=True)
            for t in range(per)
        ]
        sums(c, tops)

    @pl.when(jnp.logical_not(jnp.max(line_ref[...]) < HUGE))
    def exact():
        for c in range(0, tiles, per):

            def top_step(r, tops):
                at = at_rows(r, step)
                return tuple(
                    jnp.maximum(top, jnp.max(group(t_ref[c + t, at, :] + wide_ref[at, :]), axis=0))
                    for t, top in enumerate(tops)
                )

            start = tuple(jnp.full((8, LANES), -jnp.inf, jnp.float32) for _ in range(per))
            tops = lax.fori_loop(0, rows // step, top_step, start)
            sums(c, [jnp.max(top, axis=0, keepdims=True) for top in tops])

    copies(out_ref, line_ref[...])


def plan_kernel(t_ref, parts_ref, tgt_mass_ref, src_lse_ref, src_mass_ref, *refs):
    plan_ref, out_ref, lse_ref, wide_ref, sum_ref, line_ref = refs
    tiles, rows, _ = t_ref.shape
    lse = combined(parts_ref, lse_all)
    lse_ref[...] = lse
    line_ref[...] = (tgt_mass_ref[...] - lse) * LOG2E
    spread((src_mass_ref[...] - src_lse_ref[...]) * LOG2E, wide_ref)
    per, step = 4, 128

    def rows_step(r, unused):
        at = at_rows(r, step)
        total = jnp.zeros((step, LANES), jnp.float32)
        own = wide_ref[at, :]
        for c in range(0, tiles, per):
            terms = [t_ref[c + t, at, :] for t in range(per)]
            values = [
                jnp.exp2(terms[t] + own + line_ref[c + t : c + t + 1, :]) for t in range(per)
            ]
            for t in range(per):
                plan_ref[c + t, at, :] = values[t]
                total += values[t]
        sum_ref[at, :] = total
        return unused

    lax.fori_loop(0, rows // step, rows_step, 0)
    out_ref[...] = collapse(sum_ref)


def row_sums_kernel(plan_ref, parts_ref, mass_ref, out_ref, sum_ref, line_ref):
    tiles, rows, _ = plan_ref.shape
    step = 512
    line_ref[...] = jnp.exp(mass_ref[...]) / combined(parts_ref, add_all)

    def rows_step(r, unused):
        at = at_rows(r, step)
        total = jnp.zeros((step, LANES), jnp.float32)
        for t in range(tiles):
            total += plan_ref[t, at, :] * line_ref[t : t + 1, :]
        sum_ref[at, :] = total
        return unused

    lax.fori_loop(0, rows // step, rows_step, 0)
    out_ref[...] = collapse(sum_ref)


def column_sums(plan_ref, scale, line_ref, wide_ref):
    tiles, rows, _ = plan_ref.shape
    spread(scale, wide_ref)
    per = tiles
    for c in range(0, tiles, per):

        def rows_step(r, totals):
            at = at_rows(r)
            own = wide_ref[at, :]
            return tuple(
                total
                + jnp.sum(
                    (plan_ref[c + t, at, :] * own).reshape(STEP // 8, 8, LANES), axis=0
                )
                for t, total in enumerate(totals)
            )

        start = tuple(jnp.zeros((8, LANES), jnp.float32) for _ in range(per))
        totals = lax.fori_loop(0, rows // STEP, rows_step, start)
        for t in range(per):
            line_ref[c + t : c + t + 1, :] = jnp.sum(totals[t], axis=0, keepdims=True)


def column_sums_kernel(plan_ref, *refs):
    parts, (mass_ref, out_ref, wide_ref, line_ref) = refs[:4], refs[4:]
    scale = jnp.exp(mass_ref[...]) / add_all(values(parts))
    column_sums(plan_ref, scale, line_ref, wide_ref)
    copies(out_ref, line_ref[...])


def last_column_sums_kernel(plan_ref, *refs):
    parts, (mass_ref, lse_ref, squares_ref) = refs[:4], refs[4:7]
    out_ref, potential_ref, wide_ref, line_ref = refs[7:]
    sums = add_all(values(parts))
    mass = mass_ref[...]
    squares = squares_ref[...] / (WIDTH * EPS)
    potential = -EPS * (lse_ref[...] + jnp.log(sums) - mass - squares)
    potential_ref[...] = potential
    tiles = plan_ref.shape[0]
    line_ref[tiles:, :] = jnp.broadcast_to(jnp.sum(potential), (8, LANES))
    column_sums(plan_ref, jnp.exp(mass) / sums, line_ref, wide_ref)
    copies(out_ref, line_ref[...])


def last_kernel(parts_ref, mass_ref, lse_ref, potential_ref, own_ref, other_ref):
    tiles = mass_ref.shape[0]
    sums = combined(parts_ref, add_all)
    potential = -EPS * (lse_ref[...] + jnp.log(sums[:tiles]) - 2.0 * mass_ref[...])
    potential_ref[...] = potential
    own_ref[...] = jnp.broadcast_to(jnp.sum(potential), (8, LANES))
    other_ref[...] = sums[tiles:]


ALL = ("row_0", "row_1", "col_0", "col_1")
SIZES = (4, 4, 4, 2)


def number(y, x, z, core):
    return ((y % 4 * 4 + x % 4) * 4 + z) * 2 + core


def turned(value, stage):
    found = {0: value}
    for k in (2, 1, 3):
        pairs = []
        for y, x, z, core in itertools.product(*map(range, SIZES)):
            along_y = (core + stage) % 2
            to = number(y + k * along_y, x + k * (1 - along_y), z, core)
            pairs.append((number(y, x, z, core), to))
        found[k] = lax.ppermute(value, ALL, pairs)
    return [found[k] for k in range(4)]


def crossed(value, k):
    pairs = []
    for y, x, z, core in itertools.product(*map(range, SIZES)):
        pairs.append((number(y, x, z, core), number(y, x, (z + k) % 4, 1 - core)))
    return lax.ppermute(value, ALL, pairs)


def body(src_points, tgt_points, log_src_mass, log_tgt_mass):
    rows, columns = src_points.shape[0], log_tgt_mass.shape[0]
    row_tiles, column_tiles = rows // LANES, columns // LANES
    src_mass = log_src_mass.reshape(row_tiles, LANES)
    tgt_mass = log_tgt_mass.reshape(column_tiles, LANES)
    place = jnp.stack([lax.axis_index(name) for name in ("row_0", "row_1", "col_1")])
    place = place.astype(jnp.int32)
    wide = pltpu.VMEM((rows, LANES), jnp.float32)
    big = pltpu.VMEM((column_tiles, rows, LANES), jnp.float32)
    line = pltpu.VMEM((column_tiles, LANES), jnp.float32)
    longer = pltpu.VMEM((column_tiles + 8, LANES), jnp.float32)
    by_row, by_column = f32(row_tiles, LANES), f32(column_tiles, LANES)
    peers_row, peers_col = lax.axis_size(ROW), lax.axis_size(COL)
    columns_out = f32(peers_row, column_tiles, LANES)

    def resident(value):
        return pltpu.with_memory_space_constraint(value, pltpu.VMEM)

    def over_col(value, combine):
        both = combine([value, lax.ppermute(value, "col_1", [(0, 1), (1, 0)])])
        return [both] + [crossed(both, k) for k in (2, 1, 3)]

    def over_row(value):
        return lax.all_to_all(value, ROW, 0, 0, tiled=True)

    first = jnp.concatenate(turned(tgt_points, 0))
    pieces = turned(first, 1)
    terms, top, sums, squares = call(
        first_terms_kernel, (big, wide, wide, by_row), [SMEM] + [VMEM] * 3, []
    )(place, src_points, first, tgt_mass)
    for k in (1, 2):
        terms, sums = call(
            functools.partial(more_terms_kernel, k), (big, wide), [SMEM] + [VMEM] * 6, [], {2: 0, 3: 1}
        )(place, src_points, resident(terms), resident(sums), resident(top), pieces[k], tgt_mass)
    terms, sums, lse = call(
        functools.partial(last_terms_kernel, 3),
        (big, wide, by_row),
        [SMEM] + [VMEM] * 6,
        [wide],
        {2: 0, 3: 1},
    )(place, src_points, resident(terms), resident(sums), resident(top), pieces[3], tgt_mass)
    lse, src_lse = call(column_kernel, (columns_out, by_row), [VMEM] * 6, [wide, line])(
        resident(terms), *over_col(lse, lse_all), src_mass
    )
    plan, sums, tgt_lse = call(
        plan_kernel, (big, by_row, by_column), [VMEM] * 5, [wide, wide, line], {0: 0}
    )(resident(terms), over_row(lse), tgt_mass, src_lse, src_mass)
    plan = resident(plan)
    sums = call(column_sums_kernel, columns_out, [VMEM] * 6, [wide, line])(
        plan, *over_col(sums, add_all), src_mass
    )
    sums = call(row_sums_kernel, by_row, [VMEM] * 3, [wide, line])(plan, over_row(sums), tgt_mass)
    sums, src_potential = call(
        last_column_sums_kernel,
        (f32(peers_row, column_tiles + 8, LANES), by_row),
        [VMEM] * 8,
        [wide, longer],
    )(plan, *over_col(sums, add_all), src_mass, src_lse, squares)
    tgt_potential, tgt_sum, src_sum = call(
        last_kernel, (by_column, f32(8, LANES), f32(8, LANES)), [VMEM] * 3, []
    )(over_row(sums), tgt_mass, tgt_lse)
    tgt_sum = add_all(over_col(tgt_sum, add_all))
    sources_all, targets_all = rows * peers_row, columns * peers_col
    mean_potentials = (src_sum / sources_all + tgt_sum / targets_all)[0, 0]
    return (src_potential.reshape(-1), tgt_potential.reshape(-1), mean_potentials)


def solution(mesh):
    finer = Mesh(mesh.devices.reshape(4, 4, 4, 2), ("row_0", "row_1", "col_0", "col_1"))
    placed = (P(ROW, None), P(COL_ROW, None), P(ROW), P(COL))
    return jax.shard_map(
        body, mesh=finer, in_specs=placed, out_specs=(P(ROW), P(COL), P()), check_vma=False
    )
```

```python
import functools
import itertools
import math

import jax
import jax.numpy as jnp
from jax import lax
from jax.experimental import pallas as pl
from jax.experimental.pallas import tpu as pltpu
from jax.sharding import Mesh
from jax.sharding import PartitionSpec as P

ROW = ("row_0", "row_1")
COL = ("col_0", "col_1")
COL_ROW = ("col_0", "col_1", "row_0", "row_1")

EPS = 0.1
WIDTH = 256
NATS = 2.0 / (WIDTH * EPS)
BITS = NATS * math.log2(math.e)
LOG2E = math.log2(math.e)
LN2 = math.log(2.0)
VMEM_LIMIT = 24 * 1024 * 1024
LANES = 128
STEP = 64
ROWS = 512
HUGE = 3.0e38

VMEM = pl.BlockSpec(memory_space=pltpu.VMEM)
SMEM = pl.BlockSpec(memory_space=pltpu.SMEM)


def call(kernel, outs, ins, scratch, aliases=None):
    return pl.pallas_call(
        kernel,
        out_shape=outs,
        in_specs=ins,
        out_specs=jax.tree.map(lambda _: VMEM, outs),
        scratch_shapes=scratch,
        input_output_aliases=aliases or {},
        compiler_params=pltpu.CompilerParams(vmem_limit_bytes=VMEM_LIMIT),
    )


def f32(*shape):
    return jax.ShapeDtypeStruct(shape, jnp.float32)


def spread(dense, wide_ref):
    for b in range(dense.shape[0]):
        square = jnp.broadcast_to(dense[b : b + 1, :], (LANES, LANES))
        wide_ref[b * LANES : (b + 1) * LANES, :] = square.T


def collapse(wide_ref):
    lines = [
        jnp.sum(wide_ref[b * LANES : (b + 1) * LANES, :].T, axis=0, keepdims=True)
        for b in range(wide_ref.shape[0] // LANES)
    ]
    return jnp.concatenate(lines, axis=0)


def collapse_top(wide_ref):
    lines = [
        wide_ref[b * LANES : (b + 1) * LANES, :].T[:1, :]
        for b in range(wide_ref.shape[0] // LANES)
    ]
    return jnp.concatenate(lines, axis=0)


def add_all(parts):
    total = parts[0]
    for part in parts[1:]:
        total = total + part
    return total


def lse_all(parts):
    top = parts[0]
    for part in parts[1:]:
        top = jnp.maximum(top, part)
    return top + jnp.log(add_all([jnp.exp(part - top) for part in parts]))


def copies(out_ref, value):
    for peer in range(out_ref.shape[0]):
        out_ref[peer] = value


def combined(parts_ref, combine):
    return combine([parts_ref[peer] for peer in range(parts_ref.shape[0])])


def values(refs):
    return [ref[...] for ref in refs]


def at_rows(r, step=STEP):
    return pl.ds(pl.multiple_of(r * step, step), step)


def lane_tile(t):
    return slice(t * LANES, (t + 1) * LANES)


def target_block(place, shift, inner):
    first_core = place[2] == 0
    shift_y = jnp.where(first_core, shift, inner)
    shift_x = jnp.where(first_core, inner, shift)
    return 4 * lax.rem(place[0] + 4 - shift_y, 4) + lax.rem(place[1] + 4 - shift_x, 4)


def chunk_biases(points, mass_ref, block):
    squares = points.astype(jnp.float32) ** 2
    squares = squares[:, :LANES] + squares[:, LANES:]
    found = []
    for side in range(2):
        square = squares[side * LANES : (side + 1) * LANES, :].T
        mass = mass_ref[pl.ds(2 * block + side, 1), :]
        found.append(mass * LOG2E - jnp.sum(square, axis=0, keepdims=True) * (0.5 * BITS))
    return found


def piece_product(x_ref, points_ref, r, m):
    return lax.dot_general(
        x_ref[r : r + ROWS, :],
        points_ref[m * 256 : (m + 1) * 256, :],
        (((1,), (1,)), ((), ())),
        preferred_element_type=jnp.float32,
    )


def piece_blocks(k, place, points_ref, mass_ref):
    blocks = [target_block(place, k, m) for m in range(4)]
    biases = [
        chunk_biases(points_ref[m * 256 : (m + 1) * 256, :], mass_ref, blocks[m]) for m in range(4)
    ]
    return blocks, biases


def first_terms_kernel(place, x_ref, points_ref, mass_ref, t_ref, top_ref, sum_ref, squares_ref):
    rows = x_ref.shape[0]
    squares = x_ref[...].astype(jnp.float32) ** 2
    sum_ref[...] = squares[:, :LANES] + squares[:, LANES:]
    squares_ref[...] = collapse(sum_ref)
    blocks, biases = piece_blocks(0, place, points_ref, mass_ref)
    for r in range(0, rows, ROWS):
        top = None
        for m in range(4):
            product = piece_product(x_ref, points_ref, r, m)
            for side in range(2):
                terms = product[:, lane_tile(side)] * BITS + biases[m][side]
                t_ref[2 * blocks[m] + side, r : r + ROWS, :] = terms
                top = terms if top is None else jnp.maximum(top, terms)
        top_ref[r : r + ROWS, :] = top

    def rows_step(r, unused):
        at = at_rows(r)
        top = jnp.max(top_ref[at, :], axis=1, keepdims=True)
        total = jnp.zeros((STEP, LANES), jnp.float32)
        for m in range(4):
            for side in range(2):
                total += jnp.exp2(t_ref[2 * blocks[m] + side, at, :] - top)
        top_ref[at, :] = jnp.broadcast_to(top, (STEP, LANES))
        sum_ref[at, :] = total
        return unused

    lax.fori_loop(0, rows // STEP, rows_step, 0)


def piece_steps(k, place, x_ref, points_ref, mass_ref, top_ref, old_sum_ref, t_ref, sum_ref):
    blocks, biases = piece_blocks(k, place, points_ref, mass_ref)
    for r in range(0, x_ref.shape[0], ROWS):
        top = top_ref[r : r + ROWS, :]
        total = old_sum_ref[r : r + ROWS, :]
        for m in range(4):
            product = piece_product(x_ref, points_ref, r, m)
            for side in range(2):
                terms = product[:, lane_tile(side)] * BITS + biases[m][side]
                t_ref[2 * blocks[m] + side, r : r + ROWS, :] = terms
                total += jnp.exp2(terms - top)
        sum_ref[r : r + ROWS, :] = total


def more_terms_kernel(k, place, x_ref, old_ref, old_sum_ref, top_ref, points_ref, mass_ref, *refs):
    t_ref, sum_ref = refs
    piece_steps(k, place, x_ref, points_ref, mass_ref, top_ref, old_sum_ref, t_ref, sum_ref)


def last_terms_kernel(k, place, x_ref, old_ref, old_sum_ref, old_top_ref, points_ref, mass_ref, *refs):
    t_ref, sum_ref, out_ref, top_ref = refs
    tiles, rows, _ = t_ref.shape
    piece_steps(k, place, x_ref, points_ref, mass_ref, old_top_ref, old_sum_ref, t_ref, sum_ref)
    total = collapse(sum_ref)
    out_ref[...] = collapse_top(old_top_ref) * LN2 + jnp.log(total)

    @pl.when(jnp.logical_not(jnp.max(total) < HUGE))
    def exact():
        def rows_step(r, unused):
            at = at_rows(r)
            top = jnp.full((STEP, LANES), -jnp.inf, jnp.float32)
            for t in range(tiles):
                top = jnp.maximum(top, t_ref[t, at, :])
            top = jnp.max(top, axis=1, keepdims=True)
            total = jnp.zeros((STEP, LANES), jnp.float32)
            for t in range(tiles):
                total += jnp.exp2(t_ref[t, at, :] - top)
            top_ref[at, :] = jnp.broadcast_to(top, (STEP, LANES))
            sum_ref[at, :] = total
            return unused

        lax.fori_loop(0, rows // STEP, rows_step, 0)
        out_ref[...] = collapse_top(top_ref) * LN2 + jnp.log(collapse(sum_ref))


def column_kernel(t_ref, *refs):
    parts, (mass_ref, out_ref, lse_ref, wide_ref, line_ref) = refs[:4], refs[4:]
    tiles, rows, _ = t_ref.shape
    lse = lse_all(values(parts))
    lse_ref[...] = lse
    spread((mass_ref[...] - lse) * LOG2E, wide_ref)
    per, step = 32, 128

    def group(value):
        return value.reshape(step // 8, 8, LANES)

    def sums(c, tops):
        wide = [jnp.broadcast_to(top, (step, LANES)) for top in tops]

        def sum_step(r, totals):
            at = at_rows(r, step)
            own = wide_ref[at, :]
            return tuple(
                total
                + jnp.sum(
                    group(jnp.exp2(t_ref[c + t, at, :] + own - wide[t])), axis=0
                )
                for t, total in enumerate(totals)
            )

        start = tuple(jnp.zeros((8, LANES), jnp.float32) for _ in range(per))
        totals = lax.fori_loop(0, rows // step, sum_step, start)
        for t in range(per):
            total = jnp.sum(totals[t], axis=0, keepdims=True)
            line_ref[c + t : c + t + 1, :] = tops[t] * LN2 + jnp.log(total)

    for c in range(0, tiles, per):
        tops = [
            jnp.max(t_ref[c + t, :step, :] + wide_ref[:step, :], axis=0, keepdims=True)
            for t in range(per)
        ]
        sums(c, tops)

    @pl.when(jnp.logical_not(jnp.max(line_ref[...]) < HUGE))
    def exact():
        for c in range(0, tiles, per):

            def top_step(r, tops):
                at = at_rows(r, step)
                return tuple(
                    jnp.maximum(top, jnp.max(group(t_ref[c + t, at, :] + wide_ref[at, :]), axis=0))
                    for t, top in enumerate(tops)
                )

            start = tuple(jnp.full((8, LANES), -jnp.inf, jnp.float32) for _ in range(per))
            tops = lax.fori_loop(0, rows // step, top_step, start)
            sums(c, [jnp.max(top, axis=0, keepdims=True) for top in tops])

    copies(out_ref, line_ref[...])


def plan_kernel(t_ref, parts_ref, tgt_mass_ref, src_lse_ref, src_mass_ref, *refs):
    plan_ref, out_ref, lse_ref, wide_ref, sum_ref, line_ref = refs
    tiles, rows, _ = t_ref.shape
    lse = combined(parts_ref, lse_all)
    lse_ref[...] = lse
    line_ref[...] = (tgt_mass_ref[...] - lse) * LOG2E
    spread((src_mass_ref[...] - src_lse_ref[...]) * LOG2E, wide_ref)
    per, step = 4, 128

    def rows_step(r, unused):
        at = at_rows(r, step)
        total = jnp.zeros((step, LANES), jnp.float32)
        own = wide_ref[at, :]
        for c in range(0, tiles, per):
            terms = [t_ref[c + t, at, :] for t in range(per)]
            values = [
                jnp.exp2(terms[t] + own + line_ref[c + t : c + t + 1, :]) for t in range(per)
            ]
            for t in range(per):
                plan_ref[c + t, at, :] = values[t]
                total += values[t]
        sum_ref[at, :] = total
        return unused

    lax.fori_loop(0, rows // step, rows_step, 0)
    out_ref[...] = collapse(sum_ref)


def row_sums_kernel(plan_ref, parts_ref, mass_ref, out_ref, sum_ref, line_ref):
    tiles, rows, _ = plan_ref.shape
    step = 512
    line_ref[...] = jnp.exp(mass_ref[...]) / combined(parts_ref, add_all)

    def rows_step(r, unused):
        at = at_rows(r, step)
        total = jnp.zeros((step, LANES), jnp.float32)
        for t in range(tiles):
            total += plan_ref[t, at, :] * line_ref[t : t + 1, :]
        sum_ref[at, :] = total
        return unused

    lax.fori_loop(0, rows // step, rows_step, 0)
    out_ref[...] = collapse(sum_ref)


def column_sums(plan_ref, scale, line_ref, wide_ref):
    tiles, rows, _ = plan_ref.shape
    spread(scale, wide_ref)
    per = tiles
    for c in range(0, tiles, per):

        def rows_step(r, totals):
            at = at_rows(r)
            own = wide_ref[at, :]
            return tuple(
                total
                + jnp.sum(
                    (plan_ref[c + t, at, :] * own).reshape(STEP // 8, 8, LANES), axis=0
                )
                for t, total in enumerate(totals)
            )

        start = tuple(jnp.zeros((8, LANES), jnp.float32) for _ in range(per))
        totals = lax.fori_loop(0, rows // STEP, rows_step, start)
        for t in range(per):
            line_ref[c + t : c + t + 1, :] = jnp.sum(totals[t], axis=0, keepdims=True)


def column_sums_kernel(plan_ref, *refs):
    parts, (mass_ref, out_ref, wide_ref, line_ref) = refs[:4], refs[4:]
    scale = jnp.exp(mass_ref[...]) / add_all(values(parts))
    column_sums(plan_ref, scale, line_ref, wide_ref)
    copies(out_ref, line_ref[...])


def last_column_sums_kernel(plan_ref, *refs):
    parts, (mass_ref, lse_ref, squares_ref) = refs[:4], refs[4:7]
    out_ref, potential_ref, wide_ref, line_ref = refs[7:]
    sums = add_all(values(parts))
    mass = mass_ref[...]
    squares = squares_ref[...] / (WIDTH * EPS)
    potential = -EPS * (lse_ref[...] + jnp.log(sums) - mass - squares)
    potential_ref[...] = potential
    tiles = plan_ref.shape[0]
    line_ref[tiles:, :] = jnp.broadcast_to(jnp.sum(potential), (8, LANES))
    column_sums(plan_ref, jnp.exp(mass) / sums, line_ref, wide_ref)
    copies(out_ref, line_ref[...])


def last_kernel(parts_ref, mass_ref, lse_ref, potential_ref, own_ref, other_ref):
    tiles = mass_ref.shape[0]
    sums = combined(parts_ref, add_all)
    potential = -EPS * (lse_ref[...] + jnp.log(sums[:tiles]) - 2.0 * mass_ref[...])
    potential_ref[...] = potential
    own_ref[...] = jnp.broadcast_to(jnp.sum(potential), (8, LANES))
    other_ref[...] = sums[tiles:]


ALL = ("row_0", "row_1", "col_0", "col_1")
SIZES = (4, 4, 4, 2)


def number(y, x, z, core):
    return ((y % 4 * 4 + x % 4) * 4 + z) * 2 + core


def turned(value, stage, order):
    found = {0: value}
    for k in order:
        pairs = []
        for y, x, z, core in itertools.product(*map(range, SIZES)):
            along_y = (core + stage) % 2
            to = number(y + k * along_y, x + k * (1 - along_y), z, core)
            pairs.append((number(y, x, z, core), to))
        found[k] = lax.ppermute(value, ALL, pairs)
    return [found[k] for k in range(4)]


def crossed(value, k):
    pairs = []
    for y, x, z, core in itertools.product(*map(range, SIZES)):
        pairs.append((number(y, x, z, core), number(y, x, (z + k) % 4, 1 - core)))
    return lax.ppermute(value, ALL, pairs)


def body(src_points, tgt_points, log_src_mass, log_tgt_mass):
    rows, columns = src_points.shape[0], log_tgt_mass.shape[0]
    row_tiles, column_tiles = rows // LANES, columns // LANES
    src_mass = log_src_mass.reshape(row_tiles, LANES)
    tgt_mass = log_tgt_mass.reshape(column_tiles, LANES)
    place = jnp.stack([lax.axis_index(name) for name in ("row_0", "row_1", "col_1")])
    place = place.astype(jnp.int32)
    wide = pltpu.VMEM((rows, LANES), jnp.float32)
    big = pltpu.VMEM((column_tiles, rows, LANES), jnp.float32)
    line = pltpu.VMEM((column_tiles, LANES), jnp.float32)
    longer = pltpu.VMEM((column_tiles + 8, LANES), jnp.float32)
    by_row, by_column = f32(row_tiles, LANES), f32(column_tiles, LANES)
    peers_row, peers_col = lax.axis_size(ROW), lax.axis_size(COL)
    columns_out = f32(peers_row, column_tiles, LANES)

    def resident(value):
        return pltpu.with_memory_space_constraint(value, pltpu.VMEM)

    def over_col(value, combine):
        both = combine([value, lax.ppermute(value, "col_1", [(0, 1), (1, 0)])])
        return [both] + [crossed(both, k) for k in (2, 1, 3)]

    def over_row(value):
        return lax.all_to_all(value, ROW, 0, 0, tiled=True)

    first = jnp.concatenate(turned(tgt_points, 0, (2, 1, 3)))
    pieces = turned(first, 1, (1, 3, 2))
    terms, top, sums, squares = call(
        first_terms_kernel, (big, wide, wide, by_row), [SMEM] + [VMEM] * 3, []
    )(place, src_points, first, tgt_mass)
    for k in (1, 3):
        terms, sums = call(
            functools.partial(more_terms_kernel, k), (big, wide), [SMEM] + [VMEM] * 6, [], {2: 0, 3: 1}
        )(place, src_points, resident(terms), resident(sums), resident(top), pieces[k], tgt_mass)
    terms, sums, lse = call(
        functools.partial(last_terms_kernel, 2),
        (big, wide, by_row),
        [SMEM] + [VMEM] * 6,
        [wide],
        {2: 0, 3: 1},
    )(place, src_points, resident(terms), resident(sums), resident(top), pieces[2], tgt_mass)
    lse, src_lse = call(column_kernel, (columns_out, by_row), [VMEM] * 6, [wide, line])(
        resident(terms), *over_col(lse, lse_all), src_mass
    )
    plan, sums, tgt_lse = call(
        plan_kernel, (big, by_row, by_column), [VMEM] * 5, [wide, wide, line], {0: 0}
    )(resident(terms), over_row(lse), tgt_mass, src_lse, src_mass)
    plan = resident(plan)
    sums = call(column_sums_kernel, columns_out, [VMEM] * 6, [wide, line])(
        plan, *over_col(sums, add_all), src_mass
    )
    sums = call(row_sums_kernel, by_row, [VMEM] * 3, [wide, line])(plan, over_row(sums), tgt_mass)
    sums, src_potential = call(
        last_column_sums_kernel,
        (f32(peers_row, column_tiles + 8, LANES), by_row),
        [VMEM] * 8,
        [wide, longer],
    )(plan, *over_col(sums, add_all), src_mass, src_lse, squares)
    tgt_potential, tgt_sum, src_sum = call(
        last_kernel, (by_column, f32(8, LANES), f32(8, LANES)), [VMEM] * 3, []
    )(over_row(sums), tgt_mass, tgt_lse)
    tgt_sum = add_all(over_col(tgt_sum, add_all))
    sources_all, targets_all = rows * peers_row, columns * peers_col
    mean_potentials = (src_sum / sources_all + tgt_sum / targets_all)[0, 0]
    return (src_potential.reshape(-1), tgt_potential.reshape(-1), mean_potentials)


def solution(mesh):
    finer = Mesh(mesh.devices.reshape(4, 4, 4, 2), ("row_0", "row_1", "col_0", "col_1"))
    placed = (P(ROW, None), P(COL_ROW, None), P(ROW), P(COL))
    return jax.shard_map(
        body, mesh=finer, in_specs=placed, out_specs=(P(ROW), P(COL), P()), check_vma=False
    )
```

```python
import functools
import itertools
import math

import jax
import jax.numpy as jnp
from jax import lax
from jax.experimental import pallas as pl
from jax.experimental.pallas import tpu as pltpu
from jax.sharding import Mesh
from jax.sharding import PartitionSpec as P

ROW = ("row_0", "row_1")
COL = ("col_0", "col_1")
COL_ROW = ("col_0", "col_1", "row_0", "row_1")

EPS = 0.1
WIDTH = 256
NATS = 2.0 / (WIDTH * EPS)
BITS = NATS * math.log2(math.e)
LOG2E = math.log2(math.e)
LN2 = math.log(2.0)
VMEM_LIMIT = 24 * 1024 * 1024
LANES = 128
STEP = 64
ROWS = 512
HUGE = 3.0e38

VMEM = pl.BlockSpec(memory_space=pltpu.VMEM)
SMEM = pl.BlockSpec(memory_space=pltpu.SMEM)


def call(kernel, outs, ins, scratch, aliases=None):
    return pl.pallas_call(
        kernel,
        out_shape=outs,
        in_specs=ins,
        out_specs=jax.tree.map(lambda _: VMEM, outs),
        scratch_shapes=scratch,
        input_output_aliases=aliases or {},
        compiler_params=pltpu.CompilerParams(vmem_limit_bytes=VMEM_LIMIT),
    )


def f32(*shape):
    return jax.ShapeDtypeStruct(shape, jnp.float32)


def spread(dense, wide_ref):
    for b in range(dense.shape[0]):
        square = jnp.broadcast_to(dense[b : b + 1, :], (LANES, LANES))
        wide_ref[b * LANES : (b + 1) * LANES, :] = square.T


def collapse(wide_ref):
    lines = [
        jnp.sum(wide_ref[b * LANES : (b + 1) * LANES, :].T, axis=0, keepdims=True)
        for b in range(wide_ref.shape[0] // LANES)
    ]
    return jnp.concatenate(lines, axis=0)


def collapse_top(wide_ref):
    lines = [
        wide_ref[b * LANES : (b + 1) * LANES, :].T[:1, :]
        for b in range(wide_ref.shape[0] // LANES)
    ]
    return jnp.concatenate(lines, axis=0)


def add_all(parts):
    total = parts[0]
    for part in parts[1:]:
        total = total + part
    return total


def lse_all(parts):
    top = parts[0]
    for part in parts[1:]:
        top = jnp.maximum(top, part)
    return top + jnp.log(add_all([jnp.exp(part - top) for part in parts]))


def copies(out_ref, value):
    for peer in range(out_ref.shape[0]):
        out_ref[peer] = value


def combined(parts_ref, combine):
    return combine([parts_ref[peer] for peer in range(parts_ref.shape[0])])


def values(refs):
    return [ref[...] for ref in refs]


def at_rows(r, step=STEP):
    return pl.ds(pl.multiple_of(r * step, step), step)


def lane_tile(t):
    return slice(t * LANES, (t + 1) * LANES)


def target_block(place, shift, inner):
    first_core = place[2] == 0
    shift_y = jnp.where(first_core, shift, inner)
    shift_x = jnp.where(first_core, inner, shift)
    return 4 * lax.rem(place[0] + 4 - shift_y, 4) + lax.rem(place[1] + 4 - shift_x, 4)


def chunk_biases(points, mass_ref, block):
    squares = points.astype(jnp.float32) ** 2
    squares = squares[:, :LANES] + squares[:, LANES:]
    found = []
    for side in range(2):
        square = squares[side * LANES : (side + 1) * LANES, :].T
        mass = mass_ref[pl.ds(2 * block + side, 1), :]
        found.append(mass * LOG2E - jnp.sum(square, axis=0, keepdims=True) * (0.5 * BITS))
    return found


def piece_product(x_ref, points_ref, r, m):
    return lax.dot_general(
        x_ref[r : r + ROWS, :],
        points_ref[m * 256 : (m + 1) * 256, :],
        (((1,), (1,)), ((), ())),
        preferred_element_type=jnp.float32,
    )


def piece_blocks(k, place, points_ref, mass_ref):
    blocks = [target_block(place, k, m) for m in range(4)]
    biases = [
        chunk_biases(points_ref[m * 256 : (m + 1) * 256, :], mass_ref, blocks[m]) for m in range(4)
    ]
    return blocks, biases


def first_terms_kernel(place, x_ref, points_ref, mass_ref, t_ref, top_ref, sum_ref, squares_ref):
    rows = x_ref.shape[0]
    squares = x_ref[...].astype(jnp.float32) ** 2
    sum_ref[...] = squares[:, :LANES] + squares[:, LANES:]
    squares_ref[...] = collapse(sum_ref)
    blocks, biases = piece_blocks(0, place, points_ref, mass_ref)
    for r in range(0, rows, ROWS):
        top = None
        for m in range(4):
            product = piece_product(x_ref, points_ref, r, m)
            for side in range(2):
                terms = product[:, lane_tile(side)] * BITS + biases[m][side]
                t_ref[2 * blocks[m] + side, r : r + ROWS, :] = terms
                top = terms if top is None else jnp.maximum(top, terms)
        top_ref[r : r + ROWS, :] = top

    def rows_step(r, unused):
        at = at_rows(r)
        top = jnp.max(top_ref[at, :], axis=1, keepdims=True)
        total = jnp.zeros((STEP, LANES), jnp.float32)
        for m in range(4):
            for side in range(2):
                total += jnp.exp2(t_ref[2 * blocks[m] + side, at, :] - top)
        top_ref[at, :] = jnp.broadcast_to(top, (STEP, LANES))
        sum_ref[at, :] = total
        return unused

    lax.fori_loop(0, rows // STEP, rows_step, 0)


def piece_steps(pieces, place, x_ref, mass_ref, top_ref, old_sum_ref, t_ref, sum_ref):
    chunks = []
    for k, points_ref in pieces:
        blocks, biases = piece_blocks(k, place, points_ref, mass_ref)
        chunks += [(points_ref, m, blocks[m], biases[m]) for m in range(4)]
    for r in range(0, x_ref.shape[0], ROWS):
        top = top_ref[r : r + ROWS, :]
        total = old_sum_ref[r : r + ROWS, :]
        for points_ref, m, block, bias in chunks:
            product = piece_product(x_ref, points_ref, r, m)
            for side in range(2):
                terms = product[:, lane_tile(side)] * BITS + bias[side]
                t_ref[2 * block + side, r : r + ROWS, :] = terms
                total += jnp.exp2(terms - top)
        sum_ref[r : r + ROWS, :] = total


def more_terms_kernel(k, place, x_ref, old_ref, old_sum_ref, top_ref, points_ref, mass_ref, *refs):
    t_ref, sum_ref = refs
    pieces = [(k, points_ref)]
    piece_steps(pieces, place, x_ref, mass_ref, top_ref, old_sum_ref, t_ref, sum_ref)


def last_terms_kernel(shifts, place, x_ref, old_ref, old_sum_ref, old_top_ref, *refs):
    points_ref, more_ref, mass_ref, t_ref, sum_ref, out_ref, top_ref = refs
    tiles, rows, _ = t_ref.shape
    pieces = list(zip(shifts, (points_ref, more_ref)))
    piece_steps(pieces, place, x_ref, mass_ref, old_top_ref, old_sum_ref, t_ref, sum_ref)
    total = collapse(sum_ref)
    out_ref[...] = collapse_top(old_top_ref) * LN2 + jnp.log(total)

    @pl.when(jnp.logical_not(jnp.max(total) < HUGE))
    def exact():
        def rows_step(r, unused):
            at = at_rows(r)
            top = jnp.full((STEP, LANES), -jnp.inf, jnp.float32)
            for t in range(tiles):
                top = jnp.maximum(top, t_ref[t, at, :])
            top = jnp.max(top, axis=1, keepdims=True)
            total = jnp.zeros((STEP, LANES), jnp.float32)
            for t in range(tiles):
                total += jnp.exp2(t_ref[t, at, :] - top)
            top_ref[at, :] = jnp.broadcast_to(top, (STEP, LANES))
            sum_ref[at, :] = total
            return unused

        lax.fori_loop(0, rows // STEP, rows_step, 0)
        out_ref[...] = collapse_top(top_ref) * LN2 + jnp.log(collapse(sum_ref))


def column_kernel(t_ref, *refs):
    parts, (mass_ref, out_ref, lse_ref, wide_ref, line_ref) = refs[:4], refs[4:]
    tiles, rows, _ = t_ref.shape
    lse = lse_all(values(parts))
    lse_ref[...] = lse
    spread((mass_ref[...] - lse) * LOG2E, wide_ref)
    per, step = 32, 128

    def group(value):
        return value.reshape(step // 8, 8, LANES)

    def sums(c, tops):
        wide = [jnp.broadcast_to(top, (step, LANES)) for top in tops]

        def sum_step(r, totals):
            at = at_rows(r, step)
            own = wide_ref[at, :]
            return tuple(
                total
                + jnp.sum(
                    group(jnp.exp2(t_ref[c + t, at, :] + own - wide[t])), axis=0
                )
                for t, total in enumerate(totals)
            )

        start = tuple(jnp.zeros((8, LANES), jnp.float32) for _ in range(per))
        totals = lax.fori_loop(0, rows // step, sum_step, start)
        for t in range(per):
            total = jnp.sum(totals[t], axis=0, keepdims=True)
            line_ref[c + t : c + t + 1, :] = tops[t] * LN2 + jnp.log(total)

    for c in range(0, tiles, per):
        tops = [
            jnp.max(t_ref[c + t, :step, :] + wide_ref[:step, :], axis=0, keepdims=True)
            for t in range(per)
        ]
        sums(c, tops)

    @pl.when(jnp.logical_not(jnp.max(line_ref[...]) < HUGE))
    def exact():
        for c in range(0, tiles, per):

            def top_step(r, tops):
                at = at_rows(r, step)
                return tuple(
                    jnp.maximum(top, jnp.max(group(t_ref[c + t, at, :] + wide_ref[at, :]), axis=0))
                    for t, top in enumerate(tops)
                )

            start = tuple(jnp.full((8, LANES), -jnp.inf, jnp.float32) for _ in range(per))
            tops = lax.fori_loop(0, rows // step, top_step, start)
            sums(c, [jnp.max(top, axis=0, keepdims=True) for top in tops])

    copies(out_ref, line_ref[...])


def plan_kernel(t_ref, parts_ref, tgt_mass_ref, src_lse_ref, src_mass_ref, *refs):
    plan_ref, out_ref, lse_ref, wide_ref, sum_ref, line_ref = refs
    tiles, rows, _ = t_ref.shape
    lse = combined(parts_ref, lse_all)
    lse_ref[...] = lse
    line_ref[...] = (tgt_mass_ref[...] - lse) * LOG2E
    spread((src_mass_ref[...] - src_lse_ref[...]) * LOG2E, wide_ref)
    per, step = 4, 128

    def rows_step(r, unused):
        at = at_rows(r, step)
        total = jnp.zeros((step, LANES), jnp.float32)
        own = wide_ref[at, :]
        for c in range(0, tiles, per):
            terms = [t_ref[c + t, at, :] for t in range(per)]
            values = [
                jnp.exp2(terms[t] + own + line_ref[c + t : c + t + 1, :]) for t in range(per)
            ]
            for t in range(per):
                plan_ref[c + t, at, :] = values[t]
                total += values[t]
        sum_ref[at, :] = total
        return unused

    lax.fori_loop(0, rows // step, rows_step, 0)
    out_ref[...] = collapse(sum_ref)


def row_sums_kernel(plan_ref, parts_ref, mass_ref, out_ref, sum_ref, line_ref):
    tiles, rows, _ = plan_ref.shape
    step = 512
    line_ref[...] = jnp.exp(mass_ref[...]) / combined(parts_ref, add_all)

    def rows_step(r, unused):
        at = at_rows(r, step)
        total = jnp.zeros((step, LANES), jnp.float32)
        for t in range(tiles):
            total += plan_ref[t, at, :] * line_ref[t : t + 1, :]
        sum_ref[at, :] = total
        return unused

    lax.fori_loop(0, rows // step, rows_step, 0)
    out_ref[...] = collapse(sum_ref)


def column_sums(plan_ref, scale, line_ref, wide_ref):
    tiles, rows, _ = plan_ref.shape
    spread(scale, wide_ref)
    per = tiles
    for c in range(0, tiles, per):

        def rows_step(r, totals):
            at = at_rows(r)
            own = wide_ref[at, :]
            return tuple(
                total
                + jnp.sum(
                    (plan_ref[c + t, at, :] * own).reshape(STEP // 8, 8, LANES), axis=0
                )
                for t, total in enumerate(totals)
            )

        start = tuple(jnp.zeros((8, LANES), jnp.float32) for _ in range(per))
        totals = lax.fori_loop(0, rows // STEP, rows_step, start)
        for t in range(per):
            line_ref[c + t : c + t + 1, :] = jnp.sum(totals[t], axis=0, keepdims=True)


def column_sums_kernel(plan_ref, *refs):
    parts, (mass_ref, out_ref, wide_ref, line_ref) = refs[:4], refs[4:]
    scale = jnp.exp(mass_ref[...]) / add_all(values(parts))
    column_sums(plan_ref, scale, line_ref, wide_ref)
    copies(out_ref, line_ref[...])


def last_column_sums_kernel(plan_ref, *refs):
    parts, (mass_ref, lse_ref, squares_ref) = refs[:4], refs[4:7]
    out_ref, potential_ref, wide_ref, line_ref = refs[7:]
    sums = add_all(values(parts))
    mass = mass_ref[...]
    squares = squares_ref[...] / (WIDTH * EPS)
    potential = -EPS * (lse_ref[...] + jnp.log(sums) - mass - squares)
    potential_ref[...] = potential
    tiles = plan_ref.shape[0]
    line_ref[tiles:, :] = jnp.broadcast_to(jnp.sum(potential), (8, LANES))
    column_sums(plan_ref, jnp.exp(mass) / sums, line_ref, wide_ref)
    copies(out_ref, line_ref[...])


def last_kernel(parts_ref, mass_ref, lse_ref, potential_ref, own_ref, other_ref):
    tiles = mass_ref.shape[0]
    sums = combined(parts_ref, add_all)
    potential = -EPS * (lse_ref[...] + jnp.log(sums[:tiles]) - 2.0 * mass_ref[...])
    potential_ref[...] = potential
    own_ref[...] = jnp.broadcast_to(jnp.sum(potential), (8, LANES))
    other_ref[...] = sums[tiles:]


ALL = ("row_0", "row_1", "col_0", "col_1")
SIZES = (4, 4, 4, 2)


def number(y, x, z, core):
    return ((y % 4 * 4 + x % 4) * 4 + z) * 2 + core


def turned(value, stage, order):
    found = {0: value}
    for k in order:
        pairs = []
        for y, x, z, core in itertools.product(*map(range, SIZES)):
            along_y = (core + stage) % 2
            to = number(y + k * along_y, x + k * (1 - along_y), z, core)
            pairs.append((number(y, x, z, core), to))
        found[k] = lax.ppermute(value, ALL, pairs)
    return [found[k] for k in range(4)]


def crossed(value, k):
    pairs = []
    for y, x, z, core in itertools.product(*map(range, SIZES)):
        pairs.append((number(y, x, z, core), number(y, x, (z + k) % 4, 1 - core)))
    return lax.ppermute(value, ALL, pairs)


def body(src_points, tgt_points, log_src_mass, log_tgt_mass):
    rows, columns = src_points.shape[0], log_tgt_mass.shape[0]
    row_tiles, column_tiles = rows // LANES, columns // LANES
    src_mass = log_src_mass.reshape(row_tiles, LANES)
    tgt_mass = log_tgt_mass.reshape(column_tiles, LANES)
    place = jnp.stack([lax.axis_index(name) for name in ("row_0", "row_1", "col_1")])
    place = place.astype(jnp.int32)
    wide = pltpu.VMEM((rows, LANES), jnp.float32)
    big = pltpu.VMEM((column_tiles, rows, LANES), jnp.float32)
    line = pltpu.VMEM((column_tiles, LANES), jnp.float32)
    longer = pltpu.VMEM((column_tiles + 8, LANES), jnp.float32)
    by_row, by_column = f32(row_tiles, LANES), f32(column_tiles, LANES)
    peers_row, peers_col = lax.axis_size(ROW), lax.axis_size(COL)
    columns_out = f32(peers_row, column_tiles, LANES)

    def resident(value):
        return pltpu.with_memory_space_constraint(value, pltpu.VMEM)

    def over_col(value, combine):
        both = combine([value, lax.ppermute(value, "col_1", [(0, 1), (1, 0)])])
        return [both] + [crossed(both, k) for k in (2, 1, 3)]

    def over_row(value):
        return lax.all_to_all(value, ROW, 0, 0, tiled=True)

    first = jnp.concatenate(turned(tgt_points, 0, (2, 1, 3)))
    pieces = turned(first, 1, (1, 3, 2))
    terms, top, sums, squares = call(
        first_terms_kernel, (big, wide, wide, by_row), [SMEM] + [VMEM] * 3, []
    )(place, src_points, first, tgt_mass)
    for k in (1,):
        terms, sums = call(
            functools.partial(more_terms_kernel, k), (big, wide), [SMEM] + [VMEM] * 6, [], {2: 0, 3: 1}
        )(place, src_points, resident(terms), resident(sums), resident(top), pieces[k], tgt_mass)
    terms, sums, lse = call(
        functools.partial(last_terms_kernel, (3, 2)),
        (big, wide, by_row),
        [SMEM] + [VMEM] * 7,
        [wide],
        {2: 0, 3: 1},
    )(place, src_points, resident(terms), resident(sums), resident(top), pieces[3], pieces[2], tgt_mass)
    lse, src_lse = call(column_kernel, (columns_out, by_row), [VMEM] * 6, [wide, line])(
        resident(terms), *over_col(lse, lse_all), src_mass
    )
    plan, sums, tgt_lse = call(
        plan_kernel, (big, by_row, by_column), [VMEM] * 5, [wide, wide, line], {0: 0}
    )(resident(terms), over_row(lse), tgt_mass, src_lse, src_mass)
    plan = resident(plan)
    sums = call(column_sums_kernel, columns_out, [VMEM] * 6, [wide, line])(
        plan, *over_col(sums, add_all), src_mass
    )
    sums = call(row_sums_kernel, by_row, [VMEM] * 3, [wide, line])(plan, over_row(sums), tgt_mass)
    sums, src_potential = call(
        last_column_sums_kernel,
        (f32(peers_row, column_tiles + 8, LANES), by_row),
        [VMEM] * 8,
        [wide, longer],
    )(plan, *over_col(sums, add_all), src_mass, src_lse, squares)
    tgt_potential, tgt_sum, src_sum = call(
        last_kernel, (by_column, f32(8, LANES), f32(8, LANES)), [VMEM] * 3, []
    )(over_row(sums), tgt_mass, tgt_lse)
    tgt_sum = add_all(over_col(tgt_sum, add_all))
    sources_all, targets_all = rows * peers_row, columns * peers_col
    mean_potentials = (src_sum / sources_all + tgt_sum / targets_all)[0, 0]
    return (src_potential.reshape(-1), tgt_potential.reshape(-1), mean_potentials)


def solution(mesh):
    finer = Mesh(mesh.devices.reshape(4, 4, 4, 2), ("row_0", "row_1", "col_0", "col_1"))
    placed = (P(ROW, None), P(COL_ROW, None), P(ROW), P(COL))
    return jax.shard_map(
        body, mesh=finer, in_specs=placed, out_specs=(P(ROW), P(COL), P()), check_vma=False
    )
```

```python
import functools
import itertools
import math

import jax
import jax.numpy as jnp
from jax import lax
from jax.experimental import pallas as pl
from jax.experimental.pallas import tpu as pltpu
from jax.sharding import Mesh
from jax.sharding import PartitionSpec as P

ROW = ("row_0", "row_1")
COL = ("col_0", "col_1")
COL_ROW = ("col_0", "col_1", "row_0", "row_1")

EPS = 0.1
WIDTH = 256
NATS = 2.0 / (WIDTH * EPS)
BITS = NATS * math.log2(math.e)
LOG2E = math.log2(math.e)
LN2 = math.log(2.0)
VMEM_LIMIT = 24 * 1024 * 1024
LANES = 128
STEP = 64
ROWS = 512
HUGE = 3.0e38

VMEM = pl.BlockSpec(memory_space=pltpu.VMEM)
SMEM = pl.BlockSpec(memory_space=pltpu.SMEM)


def call(kernel, outs, ins, scratch, aliases=None):
    return pl.pallas_call(
        kernel,
        out_shape=outs,
        in_specs=ins,
        out_specs=jax.tree.map(lambda _: VMEM, outs),
        scratch_shapes=scratch,
        input_output_aliases=aliases or {},
        compiler_params=pltpu.CompilerParams(vmem_limit_bytes=VMEM_LIMIT),
    )


def f32(*shape):
    return jax.ShapeDtypeStruct(shape, jnp.float32)


def spread(dense, wide_ref):
    for b in range(dense.shape[0]):
        square = jnp.broadcast_to(dense[b : b + 1, :], (LANES, LANES))
        wide_ref[b * LANES : (b + 1) * LANES, :] = square.T


def collapse(wide_ref):
    lines = [
        jnp.sum(wide_ref[b * LANES : (b + 1) * LANES, :].T, axis=0, keepdims=True)
        for b in range(wide_ref.shape[0] // LANES)
    ]
    return jnp.concatenate(lines, axis=0)


def collapse_top(wide_ref):
    lines = [
        wide_ref[b * LANES : (b + 1) * LANES, :].T[:1, :]
        for b in range(wide_ref.shape[0] // LANES)
    ]
    return jnp.concatenate(lines, axis=0)


def add_all(parts):
    total = parts[0]
    for part in parts[1:]:
        total = total + part
    return total


def lse_all(parts):
    top = parts[0]
    for part in parts[1:]:
        top = jnp.maximum(top, part)
    return top + jnp.log(add_all([jnp.exp(part - top) for part in parts]))


def copies(out_ref, value):
    for peer in range(out_ref.shape[0]):
        out_ref[peer] = value


def combined(parts_ref, combine):
    return combine([parts_ref[peer] for peer in range(parts_ref.shape[0])])


def values(refs):
    return [ref[...] for ref in refs]


def at_rows(r, step=STEP):
    return pl.ds(pl.multiple_of(r * step, step), step)


def lane_tile(t):
    return slice(t * LANES, (t + 1) * LANES)


def target_block(place, shift, inner):
    first_core = place[2] == 0
    shift_y = jnp.where(first_core, shift, inner)
    shift_x = jnp.where(first_core, inner, shift)
    return 4 * lax.rem(place[0] + 4 - shift_y, 4) + lax.rem(place[1] + 4 - shift_x, 4)


def chunk_biases(points, mass_ref, block):
    squares = points.astype(jnp.float32) ** 2
    squares = squares[:, :LANES] + squares[:, LANES:]
    found = []
    for side in range(2):
        square = squares[side * LANES : (side + 1) * LANES, :].T
        mass = mass_ref[pl.ds(2 * block + side, 1), :]
        found.append(mass * LOG2E - jnp.sum(square, axis=0, keepdims=True) * (0.5 * BITS))
    return found


def piece_product(x_ref, points_ref, r, m):
    return lax.dot_general(
        x_ref[r : r + ROWS, :],
        points_ref[m * 256 : (m + 1) * 256, :],
        (((1,), (1,)), ((), ())),
        preferred_element_type=jnp.float32,
    )


def piece_blocks(k, place, points_ref, mass_ref):
    blocks = [target_block(place, k, m) for m in range(4)]
    biases = [
        chunk_biases(points_ref[m * 256 : (m + 1) * 256, :], mass_ref, blocks[m]) for m in range(4)
    ]
    return blocks, biases


def first_terms_kernel(place, x_ref, points_ref, mass_ref, t_ref, top_ref, sum_ref, *refs):
    squares_ref, top_line_ref = refs
    rows = x_ref.shape[0]
    squares = x_ref[...].astype(jnp.float32) ** 2
    sum_ref[...] = squares[:, :LANES] + squares[:, LANES:]
    squares_ref[...] = collapse(sum_ref)
    blocks, biases = piece_blocks(0, place, points_ref, mass_ref)
    for r in range(0, rows, ROWS):
        top = None
        for m in range(4):
            product = piece_product(x_ref, points_ref, r, m)
            for side in range(2):
                terms = product[:, lane_tile(side)] * BITS + biases[m][side]
                t_ref[2 * blocks[m] + side, r : r + ROWS, :] = terms
                top = terms if top is None else jnp.maximum(top, terms)
        top_ref[r : r + ROWS, :] = top

    def rows_step(r, unused):
        at = at_rows(r)
        top = jnp.max(top_ref[at, :], axis=1, keepdims=True)
        total = jnp.zeros((STEP, LANES), jnp.float32)
        for m in range(4):
            for side in range(2):
                total += jnp.exp2(t_ref[2 * blocks[m] + side, at, :] - top)
        top_ref[at, :] = jnp.broadcast_to(top, (STEP, LANES))
        sum_ref[at, :] = total
        return unused

    lax.fori_loop(0, rows // STEP, rows_step, 0)
    top_line_ref[...] = collapse_top(top_ref)


def piece_steps(pieces, place, x_ref, mass_ref, top_ref, old_sum_ref, t_ref, sum_ref):
    chunks = []
    for k, points_ref in pieces:
        blocks, biases = piece_blocks(k, place, points_ref, mass_ref)
        chunks += [(points_ref, m, blocks[m], biases[m]) for m in range(4)]
    for r in range(0, x_ref.shape[0], ROWS):
        top = top_ref[r : r + ROWS, :]
        total = old_sum_ref[r : r + ROWS, :]
        for points_ref, m, block, bias in chunks:
            product = piece_product(x_ref, points_ref, r, m)
            for side in range(2):
                terms = product[:, lane_tile(side)] * BITS + bias[side]
                t_ref[2 * block + side, r : r + ROWS, :] = terms
                total += jnp.exp2(terms - top)
        sum_ref[r : r + ROWS, :] = total


def more_terms_kernel(k, place, x_ref, old_ref, old_sum_ref, top_ref, points_ref, mass_ref, *refs):
    t_ref, sum_ref = refs
    pieces = [(k, points_ref)]
    piece_steps(pieces, place, x_ref, mass_ref, top_ref, old_sum_ref, t_ref, sum_ref)


def last_terms_kernel(shifts, place, x_ref, old_ref, old_sum_ref, old_top_ref, *refs):
    points_ref, more_ref, mass_ref, top_line_ref, t_ref, sum_ref, out_ref, top_ref = refs
    tiles, rows, _ = t_ref.shape
    pieces = list(zip(shifts, (points_ref, more_ref)))
    piece_steps(pieces, place, x_ref, mass_ref, old_top_ref, old_sum_ref, t_ref, sum_ref)
    total = collapse(sum_ref)
    out_ref[...] = top_line_ref[...] * LN2 + jnp.log(total)

    @pl.when(jnp.logical_not(jnp.max(total) < HUGE))
    def exact():
        def rows_step(r, unused):
            at = at_rows(r)
            top = jnp.full((STEP, LANES), -jnp.inf, jnp.float32)
            for t in range(tiles):
                top = jnp.maximum(top, t_ref[t, at, :])
            top = jnp.max(top, axis=1, keepdims=True)
            total = jnp.zeros((STEP, LANES), jnp.float32)
            for t in range(tiles):
                total += jnp.exp2(t_ref[t, at, :] - top)
            top_ref[at, :] = jnp.broadcast_to(top, (STEP, LANES))
            sum_ref[at, :] = total
            return unused

        lax.fori_loop(0, rows // STEP, rows_step, 0)
        out_ref[...] = collapse_top(top_ref) * LN2 + jnp.log(collapse(sum_ref))


def column_kernel(t_ref, *refs):
    parts, (mass_ref, out_ref, lse_ref, wide_ref, line_ref) = refs[:4], refs[4:]
    tiles, rows, _ = t_ref.shape
    lse = lse_all(values(parts))
    lse_ref[...] = lse
    spread((mass_ref[...] - lse) * LOG2E, wide_ref)
    per, step = 32, 128

    def group(value):
        return value.reshape(step // 8, 8, LANES)

    def sums(c, tops):
        wide = [jnp.broadcast_to(top, (step, LANES)) for top in tops]

        def sum_step(r, totals):
            at = at_rows(r, step)
            own = wide_ref[at, :]
            return tuple(
                total
                + jnp.sum(
                    group(jnp.exp2(t_ref[c + t, at, :] + own - wide[t])), axis=0
                )
                for t, total in enumerate(totals)
            )

        start = tuple(jnp.zeros((8, LANES), jnp.float32) for _ in range(per))
        totals = lax.fori_loop(0, rows // step, sum_step, start)
        for t in range(per):
            total = jnp.sum(totals[t], axis=0, keepdims=True)
            line_ref[c + t : c + t + 1, :] = tops[t] * LN2 + jnp.log(total)

    for c in range(0, tiles, per):
        tops = [
            jnp.max(t_ref[c + t, :32, :] + wide_ref[:32, :], axis=0, keepdims=True)
            for t in range(per)
        ]
        sums(c, tops)

    @pl.when(jnp.logical_not(jnp.max(line_ref[...]) < HUGE))
    def exact():
        for c in range(0, tiles, per):

            def top_step(r, tops):
                at = at_rows(r, step)
                return tuple(
                    jnp.maximum(top, jnp.max(group(t_ref[c + t, at, :] + wide_ref[at, :]), axis=0))
                    for t, top in enumerate(tops)
                )

            start = tuple(jnp.full((8, LANES), -jnp.inf, jnp.float32) for _ in range(per))
            tops = lax.fori_loop(0, rows // step, top_step, start)
            sums(c, [jnp.max(top, axis=0, keepdims=True) for top in tops])

    copies(out_ref, line_ref[...])


def plan_kernel(t_ref, parts_ref, tgt_mass_ref, src_lse_ref, src_mass_ref, *refs):
    plan_ref, out_ref, lse_ref, wide_ref, sum_ref, line_ref = refs
    tiles, rows, _ = t_ref.shape
    lse = combined(parts_ref, lse_all)
    lse_ref[...] = lse
    line_ref[...] = (tgt_mass_ref[...] - lse) * LOG2E
    spread((src_mass_ref[...] - src_lse_ref[...]) * LOG2E, wide_ref)
    per, step = 4, 128

    def rows_step(r, unused):
        at = at_rows(r, step)
        total = jnp.zeros((step, LANES), jnp.float32)
        own = wide_ref[at, :]
        for c in range(0, tiles, per):
            terms = [t_ref[c + t, at, :] for t in range(per)]
            values = [
                jnp.exp2(terms[t] + own + line_ref[c + t : c + t + 1, :]) for t in range(per)
            ]
            for t in range(per):
                plan_ref[c + t, at, :] = values[t]
                total += values[t]
        sum_ref[at, :] = total
        return unused

    lax.fori_loop(0, rows // step, rows_step, 0)
    out_ref[...] = collapse(sum_ref)


def row_sums_kernel(plan_ref, parts_ref, mass_ref, out_ref, sum_ref, line_ref):
    tiles, rows, _ = plan_ref.shape
    step = 512
    line_ref[...] = jnp.exp(mass_ref[...]) / combined(parts_ref, add_all)

    def rows_step(r, unused):
        at = at_rows(r, step)
        total = jnp.zeros((step, LANES), jnp.float32)
        for t in range(tiles):
            total += plan_ref[t, at, :] * line_ref[t : t + 1, :]
        sum_ref[at, :] = total
        return unused

    lax.fori_loop(0, rows // step, rows_step, 0)
    out_ref[...] = collapse(sum_ref)


def column_sums(plan_ref, scale, line_ref, wide_ref):
    tiles, rows, _ = plan_ref.shape
    spread(scale, wide_ref)
    per = tiles
    for c in range(0, tiles, per):

        def rows_step(r, totals):
            at = at_rows(r)
            own = wide_ref[at, :]
            return tuple(
                total
                + jnp.sum(
                    (plan_ref[c + t, at, :] * own).reshape(STEP // 8, 8, LANES), axis=0
                )
                for t, total in enumerate(totals)
            )

        start = tuple(jnp.zeros((8, LANES), jnp.float32) for _ in range(per))
        totals = lax.fori_loop(0, rows // STEP, rows_step, start)
        for t in range(per):
            line_ref[c + t : c + t + 1, :] = jnp.sum(totals[t], axis=0, keepdims=True)


def column_sums_kernel(plan_ref, *refs):
    parts, (mass_ref, out_ref, wide_ref, line_ref) = refs[:4], refs[4:]
    scale = jnp.exp(mass_ref[...]) / add_all(values(parts))
    column_sums(plan_ref, scale, line_ref, wide_ref)
    copies(out_ref, line_ref[...])


def last_column_sums_kernel(plan_ref, *refs):
    parts, (mass_ref, lse_ref, squares_ref) = refs[:4], refs[4:7]
    out_ref, potential_ref, wide_ref, line_ref = refs[7:]
    sums = add_all(values(parts))
    mass = mass_ref[...]
    squares = squares_ref[...] / (WIDTH * EPS)
    potential = -EPS * (lse_ref[...] + jnp.log(sums) - mass - squares)
    potential_ref[...] = potential
    tiles = plan_ref.shape[0]
    line_ref[tiles:, :] = jnp.broadcast_to(jnp.sum(potential), (8, LANES))
    column_sums(plan_ref, jnp.exp(mass) / sums, line_ref, wide_ref)
    copies(out_ref, line_ref[...])


def last_kernel(parts_ref, mass_ref, lse_ref, potential_ref, own_ref, other_ref):
    tiles = mass_ref.shape[0]
    sums = combined(parts_ref, add_all)
    potential = -EPS * (lse_ref[...] + jnp.log(sums[:tiles]) - 2.0 * mass_ref[...])
    potential_ref[...] = potential
    own_ref[...] = jnp.broadcast_to(jnp.sum(potential), (8, LANES))
    other_ref[...] = sums[tiles:]


ALL = ("row_0", "row_1", "col_0", "col_1")
SIZES = (4, 4, 4, 2)


def number(y, x, z, core):
    return ((y % 4 * 4 + x % 4) * 4 + z) * 2 + core


def turned(value, stage, order):
    found = {0: value}
    for k in order:
        pairs = []
        for y, x, z, core in itertools.product(*map(range, SIZES)):
            along_y = (core + stage) % 2
            to = number(y + k * along_y, x + k * (1 - along_y), z, core)
            pairs.append((number(y, x, z, core), to))
        found[k] = lax.ppermute(value, ALL, pairs)
    return [found[k] for k in range(4)]


def crossed(value, k):
    pairs = []
    for y, x, z, core in itertools.product(*map(range, SIZES)):
        pairs.append((number(y, x, z, core), number(y, x, (z + k) % 4, 1 - core)))
    return lax.ppermute(value, ALL, pairs)


def body(src_points, tgt_points, log_src_mass, log_tgt_mass):
    rows, columns = src_points.shape[0], log_tgt_mass.shape[0]
    row_tiles, column_tiles = rows // LANES, columns // LANES
    src_mass = log_src_mass.reshape(row_tiles, LANES)
    tgt_mass = log_tgt_mass.reshape(column_tiles, LANES)
    place = jnp.stack([lax.axis_index(name) for name in ("row_0", "row_1", "col_1")])
    place = place.astype(jnp.int32)
    wide = pltpu.VMEM((rows, LANES), jnp.float32)
    big = pltpu.VMEM((column_tiles, rows, LANES), jnp.float32)
    line = pltpu.VMEM((column_tiles, LANES), jnp.float32)
    longer = pltpu.VMEM((column_tiles + 8, LANES), jnp.float32)
    by_row, by_column = f32(row_tiles, LANES), f32(column_tiles, LANES)
    peers_row, peers_col = lax.axis_size(ROW), lax.axis_size(COL)
    columns_out = f32(peers_row, column_tiles, LANES)

    def resident(value):
        return pltpu.with_memory_space_constraint(value, pltpu.VMEM)

    def over_col(value, combine):
        both = combine([value, lax.ppermute(value, "col_1", [(0, 1), (1, 0)])])
        return [both] + [crossed(both, k) for k in (2, 1, 3)]

    def over_row(value):
        return lax.all_to_all(value, ROW, 0, 0, tiled=True)

    first = jnp.concatenate(turned(tgt_points, 0, (2, 1, 3)))
    pieces = turned(first, 1, (1, 3, 2))
    terms, top, sums, squares, top_line = call(
        first_terms_kernel, (big, wide, wide, by_row, by_row), [SMEM] + [VMEM] * 3, []
    )(place, src_points, first, tgt_mass)
    for k in (1,):
        terms, sums = call(
            functools.partial(more_terms_kernel, k), (big, wide), [SMEM] + [VMEM] * 6, [], {2: 0, 3: 1}
        )(place, src_points, resident(terms), resident(sums), resident(top), pieces[k], tgt_mass)
    terms, sums, lse = call(
        functools.partial(last_terms_kernel, (3, 2)),
        (big, wide, by_row),
        [SMEM] + [VMEM] * 8,
        [wide],
        {2: 0, 3: 1},
    )(place, src_points, resident(terms), resident(sums), resident(top), pieces[3], pieces[2], tgt_mass, top_line)
    lse, src_lse = call(column_kernel, (columns_out, by_row), [VMEM] * 6, [wide, line])(
        resident(terms), *over_col(lse, lse_all), src_mass
    )
    plan, sums, tgt_lse = call(
        plan_kernel, (big, by_row, by_column), [VMEM] * 5, [wide, wide, line], {0: 0}
    )(resident(terms), over_row(lse), tgt_mass, src_lse, src_mass)
    plan = resident(plan)
    sums = call(column_sums_kernel, columns_out, [VMEM] * 6, [wide, line])(
        plan, *over_col(sums, add_all), src_mass
    )
    sums = call(row_sums_kernel, by_row, [VMEM] * 3, [wide, line])(plan, over_row(sums), tgt_mass)
    sums, src_potential = call(
        last_column_sums_kernel,
        (f32(peers_row, column_tiles + 8, LANES), by_row),
        [VMEM] * 8,
        [wide, longer],
    )(plan, *over_col(sums, add_all), src_mass, src_lse, squares)
    tgt_potential, tgt_sum, src_sum = call(
        last_kernel, (by_column, f32(8, LANES), f32(8, LANES)), [VMEM] * 3, []
    )(over_row(sums), tgt_mass, tgt_lse)
    tgt_sum = add_all(over_col(tgt_sum, add_all))
    sources_all, targets_all = rows * peers_row, columns * peers_col
    mean_potentials = (src_sum / sources_all + tgt_sum / targets_all)[0, 0]
    return (src_potential.reshape(-1), tgt_potential.reshape(-1), mean_potentials)


def solution(mesh):
    finer = Mesh(mesh.devices.reshape(4, 4, 4, 2), ("row_0", "row_1", "col_0", "col_1"))
    placed = (P(ROW, None), P(COL_ROW, None), P(ROW), P(COL))
    return jax.shard_map(
        body, mesh=finer, in_specs=placed, out_specs=(P(ROW), P(COL), P()), check_vma=False
    )
```

```python
import functools
import itertools
import math

import jax
import jax.numpy as jnp
from jax import lax
from jax.experimental import pallas as pl
from jax.experimental.pallas import tpu as pltpu
from jax.sharding import Mesh
from jax.sharding import PartitionSpec as P

ROW = ("row_0", "row_1")
COL = ("col_0", "col_1")
COL_ROW = ("col_0", "col_1", "row_0", "row_1")

EPS = 0.1
WIDTH = 256
NATS = 2.0 / (WIDTH * EPS)
BITS = NATS * math.log2(math.e)
LOG2E = math.log2(math.e)
LN2 = math.log(2.0)
VMEM_LIMIT = 24 * 1024 * 1024
LANES = 128
STEP = 64
ROWS = 512
HUGE = 3.0e38

VMEM = pl.BlockSpec(memory_space=pltpu.VMEM)
SMEM = pl.BlockSpec(memory_space=pltpu.SMEM)


def call(kernel, outs, ins, scratch, aliases=None):
    return pl.pallas_call(
        kernel,
        out_shape=outs,
        in_specs=ins,
        out_specs=jax.tree.map(lambda _: VMEM, outs),
        scratch_shapes=scratch,
        input_output_aliases=aliases or {},
        compiler_params=pltpu.CompilerParams(vmem_limit_bytes=VMEM_LIMIT),
    )


def f32(*shape):
    return jax.ShapeDtypeStruct(shape, jnp.float32)


def spread(dense, wide_ref):
    for b in range(dense.shape[0]):
        square = jnp.broadcast_to(dense[b : b + 1, :], (LANES, LANES))
        wide_ref[b * LANES : (b + 1) * LANES, :] = square.T


def collapse(wide_ref):
    lines = [
        jnp.sum(wide_ref[b * LANES : (b + 1) * LANES, :].T, axis=0, keepdims=True)
        for b in range(wide_ref.shape[0] // LANES)
    ]
    return jnp.concatenate(lines, axis=0)


def collapse_top(wide_ref):
    lines = [
        wide_ref[b * LANES : (b + 1) * LANES, :].T[:1, :]
        for b in range(wide_ref.shape[0] // LANES)
    ]
    return jnp.concatenate(lines, axis=0)


def add_all(parts):
    total = parts[0]
    for part in parts[1:]:
        total = total + part
    return total


def lse_all(parts):
    top = parts[0]
    for part in parts[1:]:
        top = jnp.maximum(top, part)
    return top + jnp.log(add_all([jnp.exp(part - top) for part in parts]))


def copies(out_ref, value):
    for peer in range(out_ref.shape[0]):
        out_ref[peer] = value


def combined(parts_ref, combine):
    return combine([parts_ref[peer] for peer in range(parts_ref.shape[0])])


def values(refs):
    return [ref[...] for ref in refs]


def at_rows(r, step=STEP):
    return pl.ds(pl.multiple_of(r * step, step), step)


def lane_tile(t):
    return slice(t * LANES, (t + 1) * LANES)


def target_block(place, shift, inner):
    first_core = place[2] == 0
    shift_y = jnp.where(first_core, shift, inner)
    shift_x = jnp.where(first_core, inner, shift)
    return 4 * lax.rem(place[0] + 4 - shift_y, 4) + lax.rem(place[1] + 4 - shift_x, 4)


def chunk_biases(points, mass_ref, block):
    squares = points.astype(jnp.float32) ** 2
    squares = squares[:, :LANES] + squares[:, LANES:]
    found = []
    for side in range(2):
        square = squares[side * LANES : (side + 1) * LANES, :].T
        mass = mass_ref[pl.ds(2 * block + side, 1), :]
        found.append(mass * LOG2E - jnp.sum(square, axis=0, keepdims=True) * (0.5 * BITS))
    return found


def piece_product(x_ref, points_ref, r, m):
    return lax.dot_general(
        x_ref[r : r + ROWS, :],
        points_ref[m * 256 : (m + 1) * 256, :],
        (((1,), (1,)), ((), ())),
        preferred_element_type=jnp.float32,
    )


def piece_blocks(k, place, points_ref, mass_ref):
    blocks = [target_block(place, k, m) for m in range(4)]
    biases = [
        chunk_biases(points_ref[m * 256 : (m + 1) * 256, :], mass_ref, blocks[m]) for m in range(4)
    ]
    return blocks, biases


def first_terms_kernel(place, x_ref, points_ref, mass_ref, t_ref, top_ref, sum_ref, squares_ref):
    rows = x_ref.shape[0]
    squares = x_ref[...].astype(jnp.float32) ** 2
    sum_ref[...] = squares[:, :LANES] + squares[:, LANES:]
    squares_ref[...] = collapse(sum_ref)
    blocks, biases = piece_blocks(0, place, points_ref, mass_ref)
    for r in range(0, rows, ROWS):
        top = None
        for m in range(4):
            product = piece_product(x_ref, points_ref, r, m)
            for side in range(2):
                terms = product[:, lane_tile(side)] * BITS + biases[m][side]
                t_ref[2 * blocks[m] + side, r : r + ROWS, :] = terms
                top = terms if top is None else jnp.maximum(top, terms)
        top_ref[r : r + ROWS, :] = top

    def rows_step(r, unused):
        at = at_rows(r)
        top = jnp.max(top_ref[at, :], axis=1, keepdims=True)
        total = jnp.zeros((STEP, LANES), jnp.float32)
        for m in range(4):
            for side in range(2):
                total += jnp.exp2(t_ref[2 * blocks[m] + side, at, :] - top)
        top_ref[at, :] = jnp.broadcast_to(top, (STEP, LANES))
        sum_ref[at, :] = total
        return unused

    lax.fori_loop(0, rows // STEP, rows_step, 0)


def piece_steps(pieces, place, x_ref, mass_ref, top_ref, old_sum_ref, t_ref, sum_ref):
    chunks = []
    for k, points_ref in pieces:
        blocks, biases = piece_blocks(k, place, points_ref, mass_ref)
        chunks += [(points_ref, m, blocks[m], biases[m]) for m in range(4)]
    for r in range(0, x_ref.shape[0], ROWS):
        top = top_ref[r : r + ROWS, :]
        total = old_sum_ref[r : r + ROWS, :]
        for points_ref, m, block, bias in chunks:
            product = piece_product(x_ref, points_ref, r, m)
            for side in range(2):
                terms = product[:, lane_tile(side)] * BITS + bias[side]
                t_ref[2 * block + side, r : r + ROWS, :] = terms
                total += jnp.exp2(terms - top)
        sum_ref[r : r + ROWS, :] = total


def more_terms_kernel(k, place, x_ref, old_ref, old_sum_ref, top_ref, points_ref, mass_ref, *refs):
    t_ref, sum_ref = refs
    pieces = [(k, points_ref)]
    piece_steps(pieces, place, x_ref, mass_ref, top_ref, old_sum_ref, t_ref, sum_ref)


def last_terms_kernel(shifts, place, x_ref, old_ref, old_sum_ref, old_top_ref, *refs):
    points_ref, more_ref, mass_ref, t_ref, sum_ref, out_ref, top_ref = refs
    tiles, rows, _ = t_ref.shape
    pieces = list(zip(shifts, (points_ref, more_ref)))
    piece_steps(pieces, place, x_ref, mass_ref, old_top_ref, old_sum_ref, t_ref, sum_ref)
    total = collapse(sum_ref)
    out_ref[...] = collapse_top(old_top_ref) * LN2 + jnp.log(total)

    @pl.when(jnp.logical_not(jnp.max(total) < HUGE))
    def exact():
        def rows_step(r, unused):
            at = at_rows(r)
            top = jnp.full((STEP, LANES), -jnp.inf, jnp.float32)
            for t in range(tiles):
                top = jnp.maximum(top, t_ref[t, at, :])
            top = jnp.max(top, axis=1, keepdims=True)
            total = jnp.zeros((STEP, LANES), jnp.float32)
            for t in range(tiles):
                total += jnp.exp2(t_ref[t, at, :] - top)
            top_ref[at, :] = jnp.broadcast_to(top, (STEP, LANES))
            sum_ref[at, :] = total
            return unused

        lax.fori_loop(0, rows // STEP, rows_step, 0)
        out_ref[...] = collapse_top(top_ref) * LN2 + jnp.log(collapse(sum_ref))


def column_kernel(t_ref, *refs):
    parts, (mass_ref, out_ref, lse_ref, wide_ref, line_ref) = refs[:4], refs[4:]
    tiles, rows, _ = t_ref.shape
    lse = lse_all(values(parts))
    lse_ref[...] = lse
    spread((mass_ref[...] - lse) * LOG2E, wide_ref)
    per, step = 32, 128

    def group(value):
        return value.reshape(step // 8, 8, LANES)

    def sums(c, tops):
        wide = [jnp.broadcast_to(top, (step, LANES)) for top in tops]

        def sum_step(r, totals):
            at = at_rows(r, step)
            own = wide_ref[at, :]
            return tuple(
                total
                + jnp.sum(
                    group(jnp.exp2(t_ref[c + t, at, :] + own - wide[t])), axis=0
                )
                for t, total in enumerate(totals)
            )

        start = tuple(jnp.zeros((8, LANES), jnp.float32) for _ in range(per))
        totals = lax.fori_loop(0, rows // step, sum_step, start)
        for t in range(per):
            total = jnp.sum(totals[t], axis=0, keepdims=True)
            line_ref[c + t : c + t + 1, :] = tops[t] * LN2 + jnp.log(total)

    for c in range(0, tiles, per):
        tops = [
            jnp.max(t_ref[c + t, :32, :] + wide_ref[:32, :], axis=0, keepdims=True)
            for t in range(per)
        ]
        sums(c, tops)

    @pl.when(jnp.logical_not(jnp.max(line_ref[...]) < HUGE))
    def exact():
        for c in range(0, tiles, per):

            def top_step(r, tops):
                at = at_rows(r, step)
                return tuple(
                    jnp.maximum(top, jnp.max(group(t_ref[c + t, at, :] + wide_ref[at, :]), axis=0))
                    for t, top in enumerate(tops)
                )

            start = tuple(jnp.full((8, LANES), -jnp.inf, jnp.float32) for _ in range(per))
            tops = lax.fori_loop(0, rows // step, top_step, start)
            sums(c, [jnp.max(top, axis=0, keepdims=True) for top in tops])

    copies(out_ref, line_ref[...])


def plan_kernel(t_ref, parts_ref, tgt_mass_ref, src_lse_ref, src_mass_ref, *refs):
    plan_ref, out_ref, lse_ref, wide_ref, sum_ref, line_ref = refs
    tiles, rows, _ = t_ref.shape
    lse = combined(parts_ref, lse_all)
    lse_ref[...] = lse
    line_ref[...] = (tgt_mass_ref[...] - lse) * LOG2E
    spread((src_mass_ref[...] - src_lse_ref[...]) * LOG2E, wide_ref)
    per, step = 4, 128

    def rows_step(r, unused):
        at = at_rows(r, step)
        total = jnp.zeros((step, LANES), jnp.float32)
        own = wide_ref[at, :]
        for c in range(0, tiles, per):
            terms = [t_ref[c + t, at, :] for t in range(per)]
            values = [
                jnp.exp2(terms[t] + own + line_ref[c + t : c + t + 1, :]) for t in range(per)
            ]
            for t in range(per):
                plan_ref[c + t, at, :] = values[t]
                total += values[t]
        sum_ref[at, :] = total
        return unused

    lax.fori_loop(0, rows // step, rows_step, 0)
    out_ref[...] = collapse(sum_ref)


def row_sums_kernel(plan_ref, parts_ref, mass_ref, out_ref, sum_ref, line_ref):
    tiles, rows, _ = plan_ref.shape
    step = 512
    line_ref[...] = jnp.exp(mass_ref[...]) / combined(parts_ref, add_all)

    def rows_step(r, unused):
        at = at_rows(r, step)
        total = jnp.zeros((step, LANES), jnp.float32)
        for t in range(tiles):
            total += plan_ref[t, at, :] * line_ref[t : t + 1, :]
        sum_ref[at, :] = total
        return unused

    lax.fori_loop(0, rows // step, rows_step, 0)
    out_ref[...] = collapse(sum_ref)


def column_sums(plan_ref, scale, line_ref, wide_ref):
    tiles, rows, _ = plan_ref.shape
    spread(scale, wide_ref)
    per = tiles
    for c in range(0, tiles, per):

        def rows_step(r, totals):
            at = at_rows(r)
            own = wide_ref[at, :]
            return tuple(
                total
                + jnp.sum(
                    (plan_ref[c + t, at, :] * own).reshape(STEP // 8, 8, LANES), axis=0
                )
                for t, total in enumerate(totals)
            )

        start = tuple(jnp.zeros((8, LANES), jnp.float32) for _ in range(per))
        totals = lax.fori_loop(0, rows // STEP, rows_step, start)
        for t in range(per):
            line_ref[c + t : c + t + 1, :] = jnp.sum(totals[t], axis=0, keepdims=True)


def column_sums_kernel(plan_ref, *refs):
    parts, (mass_ref, out_ref, wide_ref, line_ref) = refs[:4], refs[4:]
    scale = jnp.exp(mass_ref[...]) / add_all(values(parts))
    column_sums(plan_ref, scale, line_ref, wide_ref)
    copies(out_ref, line_ref[...])


def last_column_sums_kernel(plan_ref, *refs):
    parts, (mass_ref, lse_ref, squares_ref) = refs[:4], refs[4:7]
    out_ref, potential_ref, wide_ref, line_ref = refs[7:]
    sums = add_all(values(parts))
    mass = mass_ref[...]
    squares = squares_ref[...] / (WIDTH * EPS)
    potential = -EPS * (lse_ref[...] + jnp.log(sums) - mass - squares)
    potential_ref[...] = potential
    tiles = plan_ref.shape[0]
    line_ref[tiles:, :] = jnp.broadcast_to(jnp.sum(potential), (8, LANES))
    column_sums(plan_ref, jnp.exp(mass) / sums, line_ref, wide_ref)
    copies(out_ref, line_ref[...])


def last_kernel(parts_ref, mass_ref, lse_ref, potential_ref, own_ref, other_ref):
    tiles = mass_ref.shape[0]
    sums = combined(parts_ref, add_all)
    potential = -EPS * (lse_ref[...] + jnp.log(sums[:tiles]) - 2.0 * mass_ref[...])
    potential_ref[...] = potential
    own_ref[...] = jnp.broadcast_to(jnp.sum(potential), (8, LANES))
    other_ref[...] = sums[tiles:]


ALL = ("row_0", "row_1", "col_0", "col_1")
SIZES = (4, 4, 4, 2)


def number(y, x, z, core):
    return ((y % 4 * 4 + x % 4) * 4 + z) * 2 + core


def turned(value, stage, order):
    found = {0: value}
    for k in order:
        pairs = []
        for y, x, z, core in itertools.product(*map(range, SIZES)):
            along_y = (core + stage) % 2
            to = number(y + k * along_y, x + k * (1 - along_y), z, core)
            pairs.append((number(y, x, z, core), to))
        found[k] = lax.ppermute(value, ALL, pairs)
    return [found[k] for k in range(4)]


def crossed(value, k):
    pairs = []
    for y, x, z, core in itertools.product(*map(range, SIZES)):
        pairs.append((number(y, x, z, core), number(y, x, (z + k) % 4, 1 - core)))
    return lax.ppermute(value, ALL, pairs)


def body(src_points, tgt_points, log_src_mass, log_tgt_mass):
    rows, columns = src_points.shape[0], log_tgt_mass.shape[0]
    row_tiles, column_tiles = rows // LANES, columns // LANES
    src_mass = log_src_mass.reshape(row_tiles, LANES)
    tgt_mass = log_tgt_mass.reshape(column_tiles, LANES)
    place = jnp.stack([lax.axis_index(name) for name in ("row_0", "row_1", "col_1")])
    place = place.astype(jnp.int32)
    wide = pltpu.VMEM((rows, LANES), jnp.float32)
    big = pltpu.VMEM((column_tiles, rows, LANES), jnp.float32)
    line = pltpu.VMEM((column_tiles, LANES), jnp.float32)
    longer = pltpu.VMEM((column_tiles + 8, LANES), jnp.float32)
    by_row, by_column = f32(row_tiles, LANES), f32(column_tiles, LANES)
    peers_row, peers_col = lax.axis_size(ROW), lax.axis_size(COL)
    columns_out = f32(peers_row, column_tiles, LANES)

    def resident(value):
        return pltpu.with_memory_space_constraint(value, pltpu.VMEM)

    def over_col(value, combine):
        both = combine([value, lax.ppermute(value, "col_1", [(0, 1), (1, 0)])])
        return [both] + [crossed(both, k) for k in (2, 1, 3)]

    def over_row(value):
        return lax.all_to_all(value, ROW, 0, 0, tiled=True)

    first = jnp.concatenate(turned(tgt_points, 0, (2, 1, 3)))
    pieces = turned(first, 1, (1, 3, 2))
    terms, top, sums, squares = call(
        first_terms_kernel, (big, wide, wide, by_row), [SMEM] + [VMEM] * 3, []
    )(place, src_points, first, tgt_mass)
    for k in (1,):
        terms, sums = call(
            functools.partial(more_terms_kernel, k), (big, wide), [SMEM] + [VMEM] * 6, [], {2: 0, 3: 1}
        )(place, src_points, resident(terms), resident(sums), resident(top), pieces[k], tgt_mass)
    terms, sums, lse = call(
        functools.partial(last_terms_kernel, (3, 2)),
        (big, wide, by_row),
        [SMEM] + [VMEM] * 7,
        [wide],
        {2: 0, 3: 1},
    )(place, src_points, resident(terms), resident(sums), resident(top), pieces[3], pieces[2], tgt_mass)
    lse, src_lse = call(column_kernel, (columns_out, by_row), [VMEM] * 6, [wide, line])(
        resident(terms), *over_col(lse, lse_all), src_mass
    )
    plan, sums, tgt_lse = call(
        plan_kernel, (big, by_row, by_column), [VMEM] * 5, [wide, wide, line], {0: 0}
    )(resident(terms), over_row(lse), tgt_mass, src_lse, src_mass)
    plan = resident(plan)
    sums = call(column_sums_kernel, columns_out, [VMEM] * 6, [wide, line])(
        plan, *over_col(sums, add_all), src_mass
    )
    sums = call(row_sums_kernel, by_row, [VMEM] * 3, [wide, line])(plan, over_row(sums), tgt_mass)
    sums, src_potential = call(
        last_column_sums_kernel,
        (f32(peers_row, column_tiles + 8, LANES), by_row),
        [VMEM] * 8,
        [wide, longer],
    )(plan, *over_col(sums, add_all), src_mass, src_lse, squares)
    tgt_potential, tgt_sum, src_sum = call(
        last_kernel, (by_column, f32(8, LANES), f32(8, LANES)), [VMEM] * 3, []
    )(over_row(sums), tgt_mass, tgt_lse)
    tgt_sum = add_all(over_col(tgt_sum, add_all))
    sources_all, targets_all = rows * peers_row, columns * peers_col
    mean_potentials = (src_sum / sources_all + tgt_sum / targets_all)[0, 0]
    return (src_potential.reshape(-1), tgt_potential.reshape(-1), mean_potentials)


def solution(mesh):
    finer = Mesh(mesh.devices.reshape(4, 4, 4, 2), ("row_0", "row_1", "col_0", "col_1"))
    placed = (P(ROW, None), P(COL_ROW, None), P(ROW), P(COL))
    return jax.shard_map(
        body, mesh=finer, in_specs=placed, out_specs=(P(ROW), P(COL), P()), check_vma=False
    )
```
